32 devices in a mesh: dp: 8 (over y, x, core), seq: 4 (over z).
Axes of the slice: x: 2, y: 2, z: 4, core: 2. Of those that a mesh axis runs over, the one named last changes fastest.
Arguments:
- hidden_in: bfloat16 [8192, 2048], P(('dp', 'seq')), may hold values from -60 to 60
- layer_input: bfloat16 [8192, 256], P(('dp', 'seq')), may hold values from -6 to 6
- seq_lengths: int32 [8], P('dp'), may hold values from 256 to 1024, as said below
- cotangent: bfloat16 [8192, 2048], P(('dp', 'seq')), may hold values from -6 to 6
- query_weight: bfloat16 [2048, 2048], P(('dp', 'seq')), may hold values from -0.125 to 0.125
- key_matrix: bfloat16 [2048, 512], P(('dp', 'seq')), may hold values from -0.125 to 0.125
- value_matrix: bfloat16 [2048, 512], P(('dp', 'seq')), may hold values from -0.125 to 0.125
- output_weight: bfloat16 [2048, 2048], P(('dp', 'seq')), may hold values from -0.125 to 0.125
- laurel_left: bfloat16 [2048, 64], P(('dp', 'seq')), may hold values from -0.125 to 0.125
- laurel_right: bfloat16 [64, 2048], P(None, ('dp', 'seq')), may hold values from -0.75 to 0.75
- input_gate: bfloat16 [2048, 256], P(('dp', 'seq')), may hold values from -0.125 to 0.125
- input_projection: bfloat16 [256, 2048], P(None, ('dp', 'seq')), may hold values from -0.375 to 0.375
- gate_weight: bfloat16 [2048, 8192], P(('dp', 'seq')), may hold values from -0.125 to 0.125
- up_weight: bfloat16 [2048, 8192], P(('dp', 'seq')), may hold values from -0.125 to 0.125
- down_weight: bfloat16 [8192, 2048], P(('dp', 'seq')), may hold values from -0.0625 to 0.0625
- norm_gains: bfloat16 [6, 2048], P(None, ('dp', 'seq')), may hold values from 0.5 to 1.5
- head_gains: bfloat16 [2, 256], P(None, ('dp', 'seq')), may hold values from 0.19921875 to 0.5
Outputs:
- block_out: float32 [8192, 2048], P(('dp', 'seq'))
- d_hidden: float32 [8192, 2048], P(('dp', 'seq'))
- d_query_weight: float32 [2048, 2048], P(('dp', 'seq'))
- d_key_weight: float32 [2048, 512], P(('dp', 'seq'))
- d_value_weight: float32 [2048, 512], P(('dp', 'seq'))
- d_output_weight: float32 [2048, 2048], P(('dp', 'seq'))
- d_laurel_left: float32 [2048, 64], P(('dp', 'seq'))
- d_laurel_right: float32 [64, 2048], P(None, ('dp', 'seq'))
- d_input_gate: float32 [2048, 256], P(('dp', 'seq'))
- d_input_projection: float32 [256, 2048], P(None, ('dp', 'seq'))
- d_gate_weight: float32 [2048, 8192], P(('dp', 'seq'))
- d_up_weight: float32 [2048, 8192], P(('dp', 'seq'))
- d_down_weight: float32 [8192, 2048], P(('dp', 'seq'))
- d_norm_gains: float32 [6, 2048], P(None, ('dp', 'seq'))
- d_head_gains: float32 [2, 256], P(None, ('dp', 'seq'))
The draws below stay inside these ranges and needn't reach their ends.
Inputs may be any that keep to these rules, and one draw needn't show every extreme that they name: `seq_lengths`: one sequence has exactly 1024 tokens and another exactly a quarter of 1024.
All inputs are finite; a program needn't handle non-finite values.
Results may differ from the reference program's by a relative error of at most 0.018.
Values may be sent and summed in bfloat16 or wider, within the bound.
A program may use at most 640 MiB of HBM per device.

```python
import jax
import jax.numpy as jnp
from jax import lax

MODEL_WIDTH = 2048
QUERY_HEADS = 8
KEY_VALUE_HEADS = 2
HEAD_SIZE = 256
FF = 8192
RANK = 64
PL = 256
WINDOW = 512
SEQS = 8
LEN = 1024
TOKENS = 8192


def draw_seq_lengths(key, part):
    first, second, third = jax.random.split(key, 3)
    lengths = jax.random.randint(first, (SEQS,), LEN // 4, LEN + 1)
    longest = jax.random.randint(second, (), 0, SEQS)
    shortest = (longest + 1 + jax.random.randint(third, (), 0, SEQS - 1)) % SEQS
    places = jnp.arange(SEQS)
    lengths = jnp.where(places == longest, LEN, lengths)
    lengths = jnp.where(places == shortest, LEN // 4, lengths)
    return lengths.astype(jnp.int32)


def draw_hidden_in(key, part):
    first, second, third = jax.random.split(key, 3)
    row_scale = jnp.exp(jax.random.uniform(first, (TOKENS, 1), minval=-1.15, maxval=1.15))
    column_scale = jnp.exp(jax.random.uniform(second, (1, MODEL_WIDTH), minval=-1.15, maxval=1.15))
    base = jax.random.normal(third, (TOKENS, MODEL_WIDTH))
    base = jnp.clip(base, -6.0, 6.0)
    return (base * row_scale * column_scale).astype(jnp.bfloat16)


def shard_levels(stream_key, extent, cuts, smallest, high):
    level = 1.0
    for dim, blocks in cuts:
        steps = jax.random.uniform(jax.random.fold_in(jax.random.fold_in(stream_key, 6), dim), (blocks,), jnp.float32, smallest / len(cuts), high / len(cuts))
        level = level * jnp.repeat(jnp.exp(steps), extent[dim] // blocks).reshape((-1,) + (1,) * (len(extent) - 1 - dim))
    return level


def centred(own_key, extent, spread, reach, shards=(), kind=jnp.bfloat16):
    result = jax.random.normal(own_key, extent, jnp.float32) * spread
    if len(shards) > 0:
        result = shard_levels(own_key, extent, shards, -0.22, 0.18) * result
    return jnp.clip(result, min=-reach, max=reach).astype(kind)


def setup_inputs(seed: int = 0) -> dict:
    streams_of = jax.random.split(jax.random.key(seed), 18)
    hidden_in = draw_hidden_in(jax.random.fold_in(streams_of[17], 71), 0)
    layer_input = centred(streams_of[1], (TOKENS, PL), 1.0, 6.0, ((0, 32),))
    seq_lengths = draw_seq_lengths(jax.random.fold_in(streams_of[17], 71), 0)
    cotangent = centred(streams_of[3], (TOKENS, MODEL_WIDTH), 1.0, 6.0, ((0, 32),))
    query_weight = centred(streams_of[4], (MODEL_WIDTH, QUERY_HEADS * HEAD_SIZE), MODEL_WIDTH ** -0.5, 0.125, ((0, 32),))
    key_matrix = centred(streams_of[5], (MODEL_WIDTH, KEY_VALUE_HEADS * HEAD_SIZE), MODEL_WIDTH ** -0.5, 0.125, ((0, 32),))
    value_matrix = centred(streams_of[6], (MODEL_WIDTH, KEY_VALUE_HEADS * HEAD_SIZE), MODEL_WIDTH ** -0.5, 0.125, ((0, 32),))
    output_weight = centred(streams_of[7], (QUERY_HEADS * HEAD_SIZE, MODEL_WIDTH), (QUERY_HEADS * HEAD_SIZE) ** -0.5, 0.125, ((0, 32),))
    laurel_left = centred(streams_of[8], (MODEL_WIDTH, RANK), MODEL_WIDTH ** -0.5, 0.125, ((0, 32),))
    laurel_right = centred(streams_of[9], (RANK, MODEL_WIDTH), RANK ** -0.5, 0.75, ((1, 32),))
    input_gate = centred(streams_of[10], (MODEL_WIDTH, PL), MODEL_WIDTH ** -0.5, 0.125, ((0, 32),))
    input_projection = centred(streams_of[11], (PL, MODEL_WIDTH), PL ** -0.5, 0.375, ((1, 32),))
    gate_weight = centred(streams_of[12], (MODEL_WIDTH, FF), MODEL_WIDTH ** -0.5, 0.125, ((0, 32),))
    up_weight = centred(streams_of[13], (MODEL_WIDTH, FF), MODEL_WIDTH ** -0.5, 0.125, ((0, 32),))
    down_weight = centred(streams_of[14], (FF, MODEL_WIDTH), FF ** -0.5, 0.0625, ((0, 32),))
    norm_gains = jnp.clip(0.5 + 1.0 * jax.random.uniform(streams_of[15], (6, MODEL_WIDTH), jnp.float32) ** shard_levels(streams_of[15], (6, MODEL_WIDTH), ((1, 32),), -0.2, 0.2), 0.5, 1.5).astype(jnp.bfloat16)
    head_gains = jnp.clip(0.19921875 + 0.30078125 * jax.random.uniform(streams_of[16], (2, HEAD_SIZE), jnp.float32) ** shard_levels(streams_of[16], (2, HEAD_SIZE), ((1, 32),), -0.2, 0.2), 0.19921875, 0.5).astype(jnp.bfloat16)
    return {"hidden_in": hidden_in, "layer_input": layer_input, "seq_lengths": seq_lengths, "cotangent": cotangent, "query_weight": query_weight, "key_matrix": key_matrix, "value_matrix": value_matrix, "output_weight": output_weight, "laurel_left": laurel_left, "laurel_right": laurel_right, "input_gate": input_gate, "input_projection": input_projection, "gate_weight": gate_weight, "up_weight": up_weight, "down_weight": down_weight, "norm_gains": norm_gains, "head_gains": head_gains}


EPSILON = 1e-06
ROPE_BASE = 10000.0
HALF_ROOT = 0.7071067811865476
MASKED = -1e+30
HIGHEST = lax.Precision.HIGHEST

@jax.custom_vjp
def low(v):
    return lax.optimization_barrier(v.astype(jnp.bfloat16)).astype(jnp.float32)

@jax.custom_vjp
def low_back(v):
    return v

def low_keep(v):
    return (low(v), None)

def low_pass(kept, grad):
    return (grad,)

def back_keep(v):
    return (v, None)

def back_low(kept, grad):
    return (low(grad),)
low.defvjp(low_keep, low_pass)
low_back.defvjp(back_keep, back_low)

def rms_norm(value, gain):
    return value * lax.rsqrt(lax.optimization_barrier(jnp.mean(value * value, axis=-1, keepdims=True)) + EPSILON) * gain

def rotate(value, positions):
    half = value.shape[-1] // 2
    inverse = ROPE_BASE ** (-jnp.arange(half, dtype=jnp.float32) * 2.0 / value.shape[-1])
    angle = positions.astype(jnp.float32)[:, None] * inverse[None, :]
    cosine = jnp.cos(angle)[:, None, :]
    sine = jnp.sin(angle)[:, None, :]
    first = value[..., :half]
    second = value[..., half:]
    return jnp.concatenate([first * cosine - second * sine, second * cosine + first * sine], axis=-1)

def matrix_multiply(left, right):
    return jnp.dot(left, right, precision=HIGHEST)

def gated(gate, other):
    return jax.nn.gelu(gate, approximate=True) * other

def forward(hidden, side_input, length, params):
    query_weight, key_matrix, value_matrix, output_weight, laurel_left, laurel_right, input_gate, input_projection, gate_weight, up_weight, down_weight, norm_gains, head_gains = params
    item_count = hidden.shape[0]
    positions = jnp.arange(item_count, dtype=jnp.int32)
    live_rows = (positions < length).astype(hidden.dtype)[:, None]
    normed = rms_norm(hidden, norm_gains[0])
    normalized_reduced = low(normed)
    query_raw = low_back(matrix_multiply(normalized_reduced, query_weight)).reshape(item_count, QUERY_HEADS, HEAD_SIZE)
    key_unrotated = low_back(matrix_multiply(normalized_reduced, key_matrix)).reshape(item_count, KEY_VALUE_HEADS, HEAD_SIZE)
    value_projected = low_back(matrix_multiply(normalized_reduced, value_matrix)).reshape(item_count, KEY_VALUE_HEADS, HEAD_SIZE)
    query_rotated = low(rotate(rms_norm(query_raw, head_gains[0]), positions))
    key_rot = low(rotate(rms_norm(key_unrotated, head_gains[1]), positions))
    value_rot = low(rms_norm(value_projected, 1.0))
    grouped_rows = query_rotated.reshape(item_count, KEY_VALUE_HEADS, QUERY_HEADS // KEY_VALUE_HEADS, HEAD_SIZE)
    scores = low_back(jnp.einsum('qkgd,tkd->kgqt', grouped_rows, key_rot, precision=HIGHEST))
    allowed = (positions[None, :] <= positions[:, None]) & (positions[:, None] - positions[None, :] < WINDOW)
    scores = jnp.where(allowed, scores, MASKED)
    row_top = lax.optimization_barrier(jnp.max(scores, axis=-1, keepdims=True))
    weights = jnp.exp(scores - row_top)
    probs_low = low(weights / lax.optimization_barrier(jnp.sum(weights, axis=-1, keepdims=True)))
    mixed = jnp.einsum('kgqt,tkd->qkgd', probs_low, value_rot, precision=HIGHEST)
    mixed = low(low_back(mixed)).reshape(item_count, QUERY_HEADS * HEAD_SIZE)
    attention_raw = low_back(matrix_multiply(mixed, output_weight))
    branch_one = hidden + rms_norm(attention_raw, norm_gains[1])
    left_low = low(low_back(matrix_multiply(normalized_reduced, laurel_left)))
    right_raw = low_back(matrix_multiply(left_low, laurel_right))
    merged = (branch_one + normed + rms_norm(right_raw, norm_gains[2])) * HALF_ROOT
    expand_low = low(rms_norm(merged, norm_gains[3]))
    gate_raw = low_back(matrix_multiply(expand_low, gate_weight))
    up_raw = low_back(matrix_multiply(expand_low, up_weight))
    act_low = low(gated(gate_raw, up_raw))
    reduced_raw = low_back(matrix_multiply(act_low, down_weight))
    after_feed = merged + rms_norm(reduced_raw, norm_gains[4])
    after_low = low(after_feed)
    side_raw = low_back(matrix_multiply(after_low, input_gate))
    side_low = low(gated(side_raw, side_input))
    side_out = low_back(matrix_multiply(side_low, input_projection))
    return (after_feed + rms_norm(side_out, norm_gains[5])) * live_rows

def reference(hidden_in, layer_input, seq_lengths, cotangent, query_weight, key_matrix, value_matrix, output_weight, laurel_left, laurel_right, input_gate, input_projection, gate_weight, up_weight, down_weight, norm_gains, head_gains):
    params = tuple((weight.astype(jnp.float32) for weight in (query_weight, key_matrix, value_matrix, output_weight, laurel_left, laurel_right, input_gate, input_projection, gate_weight, up_weight, down_weight, norm_gains, head_gains)))
    hiddens = hidden_in.astype(jnp.float32).reshape(SEQS, LEN, MODEL_WIDTH)
    sides = layer_input.astype(jnp.float32).reshape(SEQS, LEN, PL)
    upstreams = cotangent.astype(jnp.float32).reshape(SEQS, LEN, MODEL_WIDTH)

    def one_sequence(totals, items):
        hidden, side_input, upstream, length = items

        def apply_layer(hidden_value, param_values):
            return forward(hidden_value, side_input, length, param_values)
        out_value, pull = jax.vjp(apply_layer, hidden, params)
        grad_hidden, grad_params = pull(upstream)
        return (jax.tree.map(jnp.add, totals, grad_params), (out_value, grad_hidden))
    zeros = jax.tree.map(jnp.zeros_like, params)
    totals, (outputs, grads) = lax.scan(one_sequence, zeros, (hiddens, sides, upstreams, seq_lengths))
    return (outputs.reshape(TOKENS, MODEL_WIDTH), grads.reshape(TOKENS, MODEL_WIDTH), totals[0], totals[1], totals[2], totals[3], totals[4], totals[5], totals[6], totals[7], totals[8], totals[9], totals[10], totals[11], totals[12])
```

```python
import jax
import jax.numpy as jnp
from jax import lax
from jax.sharding import Mesh, PartitionSpec as P

QUERY_HEADS = 8
KEY_VALUE_HEADS = 2
HEAD_SIZE = 256
WINDOW = 512
EPSILON = 1e-06
ROPE_BASE = 10000.0
HALF_ROOT = 0.7071067811865476
MASKED = -1e30
GELU_SCALE = 0.7978845608028654
GELU_CUBE = 0.044715
F32 = jnp.float32
BF16 = jnp.bfloat16


def dot(left, right, left_dim=1, right_dim=0):
    return lax.dot_general(
        left, right, (((left_dim,), (right_dim,)), ((), ())), preferred_element_type=F32
    )


def inverse_rms(value):
    return lax.rsqrt(jnp.mean(value * value, axis=-1, keepdims=True) + EPSILON)


def rms_back(value, inverse, gain, grad):
    scaled = grad * gain
    inner = jnp.mean(scaled * value, axis=-1, keepdims=True)
    unit = value * inverse
    return inverse * (scaled - unit * (inverse * inner)), grad * unit


def rope_tables(positions):
    half = HEAD_SIZE // 2
    rate = ROPE_BASE ** (-jnp.arange(half, dtype=F32) * 2.0 / HEAD_SIZE)
    angle = positions.astype(F32)[:, None] * rate[None, :]
    return jnp.cos(angle)[:, None, :], jnp.sin(angle)[:, None, :]


def rotate(value, cosine, sine):
    half = value.shape[-1] // 2
    first, second = value[..., :half], value[..., half:]
    return jnp.concatenate(
        [first * cosine - second * sine, second * cosine + first * sine], axis=-1
    )


def gelu_tanh(value):
    return jnp.tanh(GELU_SCALE * (value + GELU_CUBE * value * value * value))


def gelu(value):
    return 0.5 * value * (1.0 + gelu_tanh(value))


def gelu_slope(value):
    t = gelu_tanh(value)
    inner = GELU_SCALE * (1.0 + 3.0 * GELU_CUBE * value * value)
    return 0.5 * (1.0 + t) + 0.5 * value * (1.0 - t * t) * inner


def shift(block, pieces, distance):
    route = [
        (c * pieces + i, c * pieces + i + distance)
        for c in range(2)
        for i in range(pieces)
        if 0 <= i + distance < pieces
    ]
    return lax.ppermute(block, "g", route)


def group_gather(block):
    return lax.all_gather(block, "g", axis=0, tiled=True)


def group_scatter(partial):
    return lax.psum_scatter(partial, "g", scatter_dimension=0, tiled=True)


def column_chunks(weight, planes, ranks):
    depth, width = weight.shape
    part = width // (planes * ranks)
    split = weight.reshape(depth, planes, ranks, part).transpose(2, 0, 1, 3)
    moved = lax.all_to_all(split.reshape(ranks, depth, planes * part), "g", 0, 0)
    return lax.all_gather(
        moved.reshape(ranks * depth, planes * part), "pl", axis=0, tiled=True
    )


def column_chunks_back(grad, planes, ranks):
    mine = lax.psum_scatter(grad.astype(BF16), "pl", scatter_dimension=0, tiled=True)
    depth, width = mine.shape[0] // ranks, mine.shape[1]
    part = width // planes
    moved = lax.all_to_all(mine.reshape(ranks, depth, width), "g", 0, 0)
    moved = moved.reshape(ranks, depth, planes, part).transpose(1, 2, 0, 3)
    return moved.reshape(depth, planes * ranks * part).astype(F32)


def layer(planes, ranks, *args):
    (
        hidden_in,
        layer_input,
        seq_lengths,
        cotangent,
        gate_weight,
        up_weight,
        down_weight,
        first,
        second,
        head_gain,
    ) = args
    rows, width = hidden_in.shape
    pieces = ranks // 2
    hops = max(1, WINDOW // rows)
    groups = QUERY_HEADS // KEY_VALUE_HEADS
    piece = lax.rem(lax.axis_index("g"), pieces)
    places = piece * rows + jnp.arange(rows, dtype=jnp.int32)
    key_places = (piece - hops) * rows + jnp.arange((hops + 1) * rows, dtype=jnp.int32)
    live = (places < seq_lengths[0]).astype(F32)[:, None]

    head_width = QUERY_HEADS * HEAD_SIZE
    kv_width = KEY_VALUE_HEADS * HEAD_SIZE
    rank = first.shape[1] - head_width - 2 * kv_width
    side = layer_input.shape[1]
    head_gain = head_gain.astype(F32)
    output_all = second[:, :head_width]
    at = head_width
    side_gate_all = second[:, at : at + side]
    at += side
    right_all = second[:, at : at + rank]
    at += rank
    projection_all = second[:, at : at + side]
    at += side
    gains = second[:, at:].T.astype(F32)
    gate_cols = column_chunks(gate_weight, planes, ranks)
    up_cols = column_chunks(up_weight, planes, ranks)
    down_rows = lax.all_gather(down_weight, "pl", axis=0, tiled=True)

    hidden = hidden_in.astype(F32)
    side_input = layer_input.astype(F32)
    cosine, sine = rope_tables(places)

    hidden_inv = inverse_rms(hidden)
    normed = hidden * hidden_inv * gains[0]
    normed_low = normed.astype(BF16)
    raw = dot(normed_low, first)
    query_raw = raw[:, :head_width].reshape(rows, QUERY_HEADS, HEAD_SIZE)
    key_raw = raw[:, head_width : head_width + kv_width].reshape(rows, KEY_VALUE_HEADS, HEAD_SIZE)
    value_raw = raw[:, head_width + kv_width : head_width + 2 * kv_width].reshape(
        rows, KEY_VALUE_HEADS, HEAD_SIZE
    )
    left_low = raw[:, head_width + 2 * kv_width :].astype(BF16)
    query_inv = inverse_rms(query_raw)
    key_inv = inverse_rms(key_raw)
    value_inv = inverse_rms(value_raw)
    query_low = rotate(query_raw * query_inv * head_gain[0], cosine, sine).astype(BF16)
    key_low = rotate(key_raw * key_inv * head_gain[1], cosine, sine).astype(BF16)
    value_low = (value_raw * value_inv).astype(BF16)
    moving = jnp.stack([key_low, value_low])
    window = [moving]
    for hop in range(hops):
        moving = shift(moving, pieces, 1)
        window.insert(0, moving)
    window = jnp.concatenate(window, axis=1)
    grouped = query_low.reshape(rows, KEY_VALUE_HEADS, groups, HEAD_SIZE)
    scores = jnp.einsum("qkgd,tkd->kgqt", grouped, window[0], preferred_element_type=F32)
    allowed = (
        (key_places[None, :] <= places[:, None])
        & (places[:, None] - key_places[None, :] < WINDOW)
        & (key_places[None, :] >= 0)
    )
    scores = jnp.where(allowed, scores, MASKED)
    weights = jnp.exp(scores - jnp.max(scores, axis=-1, keepdims=True))
    probs = weights / jnp.sum(weights, axis=-1, keepdims=True)
    probs_low = probs.astype(BF16)
    mixed = (
        jnp.einsum("kgqt,tkd->qkgd", probs_low, window[1], preferred_element_type=F32)
        .reshape(rows, head_width)
        .astype(BF16)
    )
    attention_raw = dot(mixed, output_all)
    attention_inv = inverse_rms(attention_raw)
    right_raw = dot(left_low, right_all, 1, 1)
    right_inv = inverse_rms(right_raw)
    merged = (
        hidden
        + attention_raw * attention_inv * gains[1]
        + normed
        + right_raw * right_inv * gains[2]
    ) * HALF_ROOT
    merged_inv = inverse_rms(merged)
    expand_low = (merged * merged_inv * gains[3]).astype(BF16)

    expand_all = group_gather(expand_low)
    gate_raw = dot(expand_all, gate_cols)
    up_raw = dot(expand_all, up_cols)
    act_low = (gelu(gate_raw) * up_raw).astype(BF16)
    reduced_raw = group_scatter(dot(act_low, down_rows).astype(BF16)).astype(F32)
    reduced_inv = inverse_rms(reduced_raw)
    after_feed = merged + reduced_raw * reduced_inv * gains[4]
    after_low = after_feed.astype(BF16)
    side_raw = dot(after_low, side_gate_all)
    side_low = (gelu(side_raw) * side_input).astype(BF16)
    side_out = dot(side_low, projection_all, 1, 1)
    side_inv = inverse_rms(side_out)
    block_out = (after_feed + side_out * side_inv * gains[5]) * live

    upstream = cotangent.astype(F32) * live
    grad_side, gain_five = rms_back(side_out, side_inv, gains[5], upstream)
    grad_side_low = grad_side.astype(BF16)
    grad_side_raw = (
        dot(grad_side_low, projection_all) * side_input * gelu_slope(side_raw)
    ).astype(BF16)
    grad_after = upstream + dot(grad_side_raw, side_gate_all, 1, 1)
    grad_reduced, gain_four = rms_back(reduced_raw, reduced_inv, gains[4], grad_after)
    grad_reduced_low = grad_reduced.astype(BF16)

    grad_reduced_all = group_gather(grad_reduced_low)
    grad_product = dot(grad_reduced_all, down_rows, 1, 1)
    grad_gate_low = (grad_product * up_raw * gelu_slope(gate_raw)).astype(BF16)
    grad_up_low = (grad_product * gelu(gate_raw)).astype(BF16)
    part = group_scatter(
        (dot(grad_gate_low, gate_cols, 1, 1) + dot(grad_up_low, up_cols, 1, 1)).astype(BF16)
    ).astype(F32)
    grad_down = lax.psum_scatter(
        dot(act_low, grad_reduced_all, 0, 0).astype(BF16), "pl", scatter_dimension=0, tiled=True
    ).astype(F32)
    grad_gate = column_chunks_back(dot(expand_all, grad_gate_low, 0, 0), planes, ranks)
    grad_up = column_chunks_back(dot(expand_all, grad_up_low, 0, 0), planes, ranks)

    grad_merged, gain_three = rms_back(merged, merged_inv, gains[3], part)
    grad_sum = (grad_after + grad_merged) * HALF_ROOT
    grad_right, gain_two = rms_back(right_raw, right_inv, gains[2], grad_sum)
    grad_right_low = grad_right.astype(BF16)
    grad_left_low = dot(grad_right_low, right_all).astype(BF16)
    grad_attention, gain_one = rms_back(attention_raw, attention_inv, gains[1], grad_sum)
    grad_attention_low = grad_attention.astype(BF16)
    grad_mixed = (
        dot(grad_attention_low, output_all, 1, 1)
        .astype(BF16)
        .reshape(rows, KEY_VALUE_HEADS, groups, HEAD_SIZE)
    )
    grad_probs = jnp.einsum("qkgd,tkd->kgqt", grad_mixed, window[1], preferred_element_type=F32)
    inner = jnp.sum(probs * grad_probs, axis=-1, keepdims=True)
    grad_scores = (probs * (grad_probs - inner)).astype(BF16)
    grad_query_rot = jnp.einsum(
        "kgqt,tkd->qkgd", grad_scores, window[0], preferred_element_type=F32
    ).reshape(rows, QUERY_HEADS, HEAD_SIZE)
    grad_window = jnp.stack(
        [
            jnp.einsum("kgqt,qkgd->tkd", grad_scores, grouped, preferred_element_type=F32),
            jnp.einsum("kgqt,qkgd->tkd", probs_low, grad_mixed, preferred_element_type=F32),
        ]
    )
    carried = grad_window[:, :rows]
    for hop in range(hops - 1, -1, -1):
        begin = (hops - hop) * rows
        carried = shift(carried.astype(BF16), pieces, -1).astype(F32)
        carried = carried + grad_window[:, begin : begin + rows]
    grad_query, head_zero = rms_back(
        query_raw, query_inv, head_gain[0], rotate(grad_query_rot, cosine, -sine)
    )
    grad_key, head_one = rms_back(
        key_raw, key_inv, head_gain[1], rotate(carried[0], cosine, -sine)
    )
    grad_value, _ = rms_back(value_raw, value_inv, 1.0, carried[1])
    grad_raw = jnp.concatenate(
        [
            grad_query.reshape(rows, head_width).astype(BF16),
            grad_key.reshape(rows, kv_width).astype(BF16),
            grad_value.reshape(rows, kv_width).astype(BF16),
            grad_left_low,
        ],
        axis=1,
    )
    grad_normed = grad_sum + dot(grad_raw, first, 1, 1)
    grad_input, gain_zero = rms_back(hidden, hidden_inv, gains[0], grad_normed)
    grad_hidden = grad_sum + grad_input

    gain_grads = jnp.stack(
        [
            jnp.sum(g, axis=0)
            for g in (gain_zero, gain_one, gain_two, gain_three, gain_four, gain_five)
        ]
    )
    head_grads = jnp.stack([jnp.sum(head_zero, axis=(0, 1)), jnp.sum(head_one, axis=(0, 1))])

    def spread(grad, dim=0):
        grad = lax.psum_scatter(grad, "pl", scatter_dimension=dim, tiled=True)
        return lax.psum_scatter(grad, "g", scatter_dimension=dim, tiled=True)

    early = jnp.concatenate(
        [
            dot(mixed, grad_attention_low, 0, 0),
            dot(after_low, grad_side_raw, 0, 0),
            dot(grad_right_low, left_low, 0, 0),
            dot(grad_side_low, side_low, 0, 0),
        ],
        axis=1,
    ).astype(BF16)
    early = spread(early).astype(F32)
    late = spread(dot(normed_low, grad_raw, 0, 0).astype(BF16)).astype(F32)
    d_gains = spread(gain_grads, 1)
    d_heads = spread(head_grads, 1)
    d_output = early[:, :head_width]
    at = head_width
    d_side_gate = early[:, at : at + side]
    at += side
    d_right = early[:, at : at + rank].T
    at += rank
    d_projection = early[:, at : at + side].T
    d_query = late[:, :head_width]
    d_key = late[:, head_width : head_width + kv_width]
    d_value = late[:, head_width + kv_width : head_width + 2 * kv_width]
    d_left = late[:, head_width + 2 * kv_width :]
    return (
        block_out,
        grad_hidden,
        d_query,
        d_key,
        d_value,
        d_output,
        d_left,
        d_right,
        d_side_gate,
        d_projection,
        grad_gate,
        grad_up,
        grad_down,
        d_gains,
        d_heads,
    )


def gather_weights(
    query_weight,
    key_matrix,
    value_matrix,
    output_weight,
    laurel_left,
    laurel_right,
    input_gate,
    input_projection,
    norm_gains,
    head_gains,
):
    both = ("dp", "seq")
    first = jnp.concatenate([query_weight, key_matrix, value_matrix, laurel_left], axis=1)
    second = jnp.concatenate(
        [output_weight, input_gate, laurel_right.T, input_projection.T, norm_gains.T], axis=1
    )
    return (
        lax.all_gather(first, both, axis=0, tiled=True),
        lax.all_gather(second, both, axis=0, tiled=True),
        lax.all_gather(head_gains, both, axis=1, tiled=True),
    )


def solution(mesh):
    pieces = mesh.shape["seq"]
    planes, ranks = mesh.shape["dp"] // 2, 2 * pieces
    grid = Mesh(mesh.devices.reshape(planes, ranks), ("pl", "g"))

    def body(*args):
        whole_row, whole_column = P(("dp", "seq"), None), P(None, ("dp", "seq"))
        gathered = jax.shard_map(
            gather_weights,
            mesh=mesh,
            in_specs=(whole_row,) * 5
            + (whole_column, whole_row, whole_column, whole_column, whole_column),
            out_specs=(P(None, None),) * 3,
            check_vma=False,
        )(*args[4:12], *args[15:17])
        row, column = P(("pl", "g"), None), P(None, ("pl", "g"))
        lengths = jnp.repeat(args[2], pieces)
        return jax.shard_map(
            lambda *inner: layer(planes, ranks, *inner),
            mesh=grid,
            in_specs=(row, row, P(("pl", "g")), row, row, row, row) + (P(None, None),) * 3,
            out_specs=(row,) * 7 + (column, row, column) + (row,) * 3 + (column,) * 2,
            check_vma=False,
        )(args[0], args[1], lengths, args[3], *args[12:15], *gathered)

    return body
```

```python
import jax
import jax.numpy as jnp
from jax import lax
from jax.experimental import pallas as pl
from jax.experimental.pallas import tpu as pltpu
from jax.sharding import Mesh, PartitionSpec as P

QUERY_HEADS = 8
KEY_VALUE_HEADS = 2
HEAD_SIZE = 256
WINDOW = 512
EPSILON = 1e-06
ROPE_BASE = 10000.0
HALF_ROOT = 0.7071067811865476
MASKED = -1e30
GELU_SCALE = 0.7978845608028654
GELU_CUBE = 0.044715
F32 = jnp.float32
BF16 = jnp.bfloat16


def dot(left, right, left_dim=1, right_dim=0):
    return lax.dot_general(
        left, right, (((left_dim,), (right_dim,)), ((), ())), preferred_element_type=F32
    )


def inverse_rms(value):
    return lax.rsqrt(jnp.mean(value * value, axis=-1, keepdims=True) + EPSILON)


def rms_back(value, inverse, gain, grad):
    scaled = grad * gain
    inner = jnp.mean(scaled * value, axis=-1, keepdims=True)
    unit = value * inverse
    return inverse * (scaled - unit * (inverse * inner)), grad * unit


def rope_tables(positions):
    half = HEAD_SIZE // 2
    rate = ROPE_BASE ** (-jnp.arange(half, dtype=F32) * 2.0 / HEAD_SIZE)
    angle = positions.astype(F32)[:, None] * rate[None, :]
    return jnp.cos(angle)[:, None, :], jnp.sin(angle)[:, None, :]


def rotate(value, cosine, sine):
    half = value.shape[-1] // 2
    first, second = value[..., :half], value[..., half:]
    return jnp.concatenate(
        [first * cosine - second * sine, second * cosine + first * sine], axis=-1
    )


def gelu_tanh(value):
    return jnp.tanh(GELU_SCALE * (value + GELU_CUBE * value * value * value))


def gelu(value):
    return 0.5 * value * (1.0 + gelu_tanh(value))


def gelu_slope(value):
    t = gelu_tanh(value)
    inner = GELU_SCALE * (1.0 + 3.0 * GELU_CUBE * value * value)
    return 0.5 * (1.0 + t) + 0.5 * value * (1.0 - t * t) * inner


AXES = ("y", "xc", "h", "l")
TEAM = ("xc", "l")
COPIES = ("y", "h")


class Sender:
    def __init__(self, send, recv):
        self.send, self.recv, self.count, self.started = send, recv, 0, []

    def go(self, source, target, peer):
        i = self.count
        self.count += 1
        copy = pltpu.make_async_remote_copy(
            src_ref=source,
            dst_ref=target,
            send_sem=self.send.at[i],
            recv_sem=self.recv.at[i],
            device_id=peer,
            device_id_type=pl.DeviceIdType.MESH,
        )
        copy.start()
        self.started.append(copy)
        return copy

    def finish(self):
        for copy in self.started:
            copy.wait_send()


def greet(peers):
    barrier = pltpu.get_barrier_semaphore()
    for peer in peers:
        pl.semaphore_signal(barrier, inc=1, device_id=peer, device_id_type=pl.DeviceIdType.MESH)
    pl.semaphore_wait(barrier, len(peers))


def plus(*parts):
    total = parts[0].astype(F32)
    for part in parts[1:]:
        total = total + part.astype(F32)
    return total


def remote_call(kernel, out, copies, identity, scratch=(), vmem=None, out_space=pl.ANY):
    return pl.pallas_call(
        kernel,
        out_shape=out,
        in_specs=[pl.BlockSpec(memory_space=pl.ANY)],
        out_specs=pl.BlockSpec(memory_space=out_space),
        scratch_shapes=[
            pltpu.SemaphoreType.DMA((copies,)),
            pltpu.SemaphoreType.DMA((copies,)),
            *scratch,
        ],
        compiler_params=pltpu.CompilerParams(
            collective_id=identity, has_side_effects=True, vmem_limit_bytes=vmem
        ),
    )


def team_places():
    xc, l = lax.axis_index("xc"), lax.axis_index("l")
    core = lax.rem(xc, 2)
    other = xc + 1 - 2 * core
    cross, side = lax.rem(xc + 2, 4), 1 - l
    own = {"O": xc * 2 + l, "X": cross * 2 + l, "L": xc * 2 + side, "D": cross * 2 + side}
    far = lax.rem(other + 2, 4)
    twin = {"O": other * 2 + l, "X": far * 2 + l, "L": other * 2 + side, "D": far * 2 + side}
    return own, twin, {"xc": other}, {"xc": cross}, {"l": side}


def team_gather_kernel(x_ref, o_ref, send, recv, local):
    own, _, core, cross, side = team_places()
    half = x_ref.shape[0] // 2
    top, low = pl.ds(0, half), pl.ds(half, half)
    keep = pltpu.make_async_copy(x_ref, o_ref.at[own["O"]], local)
    keep.start()
    greet([core, cross, side])
    out = Sender(send, recv)
    mine, from_side, from_cross = o_ref.at[own["O"]], o_ref.at[own["L"]], o_ref.at[own["X"]]
    diagonal = o_ref.at[own["D"]]
    side_top = out.go(x_ref.at[top], mine.at[top], side)
    cross_low = out.go(x_ref.at[low], mine.at[low], cross)
    side_low = out.go(x_ref.at[low], mine.at[low], side)
    cross_top = out.go(x_ref.at[top], mine.at[top], cross)
    twins = [out.go(x_ref, mine, core)]
    side_top.wait_recv()
    diagonal_top = out.go(from_side.at[top], from_side.at[top], cross)
    twins.append(out.go(from_side.at[top], from_side.at[top], core))
    cross_low.wait_recv()
    diagonal_low = out.go(from_cross.at[low], from_cross.at[low], side)
    twins.append(out.go(from_cross.at[low], from_cross.at[low], core))
    side_low.wait_recv()
    twins.append(out.go(from_side.at[low], from_side.at[low], core))
    cross_top.wait_recv()
    twins.append(out.go(from_cross.at[top], from_cross.at[top], core))
    diagonal_top.wait_recv()
    twins.append(out.go(diagonal.at[top], diagonal.at[top], core))
    diagonal_low.wait_recv()
    twins.append(out.go(diagonal.at[low], diagonal.at[low], core))
    for copy in twins:
        copy.wait_recv()
    out.finish()
    keep.wait()


def team_gather(block):
    rows, width = block.shape
    gathered = remote_call(
        team_gather_kernel,
        jax.ShapeDtypeStruct((8, rows, width), block.dtype),
        13,
        0,
        [pltpu.SemaphoreType.DMA],
    )(block)
    return gathered.reshape(8 * rows, width)


def team_scatter_kernel(p_ref, o_ref, send, recv, local, mine, twin_in, cross_in, side_in, bent_in):
    own, twin, core, cross, side = team_places()
    half = p_ref.shape[1] // 2
    top, low = pl.ds(0, half), pl.ds(half, half)
    loads = []
    for i, k in enumerate("DXLO"):
        loads.append(pltpu.make_async_copy(p_ref.at[own[k]], mine.at[i], local.at[i]))
        loads[-1].start()
    greet([core, cross, side])
    out = Sender(send, recv)
    swaps = [out.go(p_ref.at[twin[k]], twin_in.at[i], core) for i, k in enumerate("DXLO")]

    def join(i):
        loads[i].wait()
        swaps[i].wait_recv()
        mine[i] = plus(mine[i], twin_in[i]).astype(BF16)

    join(0)
    bent_cross = out.go(mine.at[0].at[top], bent_in.at[0], cross)
    bent_side = out.go(mine.at[0].at[low], bent_in.at[1], side)
    join(1)
    cross_top = out.go(mine.at[1].at[top], cross_in.at[top], cross)
    join(2)
    side_low = out.go(mine.at[2].at[low], side_in.at[low], side)
    bent_cross.wait_recv()
    mine[2, top] = plus(mine[2, top], bent_in[0]).astype(BF16)
    side_top = out.go(mine.at[2].at[top], side_in.at[top], side)
    bent_side.wait_recv()
    mine[1, low] = plus(mine[1, low], bent_in[1]).astype(BF16)
    cross_low = out.go(mine.at[1].at[low], cross_in.at[low], cross)
    loads[3].wait()
    swaps[3].wait_recv()
    o_ref[...] = plus(mine[3], twin_in[3])
    cross_top.wait_recv()
    side_low.wait_recv()
    o_ref[top] += cross_in[top].astype(F32)
    o_ref[low] += side_in[low].astype(F32)
    side_top.wait_recv()
    cross_low.wait_recv()
    o_ref[top] += side_in[top].astype(F32)
    o_ref[low] += cross_in[low].astype(F32)
    out.finish()


def team_scatter(partial_sum):
    rows, width = partial_sum.shape[0] // 8, partial_sum.shape[1]
    return remote_call(
        team_scatter_kernel,
        jax.ShapeDtypeStruct((rows, width), F32),
        10,
        1,
        [
            pltpu.SemaphoreType.DMA((4,)),
            pltpu.VMEM((4, rows, width), BF16),
            pltpu.VMEM((4, rows, width), BF16),
            pltpu.VMEM((rows, width), BF16),
            pltpu.VMEM((rows, width), BF16),
            pltpu.VMEM((2, rows // 2, width), BF16),
        ],
        40 * 2**20,
        pltpu.VMEM,
    )(partial_sum.reshape(8, rows, width))


def team_swap_kernel(x_ref, o_ref, send, recv, local):
    xc, l = lax.axis_index("xc"), lax.axis_index("l")
    me = xc * 2 + l
    keep = pltpu.make_async_copy(x_ref.at[me], o_ref.at[me], local)
    keep.start()
    places = []
    for i in range(1, 8):
        far, side = lax.rem(xc + i // 2, 4), lax.rem(l + i % 2, 2)
        back = lax.rem(xc + 4 - i // 2, 4)
        places.append((far * 2 + side, {"xc": far, "l": side}, back * 2 + side))
    greet([peer for _, peer, _ in places])
    out = Sender(send, recv)
    for rank, peer, _ in places:
        out.go(x_ref.at[rank], o_ref.at[me], peer)
    for copy in out.started:
        copy.wait_recv()
    out.finish()
    keep.wait()


def team_swap(blocks):
    return remote_call(
        team_swap_kernel,
        jax.ShapeDtypeStruct(blocks.shape, blocks.dtype),
        7,
        2,
        [pltpu.SemaphoreType.DMA],
    )(blocks)


def full_places():
    y, xc = lax.axis_index("y"), lax.axis_index("xc")
    h, l = lax.axis_index("h"), lax.axis_index("l")
    core = lax.rem(xc, 2)

    def rank(plane, depth, twin=False):
        b = xc + 1 - 2 * core if twin else xc
        b = lax.rem(b + 2, 4) if plane in "XD" else b
        a = 1 - y if plane in "YD" else y
        u = 1 - h if depth in ("H", "HL") else h
        v = 1 - l if depth in ("L", "HL") else l
        return ((a * 4 + b) * 2 + u) * 2 + v

    peers = {
        "C": {"xc": xc + 1 - 2 * core},
        "X": {"xc": lax.rem(xc + 2, 4)},
        "Y": {"y": 1 - y},
        "H": {"h": 1 - h},
        "L": {"l": 1 - l},
    }
    return rank, peers


DEPTHS = ("O", "L", "H", "HL")


def full_gather_kernel(x_ref, o_ref, send, recv, local):
    rank, peers = full_places()
    half = x_ref.shape[0] // 2
    top, low = pl.ds(0, half), pl.ds(half, half)

    def at(plane, depth):
        return o_ref.at[rank(plane, depth)]

    keep = pltpu.make_async_copy(x_ref, at("O", "O"), local)
    keep.start()
    greet(list(peers.values()))
    out = Sender(send, recv)
    twins = []
    to_h = out.go(x_ref, at("O", "O"), peers["H"])
    to_l = out.go(x_ref, at("O", "O"), peers["L"])
    direct, bent = {}, {}

    def begin(depth):
        source = x_ref if depth == "O" else at("O", depth)
        target = at("O", depth)
        y_top = out.go(source.at[top], target.at[top], peers["Y"])
        x_low = out.go(source.at[low], target.at[low], peers["X"])
        y_low = out.go(source.at[low], target.at[low], peers["Y"])
        x_top = out.go(source.at[top], target.at[top], peers["X"])
        twins.append(out.go(source, target, peers["C"]))
        direct[depth] = (y_top, x_low, y_low, x_top)

    def bend(depth):
        y_top, x_low, y_low, x_top = direct[depth]
        y_top.wait_recv()
        piece = at("Y", depth).at[top]
        bent_top = out.go(piece, piece, peers["X"])
        x_low.wait_recv()
        piece = at("X", depth).at[low]
        bent_low = out.go(piece, piece, peers["Y"])
        y_low.wait_recv()
        twins.append(out.go(at("Y", depth), at("Y", depth), peers["C"]))
        x_top.wait_recv()
        twins.append(out.go(at("X", depth), at("X", depth), peers["C"]))
        bent[depth] = (bent_top, bent_low)

    def close(depth):
        for copy in bent[depth]:
            copy.wait_recv()
        twins.append(out.go(at("D", depth), at("D", depth), peers["C"]))

    begin("O")
    to_h.wait_recv()
    to_hl = out.go(at("O", "H"), at("O", "H"), peers["L"])
    to_l.wait_recv()
    begin("L")
    bend("O")
    begin("H")
    bend("L")
    to_hl.wait_recv()
    begin("HL")
    bend("H")
    close("O")
    close("L")
    bend("HL")
    close("H")
    close("HL")
    for copy in twins:
        copy.wait_recv()
    out.finish()
    keep.wait()


def full_gather(block):
    rows, width = block.shape
    if lax.axis_size("y") != 2 or lax.axis_size("h") != 2:
        gathered = lax.all_gather(block, AXES, axis=0, tiled=False)
    else:
        gathered = remote_call(
            full_gather_kernel,
            jax.ShapeDtypeStruct((32, rows, width), block.dtype),
            43,
            3,
            [pltpu.SemaphoreType.DMA],
        )(block)
    return gathered.reshape(-1, width)


PLANES = ("D", "X", "Y", "O")
SUMS = ("HL", "L", "H", "O")


def full_scatter_kernel(
    p_ref, o_ref, send, recv, local, mine, twin_in, cross_in, lane_in, bent_in, depth_in
):
    rank, peers = full_places()
    half = p_ref.shape[1] // 2
    top, low = pl.ds(0, half), pl.ds(half, half)
    loads, swaps, flights = {}, {}, {}
    for t, depth in enumerate(SUMS):
        for k, plane in enumerate(PLANES):
            load = pltpu.make_async_copy(
                p_ref.at[rank(plane, depth)], mine.at[t, k], local.at[t * 4 + k]
            )
            load.start()
            loads[t, k] = load
    greet(list(peers.values()))
    out = Sender(send, recv)
    for t, depth in enumerate(SUMS):
        for k, plane in enumerate(PLANES):
            swaps[t, k] = out.go(
                p_ref.at[rank(plane, depth, True)], twin_in.at[t, k], peers["C"]
            )

    def join(t, k):
        loads[t, k].wait()
        swaps[t, k].wait_recv()
        mine[t, k] = plus(mine[t, k], twin_in[t, k]).astype(BF16)

    def begin(t):
        join(t, 0)
        bent_x = out.go(mine.at[t, 0].at[top], bent_in.at[t, 0], peers["X"])
        bent_y = out.go(mine.at[t, 0].at[low], bent_in.at[t, 1], peers["Y"])
        join(t, 1)
        x_top = out.go(mine.at[t, 1].at[top], cross_in.at[t].at[top], peers["X"])
        join(t, 2)
        y_low = out.go(mine.at[t, 2].at[low], lane_in.at[t].at[low], peers["Y"])
        join(t, 3)
        flights[t] = [bent_x, bent_y, x_top, y_low]

    def bend(t):
        bent_x, bent_y, x_top, y_low = flights[t]
        bent_x.wait_recv()
        mine[t, 2, top] = plus(mine[t, 2, top], bent_in[t, 0]).astype(BF16)
        y_top = out.go(mine.at[t, 2].at[top], lane_in.at[t].at[top], peers["Y"])
        bent_y.wait_recv()
        mine[t, 1, low] = plus(mine[t, 1, low], bent_in[t, 1]).astype(BF16)
        x_low = out.go(mine.at[t, 1].at[low], cross_in.at[t].at[low], peers["X"])
        flights[t] = [x_top, y_low, y_top, x_low]

    def close(t):
        for copy in flights[t]:
            copy.wait_recv()
        return plus(mine[t, 3], cross_in[t], lane_in[t])

    begin(0)
    begin(1)
    bend(0)
    begin(2)
    bend(1)
    mine[0, 3] = close(0).astype(BF16)
    to_hl = out.go(mine.at[0, 3], depth_in.at[0], peers["L"])
    begin(3)
    bend(2)
    mine[1, 3] = close(1).astype(BF16)
    to_l = out.go(mine.at[1, 3], depth_in.at[1], peers["L"])
    bend(3)
    total = close(2)
    to_hl.wait_recv()
    mine[2, 3] = plus(total, depth_in[0]).astype(BF16)
    to_h = out.go(mine.at[2, 3], depth_in.at[2], peers["H"])
    total = close(3)
    to_l.wait_recv()
    total = plus(total, depth_in[1])
    to_h.wait_recv()
    o_ref[...] = plus(total, depth_in[2])
    out.finish()


def full_scatter(partial_sum):
    shares = lax.axis_size("y") * lax.axis_size("h") * 8
    rows, width = partial_sum.shape[0] // shares, partial_sum.shape[1]
    blocks = partial_sum.reshape(shares, rows, width)
    if lax.axis_size("y") != 2 or lax.axis_size("h") != 2:
        return lax.psum_scatter(blocks, AXES, scatter_dimension=0, tiled=False).astype(F32)
    return remote_call(
        full_scatter_kernel,
        jax.ShapeDtypeStruct((rows, width), F32),
        43,
        4,
        [
            pltpu.SemaphoreType.DMA((16,)),
            pltpu.VMEM((4, 4, rows, width), BF16),
            pltpu.VMEM((4, 4, rows, width), BF16),
            pltpu.VMEM((4, rows, width), BF16),
            pltpu.VMEM((4, rows, width), BF16),
            pltpu.VMEM((4, 2, rows // 2, width), BF16),
            pltpu.VMEM((3, rows, width), BF16),
        ],
        56 * 2**20,
        pltpu.VMEM,
    )(blocks)


def shift(block, distance):
    pieces = lax.axis_size("h") * lax.axis_size("l")
    route = [(i, i + distance) for i in range(pieces) if 0 <= i + distance < pieces]
    return lax.ppermute(block, ("h", "l"), route)


def pull(block, axis, distance):
    size = lax.axis_size(axis)
    return lax.ppermute(block, axis, [(i, (i - distance) % size) for i in range(size)])


def copies_place(dy, dh):
    ys, hs = lax.axis_size("y"), lax.axis_size("h")
    y, h = lax.axis_index("y"), lax.axis_index("h")
    return lax.rem(y + dy, ys) * hs + lax.rem(h + dh, hs)


def copies_gather(block):
    ys, hs = lax.axis_size("y"), lax.axis_size("h")
    along = [block] + [pull(block, "h", k) for k in range(1, hs)]
    gathered = jnp.zeros((ys * hs * block.shape[0], block.shape[1]), block.dtype)
    for dy in range(ys):
        for dh in range(hs):
            piece = along[dh] if dy == 0 else pull(along[dh], "y", dy)
            start = copies_place(dy, dh) * block.shape[0]
            gathered = lax.dynamic_update_slice_in_dim(gathered, piece, start, axis=0)
    return gathered


def copies_scatter(partial_sum):
    ys, hs = lax.axis_size("y"), lax.axis_size("h")
    rows = partial_sum.shape[0] // (ys * hs)

    def piece(dy, dh):
        return lax.dynamic_slice_in_dim(partial_sum, copies_place(dy, dh) * rows, rows, axis=0)

    along = []
    for dh in range(hs):
        arrived = [pull(piece(dy, dh), "y", -dy) for dy in range(1, ys)]
        along.append((piece(0, dh), arrived))
    ready = [plus(own, *arrived).astype(BF16) for own, arrived in along[1:]]
    moved = [pull(ready[dh - 1], "h", -dh) for dh in range(1, hs)]
    return plus(along[0][0], *along[0][1], *moved)


def column_blocks(weight):
    ys, hs = lax.axis_size("y"), lax.axis_size("h")
    depth, width = weight.shape
    split = weight.reshape(depth, ys, 4, hs, 2, width // (ys * hs * 8))
    return split.transpose(2, 4, 0, 1, 3, 5).reshape(8, depth, width // 8)


def from_column_blocks(blocks):
    ys, hs = lax.axis_size("y"), lax.axis_size("h")
    depth, width = blocks.shape[1:]
    split = blocks.reshape(4, 2, depth, ys, hs, width // (ys * hs)).transpose(2, 3, 0, 4, 1, 5)
    return split.reshape(depth, 8 * width)


def depth_order(value):
    ys, hs = lax.axis_size("y"), lax.axis_size("h")
    rows, width = value.shape
    split = value.reshape(rows, ys, 4, hs, width // (4 * ys * hs))
    return split.transpose(0, 1, 3, 2, 4).reshape(rows, width)


def from_depth_order(value):
    ys, hs = lax.axis_size("y"), lax.axis_size("h")
    rows, width = value.shape
    split = value.reshape(rows, ys, hs, 4, width // (4 * ys * hs))
    return split.transpose(0, 1, 3, 2, 4).reshape(rows, width)


def layer(*args):
    (
        hidden_in,
        layer_input,
        seq_lengths,
        cotangent,
        query_weight,
        key_matrix,
        value_matrix,
        output_weight,
        laurel_left,
        laurel_right,
        input_gate,
        input_projection,
        gate_weight,
        up_weight,
        down_weight,
        norm_gains,
        head_gains,
    ) = args
    rows, width = hidden_in.shape
    hops = max(1, WINDOW // rows)
    groups = QUERY_HEADS // KEY_VALUE_HEADS
    piece = lax.axis_index(("h", "l"))
    places = piece * rows + jnp.arange(rows, dtype=jnp.int32)
    key_places = (piece - hops) * rows + jnp.arange((hops + 1) * rows, dtype=jnp.int32)
    live = (places < seq_lengths[0]).astype(F32)[:, None]

    head_width = QUERY_HEADS * HEAD_SIZE
    kv_width = KEY_VALUE_HEADS * HEAD_SIZE
    rank = laurel_left.shape[1]
    side = layer_input.shape[1]
    depth, head_part = query_weight.shape[0], head_gains.shape[1]
    columns = (
        query_weight,
        key_matrix,
        value_matrix,
        output_weight,
        input_gate,
        input_projection.T,
        laurel_left,
        laurel_right.T,
        norm_gains.T,
        jnp.pad(head_gains.T, ((0, depth - head_part), (0, 0))),
    )
    edges = [0]
    for column in columns:
        edges.append(edges[-1] + column.shape[1])
    full_width = -(-edges[-1] // 128) * 128
    swapped = team_swap(
        jnp.concatenate([column_blocks(gate_weight), column_blocks(up_weight)], axis=1)
    )
    gate_cols = copies_gather(swapped[:, :depth].reshape(8 * depth, -1))
    up_cols = copies_gather(swapped[:, depth:].reshape(8 * depth, -1))
    down_rows = copies_gather(down_weight)
    full = full_gather(
        jnp.pad(jnp.concatenate(columns, axis=1), ((0, 0), (0, full_width - edges[-1])))
    )
    first = full[:, : edges[3]]
    output_all, side_gate_all, projection_all, left_all, right_all = (
        full[:, edges[i] : edges[i + 1]] for i in range(3, 8)
    )
    gains = full[:, edges[8] : edges[9]].T.astype(F32)
    head_gain = (
        full[:, edges[9] : edges[10]].reshape(-1, depth, 2)[:, :head_part].reshape(-1, 2).T
    ).astype(F32)

    hidden = hidden_in.astype(F32)
    side_input = layer_input.astype(F32)
    cosine, sine = rope_tables(places)

    hidden_inv = inverse_rms(hidden)
    normed = hidden * hidden_inv * gains[0]
    normed_low = normed.astype(BF16)
    raw = dot(normed_low, first)
    query_raw = raw[:, :head_width].reshape(rows, QUERY_HEADS, HEAD_SIZE)
    key_raw = raw[:, head_width : head_width + kv_width].reshape(rows, KEY_VALUE_HEADS, HEAD_SIZE)
    value_raw = raw[:, head_width + kv_width :].reshape(
        rows, KEY_VALUE_HEADS, HEAD_SIZE
    )
    left_low = dot(normed_low, left_all).astype(BF16)
    query_inv = inverse_rms(query_raw)
    key_inv = inverse_rms(key_raw)
    value_inv = inverse_rms(value_raw)
    query_low = rotate(query_raw * query_inv * head_gain[0], cosine, sine).astype(BF16)
    key_low = rotate(key_raw * key_inv * head_gain[1], cosine, sine).astype(BF16)
    value_low = (value_raw * value_inv).astype(BF16)
    moving = jnp.stack([key_low, value_low])
    window = jnp.concatenate([shift(moving, hop) for hop in range(hops, 0, -1)] + [moving], axis=1)
    grouped = query_low.reshape(rows, KEY_VALUE_HEADS, groups, HEAD_SIZE)
    scores = jnp.einsum("qkgd,tkd->kgqt", grouped, window[0], preferred_element_type=F32)
    allowed = (
        (key_places[None, :] <= places[:, None])
        & (places[:, None] - key_places[None, :] < WINDOW)
        & (key_places[None, :] >= 0)
    )
    scores = jnp.where(allowed, scores, MASKED)
    weights = jnp.exp(scores - jnp.max(scores, axis=-1, keepdims=True))
    probs = weights / jnp.sum(weights, axis=-1, keepdims=True)
    probs_low = probs.astype(BF16)
    mixed = (
        jnp.einsum("kgqt,tkd->qkgd", probs_low, window[1], preferred_element_type=F32)
        .reshape(rows, head_width)
        .astype(BF16)
    )
    attention_raw = dot(mixed, output_all)
    attention_inv = inverse_rms(attention_raw)
    right_raw = dot(left_low, right_all, 1, 1)
    right_inv = inverse_rms(right_raw)
    merged = (
        hidden
        + attention_raw * attention_inv * gains[1]
        + normed
        + right_raw * right_inv * gains[2]
    ) * HALF_ROOT
    merged_inv = inverse_rms(merged)
    expand_low = (merged * merged_inv * gains[3]).astype(BF16)

    expand_all = team_gather(depth_order(expand_low))
    gate_raw = dot(expand_all, gate_cols)
    up_raw = dot(expand_all, up_cols)
    act_low = (gelu(gate_raw) * up_raw).astype(BF16)
    reduced_raw = team_scatter(dot(act_low, down_rows).astype(BF16))
    reduced_inv = inverse_rms(reduced_raw)
    after_feed = merged + reduced_raw * reduced_inv * gains[4]
    after_low = after_feed.astype(BF16)
    side_raw = dot(after_low, side_gate_all)
    side_low = (gelu(side_raw) * side_input).astype(BF16)
    side_out = dot(side_low, projection_all, 1, 1)
    side_inv = inverse_rms(side_out)
    block_out = (after_feed + side_out * side_inv * gains[5]) * live

    upstream = cotangent.astype(F32) * live
    grad_side, gain_five = rms_back(side_out, side_inv, gains[5], upstream)
    grad_side_low = grad_side.astype(BF16)
    grad_side_raw = (
        dot(grad_side_low, projection_all) * side_input * gelu_slope(side_raw)
    ).astype(BF16)
    grad_after = upstream + dot(grad_side_raw, side_gate_all, 1, 1)
    grad_reduced, gain_four = rms_back(reduced_raw, reduced_inv, gains[4], grad_after)
    grad_reduced_low = grad_reduced.astype(BF16)

    grad_reduced_all = team_gather(grad_reduced_low)
    grad_product = dot(grad_reduced_all, down_rows, 1, 1)
    grad_gate_low = (grad_product * up_raw * gelu_slope(gate_raw)).astype(BF16)
    grad_up_low = (grad_product * gelu(gate_raw)).astype(BF16)
    grad_down = copies_scatter(dot(act_low, grad_reduced_all, 0, 0).astype(BF16))
    part_low = (dot(grad_gate_low, gate_cols, 1, 1) + dot(grad_up_low, up_cols, 1, 1)).astype(BF16)
    mine_gate = copies_scatter(dot(expand_all, grad_gate_low, 0, 0).astype(BF16)).astype(BF16)
    mine_up = copies_scatter(dot(expand_all, grad_up_low, 0, 0).astype(BF16)).astype(BF16)
    part = from_depth_order(team_scatter(part_low))
    grad_merged, gain_three = rms_back(merged, merged_inv, gains[3], part)
    grad_sum = (grad_after + grad_merged) * HALF_ROOT
    grad_right, gain_two = rms_back(right_raw, right_inv, gains[2], grad_sum)
    grad_right_low = grad_right.astype(BF16)
    grad_left_low = dot(grad_right_low, right_all).astype(BF16)
    grad_attention, gain_one = rms_back(attention_raw, attention_inv, gains[1], grad_sum)
    grad_attention_low = grad_attention.astype(BF16)
    grad_mixed = (
        dot(grad_attention_low, output_all, 1, 1)
        .astype(BF16)
        .reshape(rows, KEY_VALUE_HEADS, groups, HEAD_SIZE)
    )
    grad_probs = jnp.einsum("qkgd,tkd->kgqt", grad_mixed, window[1], preferred_element_type=F32)
    inner = jnp.sum(probs * grad_probs, axis=-1, keepdims=True)
    grad_scores = (probs * (grad_probs - inner)).astype(BF16)
    grad_query_rot = jnp.einsum(
        "kgqt,tkd->qkgd", grad_scores, window[0], preferred_element_type=F32
    ).reshape(rows, QUERY_HEADS, HEAD_SIZE)
    grad_window = jnp.stack(
        [
            jnp.einsum("kgqt,qkgd->tkd", grad_scores, grouped, preferred_element_type=F32),
            jnp.einsum("kgqt,qkgd->tkd", probs_low, grad_mixed, preferred_element_type=F32),
        ]
    )
    carried = grad_window[:, hops * rows :]
    for hop in range(1, hops + 1):
        begin = (hops - hop) * rows
        carried = carried + shift(
            grad_window[:, begin : begin + rows].astype(BF16), -hop
        ).astype(F32)
    grad_query, head_zero = rms_back(
        query_raw, query_inv, head_gain[0], rotate(grad_query_rot, cosine, -sine)
    )
    grad_key, head_one = rms_back(
        key_raw, key_inv, head_gain[1], rotate(carried[0], cosine, -sine)
    )
    grad_value, _ = rms_back(value_raw, value_inv, 1.0, carried[1])
    grad_raw = jnp.concatenate(
        [
            grad_query.reshape(rows, head_width).astype(BF16),
            grad_key.reshape(rows, kv_width).astype(BF16),
            grad_value.reshape(rows, kv_width).astype(BF16),
        ],
        axis=1,
    )
    grad_normed = grad_sum + dot(grad_raw, first, 1, 1) + dot(grad_left_low, left_all, 1, 1)
    grad_input, gain_zero = rms_back(hidden, hidden_inv, gains[0], grad_normed)
    grad_hidden = grad_sum + grad_input

    gain_grads = jnp.stack(
        [
            jnp.sum(g, axis=0)
            for g in (gain_zero, gain_one, gain_two, gain_three, gain_four, gain_five)
        ]
    )
    head_grads = jnp.stack([jnp.sum(head_zero, axis=(0, 1)), jnp.sum(head_one, axis=(0, 1))])

    head_column = jnp.pad(
        head_grads.T.reshape(-1, head_part, 2), ((0, 0), (0, depth - head_part), (0, 0))
    ).reshape(-1, 2)
    small = jnp.concatenate(
        [
            dot(normed_low, grad_left_low, 0, 0),
            dot(grad_right_low, left_low, 0, 0),
            gain_grads.T,
            head_column,
            jnp.zeros((width, full_width - edges[-1]), F32),
        ],
        axis=1,
    )
    summed = full_scatter(
        jnp.concatenate(
            [
                dot(normed_low, grad_raw, 0, 0).astype(BF16),
                dot(mixed, grad_attention_low, 0, 0).astype(BF16),
                dot(after_low, grad_side_raw, 0, 0).astype(BF16),
                dot(grad_side_low, side_low, 0, 0).astype(BF16),
                small.astype(BF16),
            ],
            axis=1,
        )
    )
    (
        d_query,
        d_key,
        d_value,
        d_output,
        d_side_gate,
        d_projection,
        d_left,
        d_right,
        d_gains,
        d_heads,
    ) = (summed[:, edges[i] : edges[i + 1]] for i in range(10))
    d_right, d_projection, d_gains = d_right.T, d_projection.T, d_gains.T
    d_heads = d_heads[:head_part].T
    back = team_swap(
        jnp.concatenate(
            [mine_gate.reshape(8, depth, -1), mine_up.reshape(8, depth, -1)], axis=1
        )
    )
    grad_gate = from_column_blocks(back[:, :depth]).astype(F32)
    grad_up = from_column_blocks(back[:, depth:]).astype(F32)
    return (
        block_out,
        grad_hidden,
        d_query,
        d_key,
        d_value,
        d_output,
        d_left,
        d_right,
        d_side_gate,
        d_projection,
        grad_gate,
        grad_up,
        grad_down,
        d_gains,
        d_heads,
    )


def solution(mesh):
    dp, seq = mesh.shape["dp"], mesh.shape["seq"]
    grid = Mesh(mesh.devices.reshape(dp // 4, 4, seq // 2, 2), AXES)
    row, column = P(AXES, None), P(None, AXES)
    return jax.shard_map(
        layer,
        mesh=grid,
        in_specs=(row, row, P(("y", "xc")))
        + (row,) * 6
        + (column, row, column)
        + (row,) * 3
        + (column,) * 2,
        out_specs=(row,) * 7 + (column, row, column) + (row,) * 3 + (column,) * 2,
        check_vma=False,
    )
```

```python
from functools import partial

import jax
import jax.numpy as jnp
from jax import lax
from jax.experimental import pallas as pl
from jax.experimental.pallas import tpu as pltpu
from jax.sharding import Mesh, PartitionSpec as P

QUERY_HEADS = 8
KEY_VALUE_HEADS = 2
HEAD_SIZE = 256
WINDOW = 512
EPSILON = 1e-06
ROPE_BASE = 10000.0
HALF_ROOT = 0.7071067811865476
MASKED = -1e30
GELU_SCALE = 0.7978845608028654
GELU_CUBE = 0.044715
F32 = jnp.float32
BF16 = jnp.bfloat16


def dot(left, right, left_dim=1, right_dim=0):
    return lax.dot_general(
        left, right, (((left_dim,), (right_dim,)), ((), ())), preferred_element_type=F32
    )


def inverse_rms(value):
    return lax.rsqrt(jnp.mean(value * value, axis=-1, keepdims=True) + EPSILON)


def rms_back(value, inverse, gain, grad):
    scaled = grad * gain
    inner = jnp.mean(scaled * value, axis=-1, keepdims=True)
    unit = value * inverse
    return inverse * (scaled - unit * (inverse * inner)), grad * unit


def rope_tables(positions):
    half = HEAD_SIZE // 2
    rate = ROPE_BASE ** (-jnp.arange(half, dtype=F32) * 2.0 / HEAD_SIZE)
    angle = positions.astype(F32)[:, None] * rate[None, :]
    return jnp.cos(angle)[:, None, :], jnp.sin(angle)[:, None, :]


def rotate(value, cosine, sine):
    half = value.shape[-1] // 2
    first, second = value[..., :half], value[..., half:]
    return jnp.concatenate(
        [first * cosine - second * sine, second * cosine + first * sine], axis=-1
    )


def gelu_tanh(value):
    return jnp.tanh(GELU_SCALE * (value + GELU_CUBE * value * value * value))


def gelu(value):
    return 0.5 * value * (1.0 + gelu_tanh(value))


def gelu_slope(value):
    t = gelu_tanh(value)
    inner = GELU_SCALE * (1.0 + 3.0 * GELU_CUBE * value * value)
    return 0.5 * (1.0 + t) + 0.5 * value * (1.0 - t * t) * inner


AXES = ("y", "xc", "h", "l")
TEAM = ("xc", "l")
COPIES = ("y", "h")


class Sender:
    def __init__(self, send, recv):
        self.send, self.recv, self.count, self.started = send, recv, 0, []

    def go(self, source, target, peer):
        i = self.count
        self.count += 1
        copy = pltpu.make_async_remote_copy(
            src_ref=source,
            dst_ref=target,
            send_sem=self.send.at[i],
            recv_sem=self.recv.at[i],
            device_id=peer,
            device_id_type=pl.DeviceIdType.MESH,
        )
        copy.start()
        self.started.append(copy)
        return copy

    def finish(self):
        for copy in self.started:
            copy.wait_send()


def greet(peers):
    barrier = pltpu.get_barrier_semaphore()
    for peer in peers:
        pl.semaphore_signal(barrier, inc=1, device_id=peer, device_id_type=pl.DeviceIdType.MESH)
    pl.semaphore_wait(barrier, len(peers))


def plus(*parts):
    total = parts[0].astype(F32)
    for part in parts[1:]:
        total = total + part.astype(F32)
    return total


def remote_call(kernel, out, copies, identity, scratch=(), vmem=None, spaces=pl.ANY, inputs=1):
    places = [pl.BlockSpec(memory_space=space) for space in spaces] if isinstance(
        spaces, (list, tuple)
    ) else pl.BlockSpec(memory_space=spaces)
    return pl.pallas_call(
        kernel,
        out_shape=out,
        in_specs=[pl.BlockSpec(memory_space=pl.ANY)] * inputs,
        out_specs=places,
        scratch_shapes=[
            pltpu.SemaphoreType.DMA((copies,)),
            pltpu.SemaphoreType.DMA((copies,)),
            *scratch,
        ],
        compiler_params=pltpu.CompilerParams(
            collective_id=identity, has_side_effects=True, vmem_limit_bytes=vmem
        ),
    )


def team_places():
    xc, l = lax.axis_index("xc"), lax.axis_index("l")
    core = lax.rem(xc, 2)
    other = xc + 1 - 2 * core
    cross, side = lax.rem(xc + 2, 4), 1 - l
    own = {"O": xc * 2 + l, "X": cross * 2 + l, "L": xc * 2 + side, "D": cross * 2 + side}
    far = lax.rem(other + 2, 4)
    twin = {"O": other * 2 + l, "X": far * 2 + l, "L": other * 2 + side, "D": far * 2 + side}
    return own, twin, {"xc": other}, {"xc": cross}, {"l": side}


def team_gather_kernel(x_ref, o_ref, send, recv, local):
    own, _, core, cross, side = team_places()
    half = x_ref.shape[0] // 2
    top, low = pl.ds(0, half), pl.ds(half, half)
    keep = pltpu.make_async_copy(x_ref, o_ref.at[own["O"]], local)
    keep.start()
    greet([core, cross, side])
    out = Sender(send, recv)
    mine, from_side, from_cross = o_ref.at[own["O"]], o_ref.at[own["L"]], o_ref.at[own["X"]]
    diagonal = o_ref.at[own["D"]]
    side_top = out.go(x_ref.at[top], mine.at[top], side)
    cross_low = out.go(x_ref.at[low], mine.at[low], cross)
    side_low = out.go(x_ref.at[low], mine.at[low], side)
    cross_top = out.go(x_ref.at[top], mine.at[top], cross)
    twins = [out.go(x_ref, mine, core)]
    side_top.wait_recv()
    diagonal_top = out.go(from_side.at[top], from_side.at[top], cross)
    twins.append(out.go(from_side.at[top], from_side.at[top], core))
    cross_low.wait_recv()
    diagonal_low = out.go(from_cross.at[low], from_cross.at[low], side)
    twins.append(out.go(from_cross.at[low], from_cross.at[low], core))
    side_low.wait_recv()
    twins.append(out.go(from_side.at[low], from_side.at[low], core))
    cross_top.wait_recv()
    twins.append(out.go(from_cross.at[top], from_cross.at[top], core))
    diagonal_top.wait_recv()
    twins.append(out.go(diagonal.at[top], diagonal.at[top], core))
    diagonal_low.wait_recv()
    twins.append(out.go(diagonal.at[low], diagonal.at[low], core))
    for copy in twins:
        copy.wait_recv()
    out.finish()
    keep.wait()


def team_gather(block):
    rows, width = block.shape
    gathered = remote_call(
        team_gather_kernel,
        jax.ShapeDtypeStruct((8, rows, width), block.dtype),
        13,
        0,
        [pltpu.SemaphoreType.DMA],
    )(block)
    return gathered.reshape(8 * rows, width)


def team_scatter_kernel(p_ref, o_ref, send, recv, local, mine, twin_in, cross_in, side_in, bent_in):
    own, twin, core, cross, side = team_places()
    half = p_ref.shape[1] // 2
    top, low = pl.ds(0, half), pl.ds(half, half)
    loads = []
    for i, k in enumerate("DXLO"):
        loads.append(pltpu.make_async_copy(p_ref.at[own[k]], mine.at[i], local.at[i]))
        loads[-1].start()
    greet([core, cross, side])
    out = Sender(send, recv)
    swaps = [out.go(p_ref.at[twin[k]], twin_in.at[i], core) for i, k in enumerate("DXLO")]

    def join(i):
        loads[i].wait()
        swaps[i].wait_recv()
        mine[i] = plus(mine[i], twin_in[i]).astype(BF16)

    join(0)
    bent_cross = out.go(mine.at[0].at[top], bent_in.at[0], cross)
    bent_side = out.go(mine.at[0].at[low], bent_in.at[1], side)
    join(1)
    cross_top = out.go(mine.at[1].at[top], cross_in.at[top], cross)
    join(2)
    side_low = out.go(mine.at[2].at[low], side_in.at[low], side)
    bent_cross.wait_recv()
    mine[2, top] = plus(mine[2, top], bent_in[0]).astype(BF16)
    side_top = out.go(mine.at[2].at[top], side_in.at[top], side)
    bent_side.wait_recv()
    mine[1, low] = plus(mine[1, low], bent_in[1]).astype(BF16)
    cross_low = out.go(mine.at[1].at[low], cross_in.at[low], cross)
    loads[3].wait()
    swaps[3].wait_recv()
    o_ref[...] = plus(mine[3], twin_in[3])
    cross_top.wait_recv()
    side_low.wait_recv()
    o_ref[top] += cross_in[top].astype(F32)
    o_ref[low] += side_in[low].astype(F32)
    side_top.wait_recv()
    cross_low.wait_recv()
    o_ref[top] += side_in[top].astype(F32)
    o_ref[low] += cross_in[low].astype(F32)
    out.finish()


def team_scatter(partial_sum):
    rows, width = partial_sum.shape[0] // 8, partial_sum.shape[1]
    return remote_call(
        team_scatter_kernel,
        jax.ShapeDtypeStruct((rows, width), F32),
        10,
        1,
        [
            pltpu.SemaphoreType.DMA((4,)),
            pltpu.VMEM((4, rows, width), BF16),
            pltpu.VMEM((4, rows, width), BF16),
            pltpu.VMEM((rows, width), BF16),
            pltpu.VMEM((rows, width), BF16),
            pltpu.VMEM((2, rows // 2, width), BF16),
        ],
        40 * 2**20,
        pltpu.VMEM,
    )(partial_sum.reshape(8, rows, width))


def team_peers():
    xc, l = lax.axis_index("xc"), lax.axis_index("l")
    peers = []
    for i in range(1, 8):
        far, side = lax.rem(xc + i // 2, 4), lax.rem(l + i % 2, 2)
        peers.append((far * 2 + side, {"xc": far, "l": side}))
    return xc * 2 + l, peers


def full_places():
    y, xc = lax.axis_index("y"), lax.axis_index("xc")
    h, l = lax.axis_index("h"), lax.axis_index("l")
    core = lax.rem(xc, 2)

    def rank(plane, depth, twin=False):
        b = xc + 1 - 2 * core if twin else xc
        b = lax.rem(b + 2, 4) if plane in "XD" else b
        a = 1 - y if plane in "YD" else y
        u = 1 - h if depth in ("H", "HL") else h
        v = 1 - l if depth in ("L", "HL") else l
        return ((a * 4 + b) * 2 + u) * 2 + v

    peers = {
        "C": {"xc": xc + 1 - 2 * core},
        "X": {"xc": lax.rem(xc + 2, 4)},
        "Y": {"y": 1 - y},
        "H": {"h": 1 - h},
        "L": {"l": 1 - l},
    }
    return rank, peers


DEPTHS = ("O", "L", "H", "HL")


def copy_places():
    y, h = lax.axis_index("y"), lax.axis_index("h")
    return {
        "O": y * 2 + h,
        "Y": (1 - y) * 2 + h,
        "H": y * 2 + 1 - h,
        "D": (1 - y) * 2 + 1 - h,
    }


def weights_in_kernel(
    x_ref, gate_ref, up_ref, down_ref, o_ref, gates_ref, ups_ref, downs_ref, send, recv, local
):
    rank, peers = full_places()
    me, team = team_peers()
    spot = copy_places()

    def at(plane, depth):
        return o_ref.at[rank(plane, depth)]

    keeps = [
        pltpu.make_async_copy(x_ref, at("O", "O"), local.at[0]),
        pltpu.make_async_copy(down_ref, downs_ref.at[spot["O"]], local.at[1]),
        pltpu.make_async_copy(gate_ref.at[me], gates_ref.at[spot["O"], me], local.at[2]),
        pltpu.make_async_copy(up_ref.at[me], ups_ref.at[spot["O"], me], local.at[3]),
    ]
    for keep in keeps:
        keep.start()
    greet([peer for _, peer in team] + [peers["Y"], peers["H"]])
    out = Sender(send, recv)
    swaps, twins = [], []
    to_h = out.go(x_ref, at("O", "O"), peers["H"])
    to_l = out.go(x_ref, at("O", "O"), peers["L"])
    for place, peer in team:
        swaps.append(out.go(gate_ref.at[place], gates_ref.at[spot["O"], me], peer))
        swaps.append(out.go(up_ref.at[place], ups_ref.at[spot["O"], me], peer))
    direct, bent = {}, {}

    def begin(depth):
        source = x_ref if depth == "O" else at("O", depth)
        target = at("O", depth)
        to_y = out.go(source, target, peers["Y"])
        to_x = out.go(source, target, peers["X"])
        twins.append(out.go(source, target, peers["C"]))
        direct[depth] = (to_y, to_x)

    def bend(depth):
        to_y, to_x = direct[depth]
        to_y.wait_recv()
        bent[depth] = out.go(at("Y", depth), at("Y", depth), peers["X"])
        twins.append(out.go(at("Y", depth), at("Y", depth), peers["C"]))
        to_x.wait_recv()
        twins.append(out.go(at("X", depth), at("X", depth), peers["C"]))

    def close(depth):
        bent[depth].wait_recv()
        twins.append(out.go(at("D", depth), at("D", depth), peers["C"]))

    blocks = {"gate": gates_ref, "up": ups_ref, "down": downs_ref}
    flats, arrivals = {}, []

    def spread(name):
        block = blocks[name]
        source = down_ref if name == "down" else block.at[spot["O"]]
        flats[name] = out.go(source, block.at[spot["O"]], peers["H"])
        arrivals.append(out.go(source, block.at[spot["O"]], peers["Y"]))

    def corner(name):
        flats[name].wait_recv()
        piece = blocks[name].at[spot["H"]]
        arrivals.append(out.go(piece, piece, peers["Y"]))

    spread("down")
    begin("O")
    for swap in swaps:
        swap.wait_recv()
    keeps[2].wait()
    keeps[3].wait()
    spread("gate")
    to_h.wait_recv()
    to_hl = out.go(at("O", "H"), at("O", "H"), peers["L"])
    to_l.wait_recv()
    begin("L")
    begin("H")
    corner("down")
    bend("O")
    spread("up")
    to_hl.wait_recv()
    begin("HL")
    bend("L")
    corner("gate")
    bend("H")
    close("O")
    close("L")
    bend("HL")
    corner("up")
    close("H")
    close("HL")
    for copy in twins + arrivals:
        copy.wait_recv()
    out.finish()
    keeps[0].wait()
    keeps[1].wait()


def weights_in(columns, gate_blocks, up_blocks, down):
    rows, width = columns.shape
    ranks, depth, part = gate_blocks.shape
    if lax.axis_size("y") != 2 or lax.axis_size("h") != 2:
        full = lax.all_gather(columns, AXES, axis=0, tiled=False)
        gates, ups = (
            lax.all_gather(lax.all_to_all(b, TEAM, 0, 0), COPIES, axis=0, tiled=False)
            for b in (gate_blocks, up_blocks)
        )
        downs = lax.all_gather(down, COPIES, axis=0, tiled=False)
    else:
        full, gates, ups, downs = remote_call(
            weights_in_kernel,
            (
                jax.ShapeDtypeStruct((32, rows, width), BF16),
                jax.ShapeDtypeStruct((4, ranks, depth, part), BF16),
                jax.ShapeDtypeStruct((4, ranks, depth, part), BF16),
                jax.ShapeDtypeStruct((4, *down.shape), BF16),
            ),
            14 + 3 + 28 + 9,
            3,
            [pltpu.SemaphoreType.DMA((4,))],
            spaces=[pl.ANY] * 4,
            inputs=4,
        )(columns, gate_blocks, up_blocks, down)
    return (
        full.reshape(-1, width),
        gates.reshape(-1, part),
        ups.reshape(-1, part),
        downs.reshape(-1, down.shape[1]),
    )


PLANES = ("D", "X", "Y", "O")
SUMS = ("HL", "L", "H", "O")


def grads_out_kernel(edges, *refs):
    n = len(edges)
    parts, sums = refs[:n], refs[n : n + 3]
    o_ref, gate_ref, up_ref, down_ref, send, recv, local = refs[n + 3 : n + 10]
    mine, twin_in, cross_in, lane_in, bent_in, depth_in = refs[n + 10 : n + 16]
    flat, flat_y, flat_h = refs[n + 16 : n + 19], refs[n + 19 : n + 22], refs[n + 22 : n + 25]
    rank, peers = full_places()
    me, team = team_peers()
    spot = copy_places()
    loads, swaps, flights = {}, {}, {}
    count = 0

    def load(source, target):
        nonlocal count
        copy = pltpu.make_async_copy(source, target, local.at[count])
        count += 1
        copy.start()
        return copy

    for t, depth in enumerate(SUMS):
        for k, plane in enumerate(PLANES):
            place = rank(plane, depth)
            loads[t, k] = [
                load(part.at[place], mine.at[t, k, :, pl.ds(begin, part.shape[2])])
                for part, begin in zip(parts, edges)
            ]
    own_loads = [
        [load(total.at[spot[k]], buffer.at[j]) for j, k in enumerate("HO")]
        for total, buffer in zip(sums, flat)
    ]
    greet([peer for _, peer in team] + [peers["Y"], peers["H"]])
    out = Sender(send, recv)

    def swap(t):
        for k, plane in enumerate(PLANES):
            place = rank(plane, SUMS[t], True)
            swaps[t, k] = [
                out.go(
                    part.at[place], twin_in.at[t, k, :, pl.ds(begin, part.shape[2])], peers["C"]
                )
                for part, begin in zip(parts, edges)
            ]

    def join(t, k):
        for copy in loads[t, k]:
            copy.wait()
        for copy in swaps[t, k]:
            copy.wait_recv()
        mine[t, k] = plus(mine[t, k], twin_in[t, k]).astype(BF16)

    def begin(t):
        join(t, 0)
        to_bend = out.go(mine.at[t, 0], bent_in.at[t], peers["X"])
        join(t, 1)
        to_x = out.go(mine.at[t, 1], cross_in.at[t], peers["X"])
        join(t, 2)
        join(t, 3)
        flights[t] = [to_bend, to_x]

    def bend(t):
        to_bend, to_x = flights[t]
        to_bend.wait_recv()
        mine[t, 2] = plus(mine[t, 2], bent_in[t]).astype(BF16)
        flights[t] = [to_x, out.go(mine.at[t, 2], lane_in.at[t], peers["Y"])]

    def close(t):
        for copy in flights[t]:
            copy.wait_recv()
        return plus(mine[t, 3], cross_in[t], lane_in[t])

    y_side, h_side = {}, {}

    def lane(i, j):
        y_side[i, j] = out.go(sums[i].at[spot["DY"[j]]], flat_y[i].at[j], peers["Y"])

    def along(i):
        own_loads[i][0].wait()
        y_side[i, 0].wait_recv()
        flat[i][0] = plus(flat[i][0], flat_y[i][0]).astype(BF16)
        h_side[i] = out.go(flat[i].at[0], flat_h[i], peers["H"])

    swap(0)
    lane(2, 0)
    swap(1)
    swap(2)
    swap(3)
    begin(0)
    begin(1)
    along(2)
    lane(0, 0)
    bend(0)
    begin(2)
    begin(3)
    along(0)
    lane(1, 0)
    bend(1)
    mine[0, 3] = close(0).astype(BF16)
    to_hl = out.go(mine.at[0, 3], depth_in.at[0], peers["L"])
    along(1)
    lane(0, 1)
    lane(1, 1)
    bend(2)
    mine[1, 3] = close(1).astype(BF16)
    to_l = out.go(mine.at[1, 3], depth_in.at[1], peers["L"])
    lane(2, 1)
    bend(3)
    total = close(2)
    to_hl.wait_recv()
    mine[2, 3] = plus(total, depth_in[0]).astype(BF16)
    to_h = out.go(mine.at[2, 3], depth_in.at[2], peers["H"])
    returns = []
    for i, target in enumerate((gate_ref, up_ref)):
        own_loads[i][1].wait()
        y_side[i, 1].wait_recv()
        h_side[i].wait_recv()
        flat[i][1] = plus(flat[i][1], flat_y[i][1], flat_h[i][...]).astype(BF16)
        keep = load(flat[i].at[1, me], target.at[me])
        returns.append(keep)
        for place, peer in team:
            returns.append(out.go(flat[i].at[1, place], target.at[me], peer))
    total = close(3)
    to_l.wait_recv()
    total = plus(total, depth_in[1])
    to_h.wait_recv()
    o_ref[...] = plus(total, depth_in[2])
    own_loads[2][1].wait()
    y_side[2, 1].wait_recv()
    h_side[2].wait_recv()
    down_ref[...] = plus(flat[2][1], flat_y[2][1], flat_h[2][...])
    for i, copy in enumerate(returns):
        if i % 8 == 0:
            copy.wait()
        else:
            copy.wait_recv()
    out.finish()


def grads_out(parts, gate, up, down):
    ys, hs = lax.axis_size("y"), lax.axis_size("h")
    shares = ys * hs * 8
    rows = parts[0].shape[0] // shares
    blocks = [part.reshape(shares, rows, part.shape[1]) for part in parts]
    sums = [
        gate.reshape(ys * hs, 8, -1, gate.shape[1]),
        up.reshape(ys * hs, 8, -1, up.shape[1]),
        down.reshape(ys * hs, -1, down.shape[1]),
    ]
    if ys != 2 or hs != 2:
        block = jnp.concatenate(blocks, axis=2)
        total = lax.psum_scatter(block, AXES, scatter_dimension=0, tiled=False).astype(F32)
        gate, up, down = (
            lax.psum_scatter(value, COPIES, scatter_dimension=0, tiled=False) for value in sums
        )
        gate, up = (lax.all_to_all(value, TEAM, 0, 0) for value in (gate, up))
        return total, gate, up, down.astype(F32)
    edges = [0]
    for part in parts:
        edges.append(edges[-1] + part.shape[1])
    width = edges.pop()
    flats = [pltpu.VMEM((2, *value.shape[1:]), BF16) for value in sums]
    return remote_call(
        partial(grads_out_kernel, tuple(edges)),
        (
            jax.ShapeDtypeStruct((rows, width), F32),
            jax.ShapeDtypeStruct(sums[0].shape[1:], BF16),
            jax.ShapeDtypeStruct(sums[1].shape[1:], BF16),
            jax.ShapeDtypeStruct(sums[2].shape[1:], F32),
        ),
        16 * len(parts) + 12 + 3 + 6 + 3 + 14,
        4,
        [
            pltpu.SemaphoreType.DMA((16 * len(parts) + 6 + 2,)),
            pltpu.VMEM((4, 4, rows, width), BF16),
            pltpu.VMEM((4, 4, rows, width), BF16),
            pltpu.VMEM((4, rows, width), BF16),
            pltpu.VMEM((4, rows, width), BF16),
            pltpu.VMEM((4, rows, width), BF16),
            pltpu.VMEM((3, rows, width), BF16),
            *flats,
            *flats,
            *[pltpu.VMEM(value.shape[1:], BF16) for value in sums],
        ],
        60 * 2**20,
        [pltpu.VMEM, pl.ANY, pl.ANY, pltpu.VMEM],
        len(parts) + 3,
    )(*blocks, *sums)


def shift(block, distance):
    pieces = lax.axis_size("h") * lax.axis_size("l")
    route = [(i, i + distance) for i in range(pieces) if 0 <= i + distance < pieces]
    return lax.ppermute(block, ("h", "l"), route)


def column_blocks(weight):
    ys, hs = lax.axis_size("y"), lax.axis_size("h")
    depth, width = weight.shape
    split = weight.reshape(depth, ys, 4, hs, 2, width // (ys * hs * 8))
    return split.transpose(2, 4, 0, 1, 3, 5).reshape(8, depth, width // 8)


def from_column_blocks(blocks):
    ys, hs = lax.axis_size("y"), lax.axis_size("h")
    depth, width = blocks.shape[1:]
    split = blocks.reshape(4, 2, depth, ys, hs, width // (ys * hs)).transpose(2, 3, 0, 4, 1, 5)
    return split.reshape(depth, 8 * width)


def depth_order(value):
    ys, hs = lax.axis_size("y"), lax.axis_size("h")
    rows, width = value.shape
    split = value.reshape(rows, ys, 4, hs, width // (4 * ys * hs))
    return split.transpose(0, 1, 3, 2, 4).reshape(rows, width)


def from_depth_order(value):
    ys, hs = lax.axis_size("y"), lax.axis_size("h")
    rows, width = value.shape
    split = value.reshape(rows, ys, hs, 4, width // (4 * ys * hs))
    return split.transpose(0, 1, 3, 2, 4).reshape(rows, width)


def layer(*args):
    (
        hidden_in,
        layer_input,
        seq_lengths,
        cotangent,
        query_weight,
        key_matrix,
        value_matrix,
        output_weight,
        laurel_left,
        laurel_right,
        input_gate,
        input_projection,
        gate_weight,
        up_weight,
        down_weight,
        norm_gains,
        head_gains,
    ) = args
    rows, width = hidden_in.shape
    hops = max(1, WINDOW // rows)
    groups = QUERY_HEADS // KEY_VALUE_HEADS
    piece = lax.axis_index(("h", "l"))
    places = piece * rows + jnp.arange(rows, dtype=jnp.int32)
    key_places = (piece - hops) * rows + jnp.arange((hops + 1) * rows, dtype=jnp.int32)
    live = (places < seq_lengths[0]).astype(F32)[:, None]

    head_width = QUERY_HEADS * HEAD_SIZE
    kv_width = KEY_VALUE_HEADS * HEAD_SIZE
    rank = laurel_left.shape[1]
    side = layer_input.shape[1]
    depth, head_part = query_weight.shape[0], head_gains.shape[1]
    columns = (
        query_weight,
        key_matrix,
        value_matrix,
        output_weight,
        input_gate,
        input_projection.T,
        laurel_left,
        laurel_right.T,
        norm_gains.T,
        jnp.pad(head_gains.T, ((0, depth - head_part), (0, 0))),
    )
    edges = [0]
    for column in columns:
        edges.append(edges[-1] + column.shape[1])
    full_width = -(-edges[-1] // 128) * 128
    local_columns = jnp.pad(
        jnp.concatenate(columns, axis=1), ((0, 0), (0, full_width - edges[-1]))
    )
    full, gate_cols, up_cols, down_rows = weights_in(
        local_columns, column_blocks(gate_weight), column_blocks(up_weight), down_weight
    )
    first = full[:, : edges[3]]
    output_all, side_gate_all, projection_all, left_all, right_all = (
        full[:, edges[i] : edges[i + 1]] for i in range(3, 8)
    )
    gains = full[:, edges[8] : edges[9]].T.astype(F32)
    head_gain = (
        full[:, edges[9] : edges[10]].reshape(-1, depth, 2)[:, :head_part].reshape(-1, 2).T
    ).astype(F32)

    hidden = hidden_in.astype(F32)
    side_input = layer_input.astype(F32)
    cosine, sine = rope_tables(places)

    hidden_inv = inverse_rms(hidden)
    normed = hidden * hidden_inv * gains[0]
    normed_low = normed.astype(BF16)
    raw = dot(normed_low, first)
    query_raw = raw[:, :head_width].reshape(rows, QUERY_HEADS, HEAD_SIZE)
    key_raw = raw[:, head_width : head_width + kv_width].reshape(rows, KEY_VALUE_HEADS, HEAD_SIZE)
    value_raw = raw[:, head_width + kv_width :].reshape(
        rows, KEY_VALUE_HEADS, HEAD_SIZE
    )
    left_low = dot(normed_low, left_all).astype(BF16)
    query_inv = inverse_rms(query_raw)
    key_inv = inverse_rms(key_raw)
    value_inv = inverse_rms(value_raw)
    query_low = rotate(query_raw * query_inv * head_gain[0], cosine, sine).astype(BF16)
    key_low = rotate(key_raw * key_inv * head_gain[1], cosine, sine).astype(BF16)
    value_low = (value_raw * value_inv).astype(BF16)
    moving = jnp.stack([key_low, value_low])
    window = jnp.concatenate([shift(moving, hop) for hop in range(hops, 0, -1)] + [moving], axis=1)
    grouped = query_low.reshape(rows, KEY_VALUE_HEADS, groups, HEAD_SIZE)
    scores = jnp.einsum("qkgd,tkd->kgqt", grouped, window[0], preferred_element_type=F32)
    allowed = (
        (key_places[None, :] <= places[:, None])
        & (places[:, None] - key_places[None, :] < WINDOW)
        & (key_places[None, :] >= 0)
    )
    scores = jnp.where(allowed, scores, MASKED)
    weights = jnp.exp(scores - jnp.max(scores, axis=-1, keepdims=True))
    probs = weights / jnp.sum(weights, axis=-1, keepdims=True)
    probs_low = probs.astype(BF16)
    mixed = (
        jnp.einsum("kgqt,tkd->qkgd", probs_low, window[1], preferred_element_type=F32)
        .reshape(rows, head_width)
        .astype(BF16)
    )
    attention_raw = dot(mixed, output_all)
    attention_inv = inverse_rms(attention_raw)
    right_raw = dot(left_low, right_all, 1, 1)
    right_inv = inverse_rms(right_raw)
    merged = (
        hidden
        + attention_raw * attention_inv * gains[1]
        + normed
        + right_raw * right_inv * gains[2]
    ) * HALF_ROOT
    merged_inv = inverse_rms(merged)
    expand_low = (merged * merged_inv * gains[3]).astype(BF16)

    expand_all = team_gather(depth_order(expand_low))
    gate_raw = dot(expand_all, gate_cols)
    up_raw = dot(expand_all, up_cols)
    act_low = (gelu(gate_raw) * up_raw).astype(BF16)
    reduced_raw = team_scatter(dot(act_low, down_rows).astype(BF16))
    reduced_inv = inverse_rms(reduced_raw)
    after_feed = merged + reduced_raw * reduced_inv * gains[4]
    after_low = after_feed.astype(BF16)
    side_raw = dot(after_low, side_gate_all)
    side_low = (gelu(side_raw) * side_input).astype(BF16)
    side_out = dot(side_low, projection_all, 1, 1)
    side_inv = inverse_rms(side_out)
    block_out = (after_feed + side_out * side_inv * gains[5]) * live

    upstream = cotangent.astype(F32) * live
    grad_side, gain_five = rms_back(side_out, side_inv, gains[5], upstream)
    grad_side_low = grad_side.astype(BF16)
    grad_side_raw = (
        dot(grad_side_low, projection_all) * side_input * gelu_slope(side_raw)
    ).astype(BF16)
    grad_after = upstream + dot(grad_side_raw, side_gate_all, 1, 1)
    grad_reduced, gain_four = rms_back(reduced_raw, reduced_inv, gains[4], grad_after)
    grad_reduced_low = grad_reduced.astype(BF16)

    grad_reduced_all = team_gather(grad_reduced_low)
    grad_product = dot(grad_reduced_all, down_rows, 1, 1)
    grad_gate_low = (grad_product * up_raw * gelu_slope(gate_raw)).astype(BF16)
    grad_up_low = (grad_product * gelu(gate_raw)).astype(BF16)
    part_down = dot(act_low, grad_reduced_all, 0, 0).astype(BF16)
    part_low = (dot(grad_gate_low, gate_cols, 1, 1) + dot(grad_up_low, up_cols, 1, 1)).astype(BF16)
    part_gate = dot(expand_all, grad_gate_low, 0, 0).astype(BF16)
    part_up = dot(expand_all, grad_up_low, 0, 0).astype(BF16)
    part = from_depth_order(team_scatter(part_low))
    grad_merged, gain_three = rms_back(merged, merged_inv, gains[3], part)
    grad_sum = (grad_after + grad_merged) * HALF_ROOT
    grad_right, gain_two = rms_back(right_raw, right_inv, gains[2], grad_sum)
    grad_right_low = grad_right.astype(BF16)
    grad_left_low = dot(grad_right_low, right_all).astype(BF16)
    grad_attention, gain_one = rms_back(attention_raw, attention_inv, gains[1], grad_sum)
    grad_attention_low = grad_attention.astype(BF16)
    grad_mixed = (
        dot(grad_attention_low, output_all, 1, 1)
        .astype(BF16)
        .reshape(rows, KEY_VALUE_HEADS, groups, HEAD_SIZE)
    )
    grad_probs = jnp.einsum("qkgd,tkd->kgqt", grad_mixed, window[1], preferred_element_type=F32)
    inner = jnp.sum(probs * grad_probs, axis=-1, keepdims=True)
    grad_scores = (probs * (grad_probs - inner)).astype(BF16)
    grad_query_rot = jnp.einsum(
        "kgqt,tkd->qkgd", grad_scores, window[0], preferred_element_type=F32
    ).reshape(rows, QUERY_HEADS, HEAD_SIZE)
    grad_window = jnp.stack(
        [
            jnp.einsum("kgqt,qkgd->tkd", grad_scores, grouped, preferred_element_type=F32),
            jnp.einsum("kgqt,qkgd->tkd", probs_low, grad_mixed, preferred_element_type=F32),
        ]
    )
    carried = grad_window[:, hops * rows :]
    for hop in range(1, hops + 1):
        begin = (hops - hop) * rows
        carried = carried + shift(
            grad_window[:, begin : begin + rows].astype(BF16), -hop
        ).astype(F32)
    grad_query, head_zero = rms_back(
        query_raw, query_inv, head_gain[0], rotate(grad_query_rot, cosine, -sine)
    )
    grad_key, head_one = rms_back(
        key_raw, key_inv, head_gain[1], rotate(carried[0], cosine, -sine)
    )
    grad_value, _ = rms_back(value_raw, value_inv, 1.0, carried[1])
    grad_raw = jnp.concatenate(
        [
            grad_query.reshape(rows, head_width).astype(BF16),
            grad_key.reshape(rows, kv_width).astype(BF16),
            grad_value.reshape(rows, kv_width).astype(BF16),
        ],
        axis=1,
    )
    grad_normed = grad_sum + dot(grad_raw, first, 1, 1) + dot(grad_left_low, left_all, 1, 1)
    grad_input, gain_zero = rms_back(hidden, hidden_inv, gains[0], grad_normed)
    grad_hidden = grad_sum + grad_input

    gain_grads = jnp.stack(
        [
            jnp.sum(g, axis=0)
            for g in (gain_zero, gain_one, gain_two, gain_three, gain_four, gain_five)
        ]
    )
    head_grads = jnp.stack([jnp.sum(head_zero, axis=(0, 1)), jnp.sum(head_one, axis=(0, 1))])

    head_column = jnp.pad(
        head_grads.T.reshape(-1, head_part, 2), ((0, 0), (0, depth - head_part), (0, 0))
    ).reshape(-1, 2)
    tail = full_width - edges[6]
    small = (
        dot(normed_low, jnp.pad(grad_left_low, ((0, 0), (0, tail - rank))), 0, 0)
        + dot(grad_right_low, jnp.pad(left_low, ((0, 0), (rank, tail - 2 * rank))), 0, 0)
        + jnp.pad(gain_grads.T, ((0, 0), (2 * rank, tail - 2 * rank - 6)))
        + jnp.pad(head_column, ((0, 0), (2 * rank + 6, tail - 2 * rank - 8)))
    )
    weight_grads = (
        dot(normed_low, grad_raw, 0, 0).astype(BF16),
        dot(mixed, grad_attention_low, 0, 0).astype(BF16),
        dot(after_low, grad_side_raw, 0, 0).astype(BF16),
        dot(grad_side_low, side_low, 0, 0).astype(BF16),
        small.astype(BF16),
    )
    summed, back_gate, back_up, grad_down = grads_out(weight_grads, part_gate, part_up, part_down)
    grad_gate = from_column_blocks(back_gate).astype(F32)
    grad_up = from_column_blocks(back_up).astype(F32)
    (
        d_query,
        d_key,
        d_value,
        d_output,
        d_side_gate,
        d_projection,
        d_left,
        d_right,
        d_gains,
        d_heads,
    ) = (summed[:, edges[i] : edges[i + 1]] for i in range(10))
    d_right, d_projection, d_gains = d_right.T, d_projection.T, d_gains.T
    d_heads = d_heads[:head_part].T
    return (
        block_out,
        grad_hidden,
        d_query,
        d_key,
        d_value,
        d_output,
        d_left,
        d_right,
        d_side_gate,
        d_projection,
        grad_gate,
        grad_up,
        grad_down,
        d_gains,
        d_heads,
    )


def solution(mesh):
    dp, seq = mesh.shape["dp"], mesh.shape["seq"]
    grid = Mesh(mesh.devices.reshape(dp // 4, 4, seq // 2, 2), AXES)
    row, column = P(AXES, None), P(None, AXES)
    return jax.shard_map(
        layer,
        mesh=grid,
        in_specs=(row, row, P(("y", "xc")))
        + (row,) * 6
        + (column, row, column)
        + (row,) * 3
        + (column,) * 2,
        out_specs=(row,) * 7 + (column, row, column) + (row,) * 3 + (column,) * 2,
        check_vma=False,
    )
```

```python
from functools import partial

import jax
import jax.numpy as jnp
from jax import lax
from jax.experimental import pallas as pl
from jax.experimental.pallas import tpu as pltpu
from jax.sharding import Mesh, PartitionSpec as P

QUERY_HEADS = 8
KEY_VALUE_HEADS = 2
HEAD_SIZE = 256
WINDOW = 512
EPSILON = 1e-06
ROPE_BASE = 10000.0
HALF_ROOT = 0.7071067811865476
MASKED = -1e30
GELU_SCALE = 0.7978845608028654
GELU_CUBE = 0.044715
F32 = jnp.float32
BF16 = jnp.bfloat16


def dot(left, right, left_dim=1, right_dim=0):
    return lax.dot_general(
        left, right, (((left_dim,), (right_dim,)), ((), ())), preferred_element_type=F32
    )


def inverse_rms(value):
    return lax.rsqrt(jnp.mean(value * value, axis=-1, keepdims=True) + EPSILON)


def rms_back(value, inverse, gain, grad):
    scaled = grad * gain
    inner = jnp.mean(scaled * value, axis=-1, keepdims=True)
    unit = value * inverse
    return inverse * (scaled - unit * (inverse * inner)), grad * unit


def rope_tables(positions):
    half = HEAD_SIZE // 2
    rate = ROPE_BASE ** (-jnp.arange(half, dtype=F32) * 2.0 / HEAD_SIZE)
    angle = positions.astype(F32)[:, None] * rate[None, :]
    return jnp.cos(angle)[:, None, :], jnp.sin(angle)[:, None, :]


def rotate(value, cosine, sine):
    half = value.shape[-1] // 2
    first, second = value[..., :half], value[..., half:]
    return jnp.concatenate(
        [first * cosine - second * sine, second * cosine + first * sine], axis=-1
    )


def gelu_tanh(value):
    return jnp.tanh(GELU_SCALE * (value + GELU_CUBE * value * value * value))


def gelu(value):
    return 0.5 * value * (1.0 + gelu_tanh(value))


def gelu_slope(value):
    t = gelu_tanh(value)
    inner = GELU_SCALE * (1.0 + 3.0 * GELU_CUBE * value * value)
    return 0.5 * (1.0 + t) + 0.5 * value * (1.0 - t * t) * inner


AXES = ("y", "xc", "h", "l")
TEAM = ("xc", "l")
COPIES = ("y", "h")


class Sender:
    def __init__(self, send, recv):
        self.send, self.recv, self.count, self.started = send, recv, 0, []

    def go(self, source, target, peer):
        i = self.count
        self.count += 1
        copy = pltpu.make_async_remote_copy(
            src_ref=source,
            dst_ref=target,
            send_sem=self.send.at[i],
            recv_sem=self.recv.at[i],
            device_id=peer,
            device_id_type=pl.DeviceIdType.MESH,
        )
        copy.start()
        self.started.append(copy)
        return copy

    def finish(self):
        for copy in self.started:
            copy.wait_send()


def greet(peers):
    barrier = pltpu.get_barrier_semaphore()
    for peer in peers:
        pl.semaphore_signal(barrier, inc=1, device_id=peer, device_id_type=pl.DeviceIdType.MESH)
    pl.semaphore_wait(barrier, len(peers))


def plus(*parts):
    total = parts[0].astype(F32)
    for part in parts[1:]:
        total = total + part.astype(F32)
    return total


def strips(ref):
    if len(ref.shape) == 3:
        return [ref.at[i] for i in range(ref.shape[0])]
    step = min(16, ref.shape[0])
    return [ref.at[pl.ds(i, step)] for i in range(0, ref.shape[0], step)]


def add_into(target, *sources):
    for strip, *others in zip(strips(target), *[strips(source) for source in sources]):
        total = strip[...]
        if len(others) > 1:
            total = plus(total, *[other[...] for other in others])
        else:
            total = total + others[0][...].astype(total.dtype)
        strip[...] = total.astype(target.dtype)


def add_to(target, *sources):
    for strip, *others in zip(strips(target), *[strips(source) for source in sources]):
        strip[...] = plus(*[other[...] for other in others]).astype(target.dtype)


def remote_call(kernel, out, copies, identity, scratch=(), vmem=None, spaces=pl.ANY, inputs=1):
    places = [pl.BlockSpec(memory_space=space) for space in spaces] if isinstance(
        spaces, (list, tuple)
    ) else pl.BlockSpec(memory_space=spaces)
    return pl.pallas_call(
        kernel,
        out_shape=out,
        in_specs=[pl.BlockSpec(memory_space=pl.ANY)] * inputs,
        out_specs=places,
        scratch_shapes=[
            pltpu.SemaphoreType.DMA((copies,)),
            pltpu.SemaphoreType.DMA((copies,)),
            *scratch,
        ],
        compiler_params=pltpu.CompilerParams(
            collective_id=identity, has_side_effects=True, vmem_limit_bytes=vmem
        ),
    )


def team_places():
    xc, l = lax.axis_index("xc"), lax.axis_index("l")
    core = lax.rem(xc, 2)
    other = xc + 1 - 2 * core
    cross, side = lax.rem(xc + 2, 4), 1 - l
    own = {"O": xc * 2 + l, "X": cross * 2 + l, "L": xc * 2 + side, "D": cross * 2 + side}
    far = lax.rem(other + 2, 4)
    twin = {"O": other * 2 + l, "X": far * 2 + l, "L": other * 2 + side, "D": far * 2 + side}
    return own, twin, {"xc": other}, {"xc": cross}, {"l": side}


def team_gather_kernel(extra, *refs):
    if extra:
        x_ref, near_ref, far_ref, o_ref, blocks_ref, send, recv, local = refs
    else:
        x_ref, o_ref, send, recv, local = refs
    own, _, core, cross, side = team_places()
    half = x_ref.shape[0] // 2
    top, low = pl.ds(0, half), pl.ds(half, half)
    keeps = [pltpu.make_async_copy(x_ref, o_ref.at[own["O"]], local.at[0])]
    lane = {"y": 1 - lax.axis_index("y")} if extra else None
    if extra:
        spot = copy_places()
        near, far = blocks_ref.at[spot["O"]], blocks_ref.at[spot["H"]]
        keeps.append(pltpu.make_async_copy(near_ref, near, local.at[1]))
        keeps.append(pltpu.make_async_copy(far_ref, far, local.at[2]))
    for keep in keeps:
        keep.start()
    greet([core, cross, side] + ([lane] if extra else []))
    out = Sender(send, recv)
    twins = [out.go(near_ref, near, lane), out.go(far_ref, far, lane)] if extra else []
    mine, from_side, from_cross = o_ref.at[own["O"]], o_ref.at[own["L"]], o_ref.at[own["X"]]
    diagonal = o_ref.at[own["D"]]
    side_top = out.go(x_ref.at[top], mine.at[top], side)
    cross_low = out.go(x_ref.at[low], mine.at[low], cross)
    side_low = out.go(x_ref.at[low], mine.at[low], side)
    cross_top = out.go(x_ref.at[top], mine.at[top], cross)
    twins.append(out.go(x_ref, mine, core))
    side_top.wait_recv()
    diagonal_top = out.go(from_side.at[top], from_side.at[top], cross)
    twins.append(out.go(from_side.at[top], from_side.at[top], core))
    cross_low.wait_recv()
    diagonal_low = out.go(from_cross.at[low], from_cross.at[low], side)
    twins.append(out.go(from_cross.at[low], from_cross.at[low], core))
    side_low.wait_recv()
    twins.append(out.go(from_side.at[low], from_side.at[low], core))
    cross_top.wait_recv()
    twins.append(out.go(from_cross.at[top], from_cross.at[top], core))
    diagonal_top.wait_recv()
    twins.append(out.go(diagonal.at[top], diagonal.at[top], core))
    diagonal_low.wait_recv()
    twins.append(out.go(diagonal.at[low], diagonal.at[low], core))
    for copy in twins:
        copy.wait_recv()
    out.finish()
    for keep in keeps:
        keep.wait()


def team_gather(block):
    rows, width = block.shape
    gathered = remote_call(
        partial(team_gather_kernel, False),
        jax.ShapeDtypeStruct((8, rows, width), block.dtype),
        13,
        0,
        [pltpu.SemaphoreType.DMA((1,))],
        40 * 2**20,
        pltpu.VMEM,
    )(block)
    return gathered.reshape(8 * rows, width)


def team_gather_with(block, near, far):
    rows, width = block.shape
    if far is None:
        return team_gather(block), lax.all_gather(near, COPIES, axis=0, tiled=True)
    gathered, blocks = remote_call(
        partial(team_gather_kernel, True),
        (
            jax.ShapeDtypeStruct((8, rows, width), block.dtype),
            jax.ShapeDtypeStruct((4, *near.shape), near.dtype),
        ),
        15,
        2,
        [pltpu.SemaphoreType.DMA((3,))],
        vmem=40 * 2**20,
        spaces=[pltpu.VMEM] * 2,
        inputs=3,
    )(block, near, far)
    return gathered.reshape(8 * rows, width), blocks.reshape(-1, near.shape[1])


def team_scatter_kernel(extra, *refs):
    if extra:
        p_ref, f_ref, o_ref, sum_ref, send, recv, local = refs[:7]
        lane_mine, lane_in = refs[12:]
    else:
        p_ref, o_ref, send, recv, local = refs[:5]
    mine, twin_in, cross_in, side_in, bent_in = refs[7:12] if extra else refs[5:]
    own, twin, core, cross, side = team_places()
    half = p_ref.shape[1] // 2
    top, low = pl.ds(0, half), pl.ds(half, half)
    loads = []
    for i, k in enumerate("DXLO"):
        loads.append(pltpu.make_async_copy(p_ref.at[own[k]], mine.at[i], local.at[i]))
        loads[-1].start()
    lane = {"y": 1 - lax.axis_index("y")} if extra else None
    if extra:
        spot = copy_places()
        for j, k in enumerate("HO"):
            loads.append(
                pltpu.make_async_copy(f_ref.at[spot[k]], lane_mine.at[j], local.at[4 + j])
            )
            loads[-1].start()
    greet([core, cross, side] + ([lane] if extra else []))
    out = Sender(send, recv)
    lanes = []
    if extra:
        lanes = [out.go(f_ref.at[spot[k]], lane_in.at[j], lane) for j, k in enumerate("DY")]
    swaps = [out.go(p_ref.at[twin[k]], twin_in.at[i], core) for i, k in enumerate("DXLO")]

    def join(i):
        loads[i].wait()
        swaps[i].wait_recv()
        add_into(mine.at[i], twin_in.at[i])

    join(0)
    bent_cross = out.go(mine.at[0].at[top], bent_in.at[0], cross)
    bent_side = out.go(mine.at[0].at[low], bent_in.at[1], side)
    join(1)
    cross_top = out.go(mine.at[1].at[top], cross_in.at[top], cross)
    join(2)
    side_low = out.go(mine.at[2].at[low], side_in.at[low], side)
    bent_cross.wait_recv()
    add_into(mine.at[2, top], bent_in.at[0])
    side_top = out.go(mine.at[2].at[top], side_in.at[top], side)
    bent_side.wait_recv()
    add_into(mine.at[1, low], bent_in.at[1])
    cross_low = out.go(mine.at[1].at[low], cross_in.at[low], cross)
    loads[3].wait()
    swaps[3].wait_recv()
    cross_top.wait_recv()
    side_low.wait_recv()
    add_to(o_ref.at[top], mine.at[3, top], twin_in.at[3, top], cross_in.at[top])
    add_to(o_ref.at[low], mine.at[3, low], twin_in.at[3, low], side_in.at[low])
    side_top.wait_recv()
    cross_low.wait_recv()
    add_into(o_ref.at[top], side_in.at[top])
    add_into(o_ref.at[low], cross_in.at[low])
    for j, copy in enumerate(lanes):
        loads[4 + j].wait()
        copy.wait_recv()
        add_to(sum_ref.at[j], lane_mine.at[j], lane_in.at[j])
    out.finish()


def team_scatter(partial_sum, lane_sum=None):
    rows, width = partial_sum.shape[0] // 8, partial_sum.shape[1]
    scratch = [
        pltpu.VMEM((4, rows, width), BF16),
        pltpu.VMEM((4, rows, width), BF16),
        pltpu.VMEM((rows, width), BF16),
        pltpu.VMEM((rows, width), BF16),
        pltpu.VMEM((2, rows // 2, width), BF16),
    ]
    total = jax.ShapeDtypeStruct((rows, width), F32)
    blocks = partial_sum.reshape(8, rows, width)
    if lane_sum is None:
        return remote_call(
            partial(team_scatter_kernel, False),
            total,
            10,
            1,
            [pltpu.SemaphoreType.DMA((4,)), *scratch],
            40 * 2**20,
            pltpu.VMEM,
        )(blocks)
    pair = (2, *lane_sum.shape[1:])
    return remote_call(
        partial(team_scatter_kernel, True),
        (total, jax.ShapeDtypeStruct(pair, BF16)),
        12,
        5,
        [pltpu.SemaphoreType.DMA((6,)), *scratch, pltpu.VMEM(pair, BF16), pltpu.VMEM(pair, BF16)],
        48 * 2**20,
        [pltpu.VMEM] * 2,
        2,
    )(blocks, lane_sum)


def team_peers():
    xc, l = lax.axis_index("xc"), lax.axis_index("l")
    peers = []
    for i in range(1, 8):
        far, side = lax.rem(xc + i // 2, 4), lax.rem(l + i % 2, 2)
        peers.append((far * 2 + side, {"xc": far, "l": side}))
    return xc * 2 + l, peers


def full_places():
    y, xc = lax.axis_index("y"), lax.axis_index("xc")
    h, l = lax.axis_index("h"), lax.axis_index("l")
    core = lax.rem(xc, 2)

    def rank(plane, depth, twin=False):
        b = xc + 1 - 2 * core if twin else xc
        b = lax.rem(b + 2, 4) if plane in "XD" else b
        a = 1 - y if plane in "YD" else y
        u = 1 - h if depth in ("H", "HL") else h
        v = 1 - l if depth in ("L", "HL") else l
        return ((a * 4 + b) * 2 + u) * 2 + v

    peers = {
        "C": {"xc": xc + 1 - 2 * core},
        "X": {"xc": lax.rem(xc + 2, 4)},
        "Y": {"y": 1 - y},
        "H": {"h": 1 - h},
        "L": {"l": 1 - l},
    }
    return rank, peers


DEPTHS = ("O", "L", "H", "HL")


def copy_places():
    y, h = lax.axis_index("y"), lax.axis_index("h")
    return {
        "O": y * 2 + h,
        "Y": (1 - y) * 2 + h,
        "H": y * 2 + 1 - h,
        "D": (1 - y) * 2 + 1 - h,
    }


def weights_in_kernel(
    x_ref, gate_in, up_in, down_ref, o_ref, gates_ref, ups_ref, far_ref, send, recv, local, split,
    gate_ref, up_ref,
):
    rank, peers = full_places()
    me, team = team_peers()
    spot = copy_places()

    def at(plane, depth):
        return o_ref.at[rank(plane, depth)]

    pieces = []
    for source, target in ((gate_in, gate_ref), (up_in, up_ref)):
        width = source.shape[1] // 32
        for r in range(8):
            for c in range(4):
                begin = ((c // 2 * 4 + r // 2) * 2 + c % 2) * 2 + r % 2
                pieces.append(
                    pltpu.make_async_copy(
                        source.at[:, pl.ds(begin * width, width)],
                        target.at[r, :, pl.ds(c * width, width)],
                        split.at[len(pieces)],
                    )
                )
    for piece in pieces:
        piece.start()
    keeps = [
        pltpu.make_async_copy(x_ref, at("O", "O"), local.at[0]),
        pltpu.make_async_copy(gate_ref.at[me], gates_ref.at[spot["O"], me], local.at[1]),
        pltpu.make_async_copy(up_ref.at[me], ups_ref.at[spot["O"], me], local.at[2]),
    ]
    keeps[0].start()
    greet([peer for _, peer in team] + [peers["Y"], peers["H"]])
    out = Sender(send, recv)
    swaps, twins = [], []
    to_h = out.go(x_ref, at("O", "O"), peers["H"])
    to_l = out.go(x_ref, at("O", "O"), peers["L"])
    for piece in pieces:
        piece.wait()
    keeps[1].start()
    keeps[2].start()
    for place, peer in team:
        swaps.append(out.go(gate_ref.at[place], gates_ref.at[spot["O"], me], peer))
        swaps.append(out.go(up_ref.at[place], ups_ref.at[spot["O"], me], peer))
    direct, bent = {}, {}

    def begin(depth):
        source = x_ref if depth == "O" else at("O", depth)
        target = at("O", depth)
        to_y = out.go(source, target, peers["Y"])
        to_x = out.go(source, target, peers["X"])
        twins.append(out.go(source, target, peers["C"]))
        direct[depth] = (to_y, to_x)

    def bend(depth):
        to_y, to_x = direct[depth]
        to_y.wait_recv()
        bent[depth] = out.go(at("Y", depth), at("Y", depth), peers["X"])
        twins.append(out.go(at("Y", depth), at("Y", depth), peers["C"]))
        to_x.wait_recv()
        twins.append(out.go(at("X", depth), at("X", depth), peers["C"]))

    def close(depth):
        bent[depth].wait_recv()
        twins.append(out.go(at("D", depth), at("D", depth), peers["C"]))

    blocks = {"gate": gates_ref, "up": ups_ref}
    flats, arrivals = {}, []

    def spread(name):
        mine = blocks[name].at[spot["O"]]
        flats[name] = out.go(mine, mine, peers["H"])
        arrivals.append(out.go(mine, mine, peers["Y"]))

    def corner(name):
        flats[name].wait_recv()
        piece = blocks[name].at[spot["H"]]
        arrivals.append(out.go(piece, piece, peers["Y"]))

    begin("O")
    for swap in swaps:
        swap.wait_recv()
    keeps[1].wait()
    keeps[2].wait()
    spread("gate")
    to_h.wait_recv()
    to_hl = out.go(at("O", "H"), at("O", "H"), peers["L"])
    to_l.wait_recv()
    begin("L")
    begin("H")
    bend("O")
    spread("up")
    to_hl.wait_recv()
    begin("HL")
    bend("L")
    corner("gate")
    arrivals.append(out.go(down_ref, far_ref, peers["H"]))
    bend("H")
    close("O")
    close("L")
    bend("HL")
    corner("up")
    close("H")
    close("HL")
    for copy in twins + arrivals:
        copy.wait_recv()
    out.finish()
    keeps[0].wait()


def weights_in(columns, gate, up, down):
    rows, width = columns.shape
    ranks, depth, part = 8, gate.shape[0], gate.shape[1] // 8
    if not small_grid():
        full = lax.all_gather(columns, AXES, axis=0, tiled=False)
        gates, ups = (
            lax.all_gather(lax.all_to_all(b, TEAM, 0, 0), COPIES, axis=0, tiled=False)
            for b in (column_blocks(gate), column_blocks(up))
        )
        far = None
    else:
        full, gates, ups, far = remote_call(
            weights_in_kernel,
            (
                jax.ShapeDtypeStruct((32, rows, width), BF16),
                jax.ShapeDtypeStruct((4, ranks, depth, part), BF16),
                jax.ShapeDtypeStruct((4, ranks, depth, part), BF16),
                jax.ShapeDtypeStruct(down.shape, BF16),
            ),
            14 + 3 + 28 + 7,
            3,
            [
                pltpu.SemaphoreType.DMA((3,)),
                pltpu.SemaphoreType.DMA((64,)),
                pltpu.VMEM((ranks, depth, part), BF16),
                pltpu.VMEM((ranks, depth, part), BF16),
            ],
            spaces=[pl.ANY] * 4,
            inputs=4,
        )(columns, gate, up, down)
    return full.reshape(-1, width), gates.reshape(-1, part), ups.reshape(-1, part), far


PLANES = ("D", "X", "Y", "O")
SUMS = ("HL", "L", "H", "O")


def grads_out_kernel(edges, *refs):
    n = len(edges)
    parts, (far_ref, near_ref, raw_ref) = refs[:n], refs[n : n + 3]
    o_ref, gate_ref, up_ref, send, recv, local = refs[n + 3 : n + 9]
    mine, twin_in, cross_in, lane_in, bent_in, depth_in = refs[n + 9 : n + 15]
    flat, flat_h, back_in = refs[n + 15 : n + 17], refs[n + 17 : n + 19], refs[n + 19 : n + 21]
    flat_far, flat_y = refs[n + 21], refs[n + 22 :]
    rank, peers = full_places()
    me, team = team_peers()
    spot = copy_places()
    half = mine.shape[2] // 2
    top, low = pl.ds(0, half), pl.ds(half, half)
    loads, swaps, flights = {}, {}, {}
    count = 0

    def load(source, target):
        nonlocal count
        copy = pltpu.make_async_copy(source, target, local.at[count])
        count += 1
        copy.start()
        return copy

    for t, depth in enumerate(SUMS):
        for k, plane in enumerate(PLANES):
            place = rank(plane, depth)
            loads[t, k] = [
                load(part.at[place], mine.at[t, k, :, pl.ds(begin, part.shape[2])])
                for part, begin in zip(parts, edges)
            ]
    own_loads = [load(near_ref, flat[0]), load(raw_ref.at[spot["O"]], flat[1])]
    far_load = load(raw_ref.at[spot["H"]], flat_far)
    greet([peer for _, peer in team] + [peers["Y"], peers["H"]])
    out = Sender(send, recv)

    def swap(t):
        for k, plane in enumerate(PLANES):
            place = rank(plane, SUMS[t], True)
            swaps[t, k] = [
                out.go(
                    part.at[place], twin_in.at[t, k, :, pl.ds(begin, part.shape[2])], peers["C"]
                )
                for part, begin in zip(parts, edges)
            ]

    def join(t, k):
        for copy in loads[t, k]:
            copy.wait()
        for copy in swaps[t, k]:
            copy.wait_recv()
        add_into(mine.at[t, k], twin_in.at[t, k])

    def diagonal(t):
        flights[t] = [
            out.go(mine.at[t, 0, top], bent_in.at[t, top], peers["X"]),
            out.go(mine.at[t, 0, low], bent_in.at[t, low], peers["Y"]),
        ]

    def straight(t):
        flights[t].append(out.go(mine.at[t, 1, top], cross_in.at[t, top], peers["X"]))
        flights[t].append(out.go(mine.at[t, 2, low], lane_in.at[t, low], peers["Y"]))

    def bend(t):
        flights[t][0].wait_recv()
        add_into(mine.at[t, 2, top], bent_in.at[t, top])
        flights[t].append(out.go(mine.at[t, 2, top], lane_in.at[t, top], peers["Y"]))
        flights[t][1].wait_recv()
        add_into(mine.at[t, 1, low], bent_in.at[t, low])
        flights[t].append(out.go(mine.at[t, 1, low], cross_in.at[t, low], peers["X"]))

    def close(t):
        for copy in flights[t][2:]:
            copy.wait_recv()
        return (cross_in.at[t], lane_in.at[t])

    swap(0)
    h_side = [out.go(far_ref, flat_h[0], peers["H"])]
    y_side = [out.go(raw_ref.at[spot["D"]], flat_y[0], peers["Y"])]
    swap(1)
    swap(2)
    swap(3)
    for t in (0, 1):
        for k in (0, 1, 2):
            join(t, k)
        diagonal(t)
        straight(t)
    join(0, 3)
    join(1, 3)
    far_load.wait()
    y_side[0].wait_recv()
    add_into(flat_far, flat_y[0])
    h_side.append(out.go(flat_far, flat_h[1], peers["H"]))
    y_side.append(out.go(raw_ref.at[spot["Y"]], flat_y[1], peers["Y"]))
    bend(0)
    for k in (0, 1, 2):
        join(2, k)
    diagonal(2)
    straight(2)
    bend(1)
    for k in (0, 1, 2):
        join(3, k)
    diagonal(3)
    straight(3)
    join(2, 3)
    join(3, 3)
    add_into(mine.at[0, 3], *close(0))
    to_hl = out.go(mine.at[0, 3], depth_in.at[0], peers["L"])
    bend(2)
    add_into(mine.at[1, 3], *close(1))
    to_l = out.go(mine.at[1, 3], depth_in.at[1], peers["L"])
    bend(3)
    ready = close(2)
    to_hl.wait_recv()
    add_into(mine.at[2, 3], *ready, depth_in.at[0])
    to_h = out.go(mine.at[2, 3], depth_in.at[2], peers["H"])
    returns = []
    for i in range(2):
        own_loads[i].wait()
        h_side[i].wait_recv()
        arrived = [flat_h[i]]
        if i == 1:
            y_side[1].wait_recv()
            arrived.append(flat_y[1])
        add_into(flat[i], *arrived)
        returns.append([load(flat[i].at[me], back_in[i].at[me])])
        for place, peer in team:
            returns[i].append(out.go(flat[i].at[place], back_in[i].at[me], peer))
    ready = close(3)
    to_l.wait_recv()
    add_to(o_ref, mine.at[3, 3], *ready, depth_in.at[1])
    to_h.wait_recv()
    add_into(o_ref, depth_in.at[2])
    for i, target in enumerate((gate_ref, up_ref)):
        returns[i][0].wait()
        for copy in returns[i][1:]:
            copy.wait_recv()
        width = target.shape[1] // 32
        for r in range(8):
            for c in range(4):
                begin = ((c // 2 * 4 + r // 2) * 2 + c % 2) * 2 + r % 2
                target[:, pl.ds(begin * width, width)] = back_in[i][
                    r, :, pl.ds(c * width, width)
                ].astype(F32)
    out.finish()


def grads_out(parts, gate, up):
    shares = lax.axis_size("y") * lax.axis_size("h") * 8
    rows = parts[0].shape[0] // shares
    blocks = [part.reshape(shares, rows, part.shape[1]) for part in parts]
    if not small_grid():
        block = jnp.concatenate(blocks, axis=2)
        total = lax.psum_scatter(block, AXES, scatter_dimension=0, tiled=False).astype(F32)
        up = lax.psum_scatter(up, COPIES, scatter_dimension=0, tiled=False)
        gate, up = (
            from_column_blocks(lax.all_to_all(value, TEAM, 0, 0)).astype(F32)
            for value in (gate, up)
        )
        return total, gate, up
    edges = [0]
    for part in parts:
        edges.append(edges[-1] + part.shape[1])
    width = edges.pop()
    flat = gate[0].shape
    return remote_call(
        partial(grads_out_kernel, tuple(edges)),
        (
            jax.ShapeDtypeStruct((rows, width), F32),
            jax.ShapeDtypeStruct((flat[1], 8 * flat[2]), F32),
            jax.ShapeDtypeStruct((flat[1], 8 * flat[2]), F32),
        ),
        16 * len(parts) + 24 + 3 + 4 + 14,
        4,
        [
            pltpu.SemaphoreType.DMA((16 * len(parts) + 3 + 2,)),
            pltpu.VMEM((4, 4, rows, width), BF16),
            pltpu.VMEM((4, 4, rows, width), BF16),
            pltpu.VMEM((4, rows, width), BF16),
            pltpu.VMEM((4, rows, width), BF16),
            pltpu.VMEM((4, rows, width), BF16),
            pltpu.VMEM((3, rows, width), BF16),
            *[pltpu.VMEM(flat, BF16)] * 9,
        ],
        56 * 2**20,
        [pltpu.VMEM] * 3,
        len(parts) + 3,
    )(*blocks, *gate, up)


def small_grid():
    return lax.axis_size("y") == 2 and lax.axis_size("h") == 2


def lane_sums(value):
    if not small_grid():
        return lax.psum_scatter(value, COPIES, scatter_dimension=0, tiled=False)
    spot = copy_places()

    def piece(k):
        return lax.dynamic_index_in_dim(value, spot[k], axis=0, keepdims=False)

    sent = jnp.stack([piece("D"), piece("Y")])
    arrived = lax.ppermute(sent, "y", [(0, 1), (1, 0)])
    return [plus(piece(k), arrived[j]).astype(BF16) for j, k in enumerate("HO")]


def shift(block, distance):
    pieces = lax.axis_size("h") * lax.axis_size("l")
    route = [(i, i + distance) for i in range(pieces) if 0 <= i + distance < pieces]
    return lax.ppermute(block, ("h", "l"), route)


def column_blocks(weight):
    ys, hs = lax.axis_size("y"), lax.axis_size("h")
    depth, width = weight.shape
    split = weight.reshape(depth, ys, 4, hs, 2, width // (ys * hs * 8))
    return split.transpose(2, 4, 0, 1, 3, 5).reshape(8, depth, width // 8)


def from_column_blocks(blocks):
    ys, hs = lax.axis_size("y"), lax.axis_size("h")
    depth, width = blocks.shape[1:]
    split = blocks.reshape(4, 2, depth, ys, hs, width // (ys * hs)).transpose(2, 3, 0, 4, 1, 5)
    return split.reshape(depth, 8 * width)


def depth_order(value):
    ys, hs = lax.axis_size("y"), lax.axis_size("h")
    rows, width = value.shape
    split = value.reshape(rows, ys, 4, hs, width // (4 * ys * hs))
    return split.transpose(0, 1, 3, 2, 4).reshape(rows, width)


def from_depth_order(value):
    ys, hs = lax.axis_size("y"), lax.axis_size("h")
    rows, width = value.shape
    split = value.reshape(rows, ys, hs, 4, width // (4 * ys * hs))
    return split.transpose(0, 1, 3, 2, 4).reshape(rows, width)


def layer(*args):
    (
        hidden_in,
        layer_input,
        seq_lengths,
        cotangent,
        query_weight,
        key_matrix,
        value_matrix,
        output_weight,
        laurel_left,
        laurel_right,
        input_gate,
        input_projection,
        gate_weight,
        up_weight,
        down_weight,
        norm_gains,
        head_gains,
    ) = args
    rows, width = hidden_in.shape
    hops = max(1, WINDOW // rows)
    groups = QUERY_HEADS // KEY_VALUE_HEADS
    piece = lax.axis_index(("h", "l"))
    places = piece * rows + jnp.arange(rows, dtype=jnp.int32)
    key_places = (piece - hops) * rows + jnp.arange((hops + 1) * rows, dtype=jnp.int32)
    live = (places < seq_lengths[0]).astype(F32)[:, None]

    head_width = QUERY_HEADS * HEAD_SIZE
    kv_width = KEY_VALUE_HEADS * HEAD_SIZE
    rank = laurel_left.shape[1]
    side = layer_input.shape[1]
    depth, head_part = query_weight.shape[0], head_gains.shape[1]
    columns = (
        query_weight,
        key_matrix,
        value_matrix,
        output_weight,
        input_gate,
        input_projection.T,
        laurel_left,
        laurel_right.T,
        norm_gains.T,
        jnp.pad(head_gains.T, ((0, depth - head_part), (0, 0))),
    )
    edges = [0]
    for column in columns:
        edges.append(edges[-1] + column.shape[1])
    full_width = -(-edges[-1] // 128) * 128
    local_columns = jnp.pad(
        jnp.concatenate(columns, axis=1), ((0, 0), (0, full_width - edges[-1]))
    )
    full, gate_cols, up_cols, far_down = weights_in(
        local_columns, gate_weight, up_weight, down_weight
    )
    first = full[:, : edges[3]]
    output_all, side_gate_all, projection_all, left_all, right_all = (
        full[:, edges[i] : edges[i + 1]] for i in range(3, 8)
    )
    gains = full[:, edges[8] : edges[9]].T.astype(F32)
    head_gain = (
        full[:, edges[9] : edges[10]].reshape(-1, depth, 2)[:, :head_part].reshape(-1, 2).T
    ).astype(F32)

    hidden = hidden_in.astype(F32)
    side_input = layer_input.astype(F32)
    cosine, sine = rope_tables(places)

    hidden_inv = inverse_rms(hidden)
    normed = hidden * hidden_inv * gains[0]
    normed_low = normed.astype(BF16)
    raw = dot(normed_low, first)
    query_raw = raw[:, :head_width].reshape(rows, QUERY_HEADS, HEAD_SIZE)
    key_raw = raw[:, head_width : head_width + kv_width].reshape(rows, KEY_VALUE_HEADS, HEAD_SIZE)
    value_raw = raw[:, head_width + kv_width :].reshape(
        rows, KEY_VALUE_HEADS, HEAD_SIZE
    )
    left_low = dot(normed_low, left_all).astype(BF16)
    query_inv = inverse_rms(query_raw)
    key_inv = inverse_rms(key_raw)
    value_inv = inverse_rms(value_raw)
    query_low = rotate(query_raw * query_inv * head_gain[0], cosine, sine).astype(BF16)
    key_low = rotate(key_raw * key_inv * head_gain[1], cosine, sine).astype(BF16)
    value_low = (value_raw * value_inv).astype(BF16)
    moving = jnp.stack([key_low, value_low])
    window = jnp.concatenate([shift(moving, hop) for hop in range(hops, 0, -1)] + [moving], axis=1)
    grouped = query_low.reshape(rows, KEY_VALUE_HEADS, groups, HEAD_SIZE)
    scores = jnp.einsum("qkgd,tkd->kgqt", grouped, window[0], preferred_element_type=F32)
    allowed = (
        (key_places[None, :] <= places[:, None])
        & (places[:, None] - key_places[None, :] < WINDOW)
        & (key_places[None, :] >= 0)
    )
    scores = jnp.where(allowed, scores, MASKED)
    weights = jnp.exp(scores - jnp.max(scores, axis=-1, keepdims=True))
    probs = weights / jnp.sum(weights, axis=-1, keepdims=True)
    probs_low = probs.astype(BF16)
    mixed = (
        jnp.einsum("kgqt,tkd->qkgd", probs_low, window[1], preferred_element_type=F32)
        .reshape(rows, head_width)
        .astype(BF16)
    )
    attention_raw = dot(mixed, output_all)
    attention_inv = inverse_rms(attention_raw)
    right_raw = dot(left_low, right_all, 1, 1)
    right_inv = inverse_rms(right_raw)
    merged = (
        hidden
        + attention_raw * attention_inv * gains[1]
        + normed
        + right_raw * right_inv * gains[2]
    ) * HALF_ROOT
    merged_inv = inverse_rms(merged)
    expand_low = (merged * merged_inv * gains[3]).astype(BF16)

    expand_all, down_rows = team_gather_with(depth_order(expand_low), down_weight, far_down)
    gate_raw = dot(expand_all, gate_cols)
    up_raw = dot(expand_all, up_cols)
    act_low = (gelu(gate_raw) * up_raw).astype(BF16)
    reduced_raw = team_scatter(dot(act_low, down_rows).astype(BF16))
    reduced_inv = inverse_rms(reduced_raw)
    after_feed = merged + reduced_raw * reduced_inv * gains[4]
    after_low = after_feed.astype(BF16)
    side_raw = dot(after_low, side_gate_all)
    side_low = (gelu(side_raw) * side_input).astype(BF16)
    side_out = dot(side_low, projection_all, 1, 1)
    side_inv = inverse_rms(side_out)
    block_out = (after_feed + side_out * side_inv * gains[5]) * live

    upstream = cotangent.astype(F32) * live
    grad_side, gain_five = rms_back(side_out, side_inv, gains[5], upstream)
    grad_side_low = grad_side.astype(BF16)
    grad_side_raw = (
        dot(grad_side_low, projection_all) * side_input * gelu_slope(side_raw)
    ).astype(BF16)
    grad_after = upstream + dot(grad_side_raw, side_gate_all, 1, 1)
    grad_reduced, gain_four = rms_back(reduced_raw, reduced_inv, gains[4], grad_after)
    grad_reduced_low = grad_reduced.astype(BF16)

    grad_reduced_all = team_gather(grad_reduced_low)
    grad_product = dot(grad_reduced_all, down_rows, 1, 1)
    grad_gate_low = (grad_product * up_raw * gelu_slope(gate_raw)).astype(BF16)
    grad_up_low = (grad_product * gelu(gate_raw)).astype(BF16)
    part_down = dot(act_low, grad_reduced_all, 0, 0).astype(BF16)
    part_low = (dot(grad_gate_low, gate_cols, 1, 1) + dot(grad_up_low, up_cols, 1, 1)).astype(BF16)
    part_gate = dot(expand_all, grad_gate_low, 0, 0).astype(BF16)
    part_up = dot(expand_all, grad_up_low, 0, 0).astype(BF16)
    down_blocks = part_down.reshape(-1, *down_weight.shape)
    part_gate, part_up = (
        value.reshape(-1, 8, depth, value.shape[1]) for value in (part_gate, part_up)
    )
    part_low, part_gate, part_up = lax.optimization_barrier((part_low, part_gate, part_up))
    if small_grid():
        part, down_sums = team_scatter(part_low, down_blocks)
        grad_down = plus(down_sums[1], lax.ppermute(down_sums[0], "h", [(0, 1), (1, 0)]))
    else:
        part = team_scatter(part_low)
        grad_down = lax.psum_scatter(down_blocks, COPIES, scatter_dimension=0).astype(F32)
    sums_gate = lane_sums(part_gate)
    part = from_depth_order(part)
    grad_merged, gain_three = rms_back(merged, merged_inv, gains[3], part)
    grad_sum = (grad_after + grad_merged) * HALF_ROOT
    grad_right, gain_two = rms_back(right_raw, right_inv, gains[2], grad_sum)
    grad_right_low = grad_right.astype(BF16)
    grad_left_low = dot(grad_right_low, right_all).astype(BF16)
    grad_attention, gain_one = rms_back(attention_raw, attention_inv, gains[1], grad_sum)
    grad_attention_low = grad_attention.astype(BF16)
    grad_mixed = (
        dot(grad_attention_low, output_all, 1, 1)
        .astype(BF16)
        .reshape(rows, KEY_VALUE_HEADS, groups, HEAD_SIZE)
    )
    grad_probs = jnp.einsum("qkgd,tkd->kgqt", grad_mixed, window[1], preferred_element_type=F32)
    inner = jnp.sum(probs * grad_probs, axis=-1, keepdims=True)
    grad_scores = (probs * (grad_probs - inner)).astype(BF16)
    grad_query_rot = jnp.einsum(
        "kgqt,tkd->qkgd", grad_scores, window[0], preferred_element_type=F32
    ).reshape(rows, QUERY_HEADS, HEAD_SIZE)
    grad_window = jnp.stack(
        [
            jnp.einsum("kgqt,qkgd->tkd", grad_scores, grouped, preferred_element_type=F32),
            jnp.einsum("kgqt,qkgd->tkd", probs_low, grad_mixed, preferred_element_type=F32),
        ]
    )
    carried = grad_window[:, hops * rows :]
    for hop in range(1, hops + 1):
        begin = (hops - hop) * rows
        carried = carried + shift(
            grad_window[:, begin : begin + rows].astype(BF16), -hop
        ).astype(F32)
    grad_query, head_zero = rms_back(
        query_raw, query_inv, head_gain[0], rotate(grad_query_rot, cosine, -sine)
    )
    grad_key, head_one = rms_back(
        key_raw, key_inv, head_gain[1], rotate(carried[0], cosine, -sine)
    )
    grad_value, _ = rms_back(value_raw, value_inv, 1.0, carried[1])
    grad_raw = jnp.concatenate(
        [
            grad_query.reshape(rows, head_width).astype(BF16),
            grad_key.reshape(rows, kv_width).astype(BF16),
            grad_value.reshape(rows, kv_width).astype(BF16),
        ],
        axis=1,
    )
    grad_normed = grad_sum + dot(grad_raw, first, 1, 1) + dot(grad_left_low, left_all, 1, 1)
    grad_input, gain_zero = rms_back(hidden, hidden_inv, gains[0], grad_normed)
    grad_hidden = grad_sum + grad_input

    gain_grads = jnp.stack(
        [
            jnp.sum(g, axis=0)
            for g in (gain_zero, gain_one, gain_two, gain_three, gain_four, gain_five)
        ]
    )
    head_grads = jnp.stack([jnp.sum(head_zero, axis=(0, 1)), jnp.sum(head_one, axis=(0, 1))])

    head_column = jnp.pad(
        head_grads.T.reshape(-1, head_part, 2), ((0, 0), (0, depth - head_part), (0, 0))
    ).reshape(-1, 2)
    tail = full_width - edges[6]
    small = (
        dot(normed_low, jnp.pad(grad_left_low, ((0, 0), (0, tail - rank))), 0, 0)
        + dot(grad_right_low, jnp.pad(left_low, ((0, 0), (rank, tail - 2 * rank))), 0, 0)
        + jnp.pad(gain_grads.T, ((0, 0), (2 * rank, tail - 2 * rank - 6)))
        + jnp.pad(head_column, ((0, 0), (2 * rank + 6, tail - 2 * rank - 8)))
    )
    weight_grads = (
        dot(normed_low, grad_raw, 0, 0).astype(BF16),
        dot(mixed, grad_attention_low, 0, 0).astype(BF16),
        dot(after_low, grad_side_raw, 0, 0).astype(BF16),
        dot(grad_side_low, side_low, 0, 0).astype(BF16),
        small.astype(BF16),
    )
    summed, grad_gate, grad_up = grads_out(weight_grads, sums_gate, part_up)
    (
        d_query,
        d_key,
        d_value,
        d_output,
        d_side_gate,
        d_projection,
        d_left,
        d_right,
        d_gains,
        d_heads,
    ) = (summed[:, edges[i] : edges[i + 1]] for i in range(10))
    d_right, d_projection, d_gains = d_right.T, d_projection.T, d_gains.T
    d_heads = d_heads[:head_part].T
    return (
        block_out,
        grad_hidden,
        d_query,
        d_key,
        d_value,
        d_output,
        d_left,
        d_right,
        d_side_gate,
        d_projection,
        grad_gate,
        grad_up,
        grad_down,
        d_gains,
        d_heads,
    )


def solution(mesh):
    dp, seq = mesh.shape["dp"], mesh.shape["seq"]
    grid = Mesh(mesh.devices.reshape(dp // 4, 4, seq // 2, 2), AXES)
    row, column = P(AXES, None), P(None, AXES)
    return jax.shard_map(
        layer,
        mesh=grid,
        in_specs=(row, row, P(("y", "xc")))
        + (row,) * 6
        + (column, row, column)
        + (row,) * 3
        + (column,) * 2,
        out_specs=(row,) * 7 + (column, row, column) + (row,) * 3 + (column,) * 2,
        check_vma=False,
    )
```

```python
from functools import partial

import jax
import jax.numpy as jnp
from jax import lax
from jax.experimental import pallas as pl
from jax.experimental.pallas import tpu as pltpu
from jax.sharding import Mesh, PartitionSpec as P

QUERY_HEADS = 8
KEY_VALUE_HEADS = 2
HEAD_SIZE = 256
WINDOW = 512
EPSILON = 1e-06
ROPE_BASE = 10000.0
HALF_ROOT = 0.7071067811865476
MASKED = -1e30
GELU_SCALE = 0.7978845608028654
GELU_CUBE = 0.044715
F32 = jnp.float32
BF16 = jnp.bfloat16


def dot(left, right, left_dim=1, right_dim=0):
    return lax.dot_general(
        left, right, (((left_dim,), (right_dim,)), ((), ())), preferred_element_type=F32
    )


def inverse_rms(value):
    return lax.rsqrt(jnp.mean(value * value, axis=-1, keepdims=True) + EPSILON)


def rms_back(value, inverse, gain, grad):
    scaled = grad * gain
    inner = jnp.mean(scaled * value, axis=-1, keepdims=True)
    unit = value * inverse
    return inverse * (scaled - unit * (inverse * inner)), grad * unit


def rope_tables(positions):
    half = HEAD_SIZE // 2
    rate = ROPE_BASE ** (-jnp.arange(half, dtype=F32) * 2.0 / HEAD_SIZE)
    angle = positions.astype(F32)[:, None] * rate[None, :]
    return jnp.cos(angle), jnp.sin(angle)


def head_columns(head):
    return pl.ds(head * HEAD_SIZE, HEAD_SIZE)


def heads_kernel(raw_ref, cos_ref, sin_ref, gain_ref, query_ref, pair_ref):
    half = HEAD_SIZE // 2
    cosine, sine = cos_ref[...], sin_ref[...]
    for head in range(QUERY_HEADS + 2 * KEY_VALUE_HEADS):
        value = raw_ref[:, head_columns(head)]
        value = value * inverse_rms(value)
        slot, kind = head - QUERY_HEADS, (head - QUERY_HEADS) // KEY_VALUE_HEADS
        if kind == 1:
            pair_ref[1, :, head_columns(slot - KEY_VALUE_HEADS)] = value.astype(BF16)
            continue
        value = value * gain_ref[pl.ds(0 if slot < 0 else 1, 1), :]
        first, second = value[:, :half], value[:, half:]
        turned = jnp.concatenate(
            [first * cosine - second * sine, second * cosine + first * sine], axis=1
        ).astype(BF16)
        if slot < 0:
            query_ref[:, head_columns(head)] = turned
        else:
            pair_ref[0, :, head_columns(slot)] = turned


def heads_back_kernel(
    raw_ref, query_ref, pair_ref, cos_ref, sin_ref, gain_ref, out_ref, gain_grad_ref
):
    half = HEAD_SIZE // 2
    cosine, sine = cos_ref[...], sin_ref[...]

    @pl.when(pl.program_id(0) == 0)
    def _():
        gain_grad_ref[...] = jnp.zeros_like(gain_grad_ref)

    for head in range(QUERY_HEADS + 2 * KEY_VALUE_HEADS):
        value = raw_ref[:, head_columns(head)]
        slot, kind = head - QUERY_HEADS, (head - QUERY_HEADS) // KEY_VALUE_HEADS
        if slot < 0:
            grad = query_ref[:, head_columns(head)]
        else:
            grad = pair_ref[kind, :, head_columns(slot - kind * KEY_VALUE_HEADS)]
        gain = 1.0
        if kind < 1:
            row = pl.ds(0 if slot < 0 else 1, 1)
            gain = gain_ref[row, :]
            first, second = grad[:, :half], grad[:, half:]
            grad = jnp.concatenate(
                [first * cosine + second * sine, second * cosine - first * sine], axis=1
            )
        result, gain_part = rms_back(value, inverse_rms(value), gain, grad)
        out_ref[:, head_columns(head)] = result.astype(BF16)
        if kind < 1:
            gain_grad_ref[row, :] += jnp.sum(gain_part, axis=0, keepdims=True)


def strip_spec(rows, *shape):
    front = len(shape) - 2
    return pl.BlockSpec(
        (*shape[:front], rows, shape[-1]), lambda i: (*(0,) * front, i, 0)
    )


def heads(raw, cosine, sine, gain):
    rows, width = raw.shape
    strip = min(64, rows)
    query_width, pair_width = QUERY_HEADS * HEAD_SIZE, KEY_VALUE_HEADS * HEAD_SIZE
    return pl.pallas_call(
        heads_kernel,
        out_shape=(
            jax.ShapeDtypeStruct((rows, query_width), BF16),
            jax.ShapeDtypeStruct((2, rows, pair_width), BF16),
        ),
        grid=(rows // strip,),
        in_specs=[
            strip_spec(strip, rows, width),
            strip_spec(strip, *cosine.shape),
            strip_spec(strip, *sine.shape),
            pl.BlockSpec(gain.shape, lambda i: (0, 0)),
        ],
        out_specs=(
            strip_spec(strip, rows, query_width),
            strip_spec(strip, 2, rows, pair_width),
        ),
    )(raw, cosine, sine, gain)


def heads_back(raw, query_grad, pair_grad, cosine, sine, gain):
    rows, width = raw.shape
    strip = min(64, rows)
    return pl.pallas_call(
        heads_back_kernel,
        out_shape=(
            jax.ShapeDtypeStruct((rows, width), BF16),
            jax.ShapeDtypeStruct(gain.shape, F32),
        ),
        grid=(rows // strip,),
        in_specs=[
            strip_spec(strip, rows, width),
            strip_spec(strip, *query_grad.shape),
            strip_spec(strip, *pair_grad.shape),
            strip_spec(strip, *cosine.shape),
            strip_spec(strip, *sine.shape),
            pl.BlockSpec(gain.shape, lambda i: (0, 0)),
        ],
        out_specs=(
            strip_spec(strip, rows, width),
            pl.BlockSpec(gain.shape, lambda i: (0, 0)),
        ),
    )(raw, query_grad, pair_grad, cosine, sine, gain)


def gelu_tanh(value):
    return jnp.tanh(GELU_SCALE * (value + GELU_CUBE * value * value * value))


def gelu(value):
    return 0.5 * value * (1.0 + gelu_tanh(value))


def gelu_slope(value):
    t = gelu_tanh(value)
    inner = GELU_SCALE * (1.0 + 3.0 * GELU_CUBE * value * value)
    return 0.5 * (1.0 + t) + 0.5 * value * (1.0 - t * t) * inner


AXES = ("y", "xc", "h", "l")
TEAM = ("xc", "l")
COPIES = ("y", "h")


class Sender:
    def __init__(self, send, recv):
        self.send, self.recv, self.count, self.started = send, recv, 0, []

    def go(self, source, target, peer):
        i = self.count
        self.count += 1
        copy = pltpu.make_async_remote_copy(
            src_ref=source,
            dst_ref=target,
            send_sem=self.send.at[i],
            recv_sem=self.recv.at[i],
            device_id=peer,
            device_id_type=pl.DeviceIdType.MESH,
        )
        copy.start()
        self.started.append(copy)
        return copy

    def finish(self):
        for copy in self.started:
            copy.wait_send()


def greet(peers):
    barrier = pltpu.get_barrier_semaphore()
    for peer in peers:
        pl.semaphore_signal(barrier, inc=1, device_id=peer, device_id_type=pl.DeviceIdType.MESH)
    pl.semaphore_wait(barrier, len(peers))


def plus(*parts):
    total = parts[0].astype(F32)
    for part in parts[1:]:
        total = total + part.astype(F32)
    return total


def strips(ref):
    if len(ref.shape) == 4:
        return [ref.at[i, j] for i in range(ref.shape[0]) for j in range(ref.shape[1])]
    step = min(16, ref.shape[0])
    return [ref.at[pl.ds(i, step)] for i in range(0, ref.shape[0], step)]


def add_into(target, *sources):
    for strip, *others in zip(strips(target), *[strips(source) for source in sources]):
        total = strip[...]
        if len(others) > 1:
            total = plus(total, *[other[...] for other in others])
        else:
            total = total + others[0][...].astype(total.dtype)
        strip[...] = total.astype(target.dtype)


def add_to(target, *sources):
    for strip, *others in zip(strips(target), *[strips(source) for source in sources]):
        strip[...] = plus(*[other[...] for other in others]).astype(target.dtype)


def remote_call(kernel, out, copies, identity, scratch=(), vmem=None, spaces=pl.ANY, inputs=1):
    places = [pl.BlockSpec(memory_space=space) for space in spaces] if isinstance(
        spaces, (list, tuple)
    ) else pl.BlockSpec(memory_space=spaces)
    return pl.pallas_call(
        kernel,
        out_shape=out,
        in_specs=[pl.BlockSpec(memory_space=pl.ANY)] * inputs,
        out_specs=places,
        scratch_shapes=[
            pltpu.SemaphoreType.DMA((copies,)),
            pltpu.SemaphoreType.DMA((copies,)),
            *scratch,
        ],
        compiler_params=pltpu.CompilerParams(
            collective_id=identity, has_side_effects=True, vmem_limit_bytes=vmem
        ),
    )


def team_places():
    xc, l = lax.axis_index("xc"), lax.axis_index("l")
    core = lax.rem(xc, 2)
    other = xc + 1 - 2 * core
    cross, side = lax.rem(xc + 2, 4), 1 - l
    own = {"O": xc * 2 + l, "X": cross * 2 + l, "L": xc * 2 + side, "D": cross * 2 + side}
    far = lax.rem(other + 2, 4)
    twin = {"O": other * 2 + l, "X": far * 2 + l, "L": other * 2 + side, "D": far * 2 + side}
    return own, twin, {"xc": other}, {"xc": cross}, {"l": side}


def team_gather_kernel(extra, *refs):
    if extra:
        x_ref, near_ref, far_ref, o_ref, blocks_ref, send, recv, local = refs
    else:
        x_ref, o_ref, send, recv, local = refs
    own, _, core, cross, side = team_places()
    half = x_ref.shape[0] // 2
    top, low = pl.ds(0, half), pl.ds(half, half)
    keeps = [pltpu.make_async_copy(x_ref, o_ref.at[own["O"]], local.at[0])]
    lane = {"y": 1 - lax.axis_index("y")} if extra else None
    if extra:
        spot = copy_places()
        near, far = blocks_ref.at[spot["O"]], blocks_ref.at[spot["H"]]
        keeps.append(pltpu.make_async_copy(near_ref, near, local.at[1]))
        keeps.append(pltpu.make_async_copy(far_ref, far, local.at[2]))
    for keep in keeps:
        keep.start()
    greet([core, cross, side] + ([lane] if extra else []))
    out = Sender(send, recv)
    twins = [out.go(near_ref, near, lane), out.go(far_ref, far, lane)] if extra else []
    mine, from_side, from_cross = o_ref.at[own["O"]], o_ref.at[own["L"]], o_ref.at[own["X"]]
    diagonal = o_ref.at[own["D"]]
    side_top = out.go(x_ref.at[top], mine.at[top], side)
    cross_low = out.go(x_ref.at[low], mine.at[low], cross)
    side_low = out.go(x_ref.at[low], mine.at[low], side)
    cross_top = out.go(x_ref.at[top], mine.at[top], cross)
    twins.append(out.go(x_ref, mine, core))
    side_top.wait_recv()
    diagonal_top = out.go(from_side.at[top], from_side.at[top], cross)
    twins.append(out.go(from_side.at[top], from_side.at[top], core))
    cross_low.wait_recv()
    diagonal_low = out.go(from_cross.at[low], from_cross.at[low], side)
    twins.append(out.go(from_cross.at[low], from_cross.at[low], core))
    side_low.wait_recv()
    twins.append(out.go(from_side.at[low], from_side.at[low], core))
    cross_top.wait_recv()
    twins.append(out.go(from_cross.at[top], from_cross.at[top], core))
    diagonal_top.wait_recv()
    twins.append(out.go(diagonal.at[top], diagonal.at[top], core))
    diagonal_low.wait_recv()
    twins.append(out.go(diagonal.at[low], diagonal.at[low], core))
    for copy in twins:
        copy.wait_recv()
    out.finish()
    for keep in keeps:
        keep.wait()


def team_gather(block):
    rows, width = block.shape
    gathered = remote_call(
        partial(team_gather_kernel, False),
        jax.ShapeDtypeStruct((8, rows, width), block.dtype),
        13,
        0,
        [pltpu.SemaphoreType.DMA((1,))],
        40 * 2**20,
        pltpu.VMEM,
    )(block)
    return gathered.reshape(8 * rows, width)


def team_gather_with(block, near, far):
    rows, width = block.shape
    if far is None:
        return team_gather(block), lax.all_gather(near, COPIES, axis=0, tiled=True)
    gathered, blocks = remote_call(
        partial(team_gather_kernel, True),
        (
            jax.ShapeDtypeStruct((8, rows, width), block.dtype),
            jax.ShapeDtypeStruct((4, *near.shape), near.dtype),
        ),
        15,
        2,
        [pltpu.SemaphoreType.DMA((3,))],
        vmem=40 * 2**20,
        spaces=[pltpu.VMEM] * 2,
        inputs=3,
    )(block, near, far)
    return gathered.reshape(8 * rows, width), blocks.reshape(-1, near.shape[1])


def team_scatter_kernel(extra, *refs):
    if extra:
        p_ref, f_ref, o_ref, sum_ref, send, recv, local = refs[:7]
        lane_mine, lane_in = refs[12:]
    else:
        p_ref, o_ref, send, recv, local = refs[:5]
    mine, twin_in, cross_in, side_in, bent_in = refs[7:12] if extra else refs[5:]
    own, twin, core, cross, side = team_places()
    half = p_ref.shape[1] // 2
    top, low = pl.ds(0, half), pl.ds(half, half)
    loads = []
    for i, k in enumerate("DXLO"):
        loads.append(pltpu.make_async_copy(p_ref.at[own[k]], mine.at[i], local.at[i]))
        loads[-1].start()
    lane = {"y": 1 - lax.axis_index("y")} if extra else None
    if extra:
        spot = copy_places()
        for j, k in enumerate("HO"):
            loads.append(
                pltpu.make_async_copy(f_ref.at[spot[k]], lane_mine.at[j], local.at[4 + j])
            )
            loads[-1].start()
    greet([core, cross, side] + ([lane] if extra else []))
    out = Sender(send, recv)
    lanes = []
    if extra:
        lanes = [out.go(f_ref.at[spot[k]], lane_in.at[j], lane) for j, k in enumerate("DY")]
    swaps = [out.go(p_ref.at[twin[k]], twin_in.at[i], core) for i, k in enumerate("DXLO")]

    def join(i):
        loads[i].wait()
        swaps[i].wait_recv()
        add_into(mine.at[i], twin_in.at[i])

    join(0)
    bent_cross = out.go(mine.at[0].at[top], bent_in.at[0], cross)
    bent_side = out.go(mine.at[0].at[low], bent_in.at[1], side)
    join(1)
    cross_top = out.go(mine.at[1].at[top], cross_in.at[top], cross)
    join(2)
    side_low = out.go(mine.at[2].at[low], side_in.at[low], side)
    bent_cross.wait_recv()
    add_into(mine.at[2, top], bent_in.at[0])
    side_top = out.go(mine.at[2].at[top], side_in.at[top], side)
    bent_side.wait_recv()
    add_into(mine.at[1, low], bent_in.at[1])
    cross_low = out.go(mine.at[1].at[low], cross_in.at[low], cross)
    loads[3].wait()
    swaps[3].wait_recv()
    cross_top.wait_recv()
    side_low.wait_recv()
    add_to(o_ref.at[top], mine.at[3, top], twin_in.at[3, top], cross_in.at[top])
    add_to(o_ref.at[low], mine.at[3, low], twin_in.at[3, low], side_in.at[low])
    side_top.wait_recv()
    cross_low.wait_recv()
    add_into(o_ref.at[top], side_in.at[top])
    add_into(o_ref.at[low], cross_in.at[low])
    for j, copy in enumerate(lanes):
        loads[4 + j].wait()
        copy.wait_recv()
        add_to(sum_ref.at[j], lane_mine.at[j], lane_in.at[j])
    out.finish()


def team_scatter(partial_sum, lane_sum=None):
    rows, width = partial_sum.shape[0] // 8, partial_sum.shape[1]
    scratch = [
        pltpu.VMEM((4, rows, width), BF16),
        pltpu.VMEM((4, rows, width), BF16),
        pltpu.VMEM((rows, width), BF16),
        pltpu.VMEM((rows, width), BF16),
        pltpu.VMEM((2, rows // 2, width), BF16),
    ]
    total = jax.ShapeDtypeStruct((rows, width), F32)
    blocks = partial_sum.reshape(8, rows, width)
    if lane_sum is None:
        return remote_call(
            partial(team_scatter_kernel, False),
            total,
            10,
            1,
            [pltpu.SemaphoreType.DMA((4,)), *scratch],
            40 * 2**20,
            pltpu.VMEM,
        )(blocks)
    pair = (2, *lane_sum.shape[1:])
    return remote_call(
        partial(team_scatter_kernel, True),
        (total, jax.ShapeDtypeStruct(pair, BF16)),
        12,
        5,
        [pltpu.SemaphoreType.DMA((6,)), *scratch, pltpu.VMEM(pair, BF16), pltpu.VMEM(pair, BF16)],
        48 * 2**20,
        [pltpu.VMEM] * 2,
        2,
    )(blocks, lane_sum)


def team_peers():
    xc, l = lax.axis_index("xc"), lax.axis_index("l")
    peers = []
    for i in range(1, 8):
        far, side = lax.rem(xc + i // 2, 4), lax.rem(l + i % 2, 2)
        peers.append(((far, side), {"xc": far, "l": side}))
    return (xc, l), peers


def full_places():
    y, xc = lax.axis_index("y"), lax.axis_index("xc")
    h, l = lax.axis_index("h"), lax.axis_index("l")
    core = lax.rem(xc, 2)

    def rank(plane, depth, twin=False):
        b = xc + 1 - 2 * core if twin else xc
        b = lax.rem(b + 2, 4) if plane in "XD" else b
        a = 1 - y if plane in "YD" else y
        u = 1 - h if depth in ("H", "HL") else h
        v = 1 - l if depth in ("L", "HL") else l
        return ((a * 4 + b) * 2 + u) * 2 + v

    peers = {
        "C": {"xc": xc + 1 - 2 * core},
        "X": {"xc": lax.rem(xc + 2, 4)},
        "Y": {"y": 1 - y},
        "H": {"h": 1 - h},
        "L": {"l": 1 - l},
    }
    return rank, peers


DEPTHS = ("O", "L", "H", "HL")


def copy_places():
    y, h = lax.axis_index("y"), lax.axis_index("h")
    return {
        "O": y * 2 + h,
        "Y": (1 - y) * 2 + h,
        "H": y * 2 + 1 - h,
        "D": (1 - y) * 2 + 1 - h,
    }


def weights_in_kernel(
    x_ref, gate_in, up_in, down_ref, o_ref, gates_ref, ups_ref, far_ref, send, recv, local, split,
    gate_ref, up_ref,
):
    rank, peers = full_places()
    me, team = team_peers()
    y, h = lax.axis_index("y"), lax.axis_index("h")

    def at(plane, depth):
        return o_ref.at[rank(plane, depth)]

    pieces = []
    for source, target in ((gate_in, gate_ref), (up_in, up_ref)):
        width = source.shape[1] // 32
        for r in range(8):
            for c in range(4):
                begin = ((c // 2 * 4 + r // 2) * 2 + c % 2) * 2 + r % 2
                pieces.append(
                    pltpu.make_async_copy(
                        source.at[:, pl.ds(begin * width, width)],
                        target.at[r // 2, r % 2, :, pl.ds(c * width, width)],
                        split.at[len(pieces)],
                    )
                )
    for piece in pieces:
        piece.start()
    keeps = [
        pltpu.make_async_copy(x_ref, at("O", "O"), local.at[0]),
        pltpu.make_async_copy(gate_ref.at[me], gates_ref.at[y, me[0], h, me[1]], local.at[1]),
        pltpu.make_async_copy(up_ref.at[me], ups_ref.at[y, me[0], h, me[1]], local.at[2]),
    ]
    keeps[0].start()
    greet([peer for _, peer in team] + [peers["Y"], peers["H"]])
    out = Sender(send, recv)
    swaps, twins = [], []
    to_h = out.go(x_ref, at("O", "O"), peers["H"])
    to_l = out.go(x_ref, at("O", "O"), peers["L"])
    for piece in pieces:
        piece.wait()
    keeps[1].start()
    keeps[2].start()
    for place, peer in team:
        swaps.append(out.go(gate_ref.at[place], gates_ref.at[y, me[0], h, me[1]], peer))
        swaps.append(out.go(up_ref.at[place], ups_ref.at[y, me[0], h, me[1]], peer))
    direct, bent = {}, {}

    def begin(depth):
        source = x_ref if depth == "O" else at("O", depth)
        target = at("O", depth)
        to_y = out.go(source, target, peers["Y"])
        to_x = out.go(source, target, peers["X"])
        twins.append(out.go(source, target, peers["C"]))
        direct[depth] = (to_y, to_x)

    def bend(depth):
        to_y, to_x = direct[depth]
        to_y.wait_recv()
        bent[depth] = out.go(at("Y", depth), at("Y", depth), peers["X"])
        twins.append(out.go(at("Y", depth), at("Y", depth), peers["C"]))
        to_x.wait_recv()
        twins.append(out.go(at("X", depth), at("X", depth), peers["C"]))

    def close(depth):
        bent[depth].wait_recv()
        twins.append(out.go(at("D", depth), at("D", depth), peers["C"]))

    blocks = {"gate": gates_ref, "up": ups_ref}
    flats, arrivals = {}, []

    def spread(name):
        mine = blocks[name].at[y, :, h]
        flats[name] = out.go(mine, mine, peers["H"])
        arrivals.append(out.go(mine, mine, peers["Y"]))

    def corner(name):
        flats[name].wait_recv()
        piece = blocks[name].at[y, :, 1 - h]
        arrivals.append(out.go(piece, piece, peers["Y"]))

    begin("O")
    for swap in swaps:
        swap.wait_recv()
    keeps[1].wait()
    keeps[2].wait()
    spread("gate")
    to_h.wait_recv()
    to_hl = out.go(at("O", "H"), at("O", "H"), peers["L"])
    to_l.wait_recv()
    begin("L")
    begin("H")
    bend("O")
    spread("up")
    to_hl.wait_recv()
    begin("HL")
    bend("L")
    corner("gate")
    arrivals.append(out.go(down_ref, far_ref, peers["H"]))
    bend("H")
    close("O")
    close("L")
    bend("HL")
    corner("up")
    close("H")
    close("HL")
    for copy in twins + arrivals:
        copy.wait_recv()
    out.finish()
    keeps[0].wait()


def weights_in(columns, gate, up, down):
    rows, width = columns.shape
    depth, part = gate.shape[0], gate.shape[1] // 8
    if not small_grid():
        full = lax.all_gather(columns, AXES, axis=0, tiled=False)
        gates, ups = (
            rows_in_order(
                lax.all_gather(lax.all_to_all(b, TEAM, 0, 0), COPIES, axis=0, tiled=False)
            )
            for b in (column_blocks(gate), column_blocks(up))
        )
        far = None
    else:
        full, gates, ups, far = remote_call(
            weights_in_kernel,
            (
                jax.ShapeDtypeStruct((32, rows, width), BF16),
                jax.ShapeDtypeStruct((2, 4, 2, 2, depth, part), BF16),
                jax.ShapeDtypeStruct((2, 4, 2, 2, depth, part), BF16),
                jax.ShapeDtypeStruct(down.shape, BF16),
            ),
            14 + 3 + 28 + 7,
            3,
            [
                pltpu.SemaphoreType.DMA((3,)),
                pltpu.SemaphoreType.DMA((64,)),
                pltpu.VMEM((4, 2, depth, part), BF16),
                pltpu.VMEM((4, 2, depth, part), BF16),
            ],
            spaces=[pl.ANY] * 4,
            inputs=4,
        )(columns, gate, up, down)
    return full.reshape(-1, width), gates.reshape(-1, part), ups.reshape(-1, part), far


PLANES = ("D", "X", "Y", "O")
SUMS = ("HL", "L", "H", "O")


def grads_out_kernel(edges, *refs):
    n = len(edges)
    parts, (far_ref, near_ref, raw_ref) = refs[:n], refs[n : n + 3]
    o_ref, gate_ref, up_ref, send, recv, local = refs[n + 3 : n + 9]
    mine, twin_in, cross_in, lane_in, bent_in, depth_in = refs[n + 9 : n + 15]
    flat, flat_h, back_in = refs[n + 15 : n + 17], refs[n + 17 : n + 19], refs[n + 19 : n + 21]
    flat_far, flat_y = refs[n + 21], refs[n + 22 :]
    rank, peers = full_places()
    me, team = team_peers()
    y, h = lax.axis_index("y"), lax.axis_index("h")
    half = mine.shape[2] // 2
    top, low = pl.ds(0, half), pl.ds(half, half)
    loads, swaps, flights = {}, {}, {}
    count = 0

    def load(source, target):
        nonlocal count
        copy = pltpu.make_async_copy(source, target, local.at[count])
        count += 1
        copy.start()
        return copy

    for t, depth in enumerate(SUMS):
        for k, plane in enumerate(PLANES):
            place = rank(plane, depth)
            loads[t, k] = [
                load(part.at[place], mine.at[t, k, :, pl.ds(begin, part.shape[2])])
                for part, begin in zip(parts, edges)
            ]
    own_loads = [load(near_ref, flat[0]), load(raw_ref.at[y, :, h], flat[1])]
    far_load = load(raw_ref.at[y, :, 1 - h], flat_far)
    greet([peer for _, peer in team] + [peers["Y"], peers["H"]])
    out = Sender(send, recv)

    def swap(t):
        for k, plane in enumerate(PLANES):
            place = rank(plane, SUMS[t], True)
            swaps[t, k] = [
                out.go(
                    part.at[place], twin_in.at[t, k, :, pl.ds(begin, part.shape[2])], peers["C"]
                )
                for part, begin in zip(parts, edges)
            ]

    def join(t, k):
        for copy in loads[t, k]:
            copy.wait()
        for copy in swaps[t, k]:
            copy.wait_recv()
        add_into(mine.at[t, k], twin_in.at[t, k])

    def diagonal(t):
        flights[t] = [
            out.go(mine.at[t, 0, top], bent_in.at[t, top], peers["X"]),
            out.go(mine.at[t, 0, low], bent_in.at[t, low], peers["Y"]),
        ]

    def straight(t):
        flights[t].append(out.go(mine.at[t, 1, top], cross_in.at[t, top], peers["X"]))
        flights[t].append(out.go(mine.at[t, 2, low], lane_in.at[t, low], peers["Y"]))

    def bend(t):
        flights[t][0].wait_recv()
        add_into(mine.at[t, 2, top], bent_in.at[t, top])
        flights[t].append(out.go(mine.at[t, 2, top], lane_in.at[t, top], peers["Y"]))
        flights[t][1].wait_recv()
        add_into(mine.at[t, 1, low], bent_in.at[t, low])
        flights[t].append(out.go(mine.at[t, 1, low], cross_in.at[t, low], peers["X"]))

    def close(t):
        for copy in flights[t][2:]:
            copy.wait_recv()
        return (cross_in.at[t], lane_in.at[t])

    swap(0)
    h_side = [out.go(far_ref, flat_h[0], peers["H"])]
    y_side = [out.go(raw_ref.at[1 - y, :, 1 - h], flat_y[0], peers["Y"])]
    swap(1)
    swap(2)
    swap(3)
    for t in (0, 1):
        for k in (0, 1, 2):
            join(t, k)
        diagonal(t)
        straight(t)
    join(0, 3)
    join(1, 3)
    far_load.wait()
    y_side[0].wait_recv()
    add_into(flat_far, flat_y[0])
    h_side.append(out.go(flat_far, flat_h[1], peers["H"]))
    y_side.append(out.go(raw_ref.at[1 - y, :, h], flat_y[1], peers["Y"]))
    bend(0)
    for k in (0, 1, 2):
        join(2, k)
    diagonal(2)
    straight(2)
    bend(1)
    for k in (0, 1, 2):
        join(3, k)
    diagonal(3)
    straight(3)
    join(2, 3)
    join(3, 3)
    add_into(mine.at[0, 3], *close(0))
    to_hl = out.go(mine.at[0, 3], depth_in.at[0], peers["L"])
    bend(2)
    add_into(mine.at[1, 3], *close(1))
    to_l = out.go(mine.at[1, 3], depth_in.at[1], peers["L"])
    bend(3)
    ready = close(2)
    to_hl.wait_recv()
    add_into(mine.at[2, 3], *ready, depth_in.at[0])
    to_h = out.go(mine.at[2, 3], depth_in.at[2], peers["H"])
    returns = []
    for i in range(2):
        own_loads[i].wait()
        h_side[i].wait_recv()
        arrived = [flat_h[i]]
        if i == 1:
            y_side[1].wait_recv()
            arrived.append(flat_y[1])
        add_into(flat[i], *arrived)
        returns.append([load(flat[i].at[me], back_in[i].at[me])])
        for place, peer in team:
            returns[i].append(out.go(flat[i].at[place], back_in[i].at[me], peer))
    ready = close(3)
    to_l.wait_recv()
    add_to(o_ref, mine.at[3, 3], *ready, depth_in.at[1])
    to_h.wait_recv()
    add_into(o_ref, depth_in.at[2])
    for i, target in enumerate((gate_ref, up_ref)):
        returns[i][0].wait()
        for copy in returns[i][1:]:
            copy.wait_recv()
        width = target.shape[1] // 32
        for r in range(8):
            for c in range(4):
                begin = ((c // 2 * 4 + r // 2) * 2 + c % 2) * 2 + r % 2
                target[:, pl.ds(begin * width, width)] = back_in[i][
                    r // 2, r % 2, :, pl.ds(c * width, width)
                ].astype(F32)
    out.finish()


def grads_out(parts, gate, up):
    shares = lax.axis_size("y") * lax.axis_size("h") * 8
    rows = parts[0].shape[0] // shares
    blocks = [part.reshape(shares, rows, part.shape[1]) for part in parts]
    if not small_grid():
        block = jnp.concatenate(blocks, axis=2)
        total = lax.psum_scatter(block, AXES, scatter_dimension=0, tiled=False).astype(F32)
        up = lax.psum_scatter(rows_by_copy(up), COPIES, scatter_dimension=0, tiled=False)
        gate, up = (
            from_column_blocks(lax.all_to_all(value, TEAM, 0, 0)).astype(F32)
            for value in (gate, up)
        )
        return total, gate, up
    edges = [0]
    for part in parts:
        edges.append(edges[-1] + part.shape[1])
    width = edges.pop()
    flat = gate[0].shape
    return remote_call(
        partial(grads_out_kernel, tuple(edges)),
        (
            jax.ShapeDtypeStruct((rows, width), F32),
            jax.ShapeDtypeStruct((flat[2], 8 * flat[3]), F32),
            jax.ShapeDtypeStruct((flat[2], 8 * flat[3]), F32),
        ),
        16 * len(parts) + 24 + 3 + 4 + 14,
        4,
        [
            pltpu.SemaphoreType.DMA((16 * len(parts) + 3 + 2,)),
            pltpu.VMEM((4, 4, rows, width), BF16),
            pltpu.VMEM((4, 4, rows, width), BF16),
            pltpu.VMEM((4, rows, width), BF16),
            pltpu.VMEM((4, rows, width), BF16),
            pltpu.VMEM((4, rows, width), BF16),
            pltpu.VMEM((3, rows, width), BF16),
            *[pltpu.VMEM(flat, BF16)] * 9,
        ],
        56 * 2**20,
        [pltpu.VMEM] * 3,
        len(parts) + 3,
    )(*blocks, *gate, up)


def small_grid():
    return lax.axis_size("y") == 2 and lax.axis_size("h") == 2


def lane_sums(value):
    if not small_grid():
        return lax.psum_scatter(rows_by_copy(value), COPIES, scatter_dimension=0, tiled=False)
    y, h = lax.axis_index("y"), lax.axis_index("h")

    def piece(a, b):
        plane = lax.dynamic_index_in_dim(value, a, axis=0, keepdims=False)
        return lax.dynamic_index_in_dim(plane, b, axis=1, keepdims=False)

    sent = jnp.stack([piece(1 - y, 1 - h), piece(1 - y, h)])
    arrived = lax.ppermute(sent, "y", [(0, 1), (1, 0)])
    return [
        plus(piece(y, 1 - h), arrived[0]).astype(BF16),
        plus(piece(y, h), arrived[1]).astype(BF16),
    ]


def shift(block, distance):
    pieces = lax.axis_size("h") * lax.axis_size("l")
    route = [(i, i + distance) for i in range(pieces) if 0 <= i + distance < pieces]
    return lax.ppermute(block, ("h", "l"), route)


def column_blocks(weight):
    ys, hs = lax.axis_size("y"), lax.axis_size("h")
    depth, width = weight.shape
    split = weight.reshape(depth, ys, 4, hs, 2, width // (ys * hs * 8))
    return split.transpose(2, 4, 0, 1, 3, 5).reshape(8, depth, width // 8)


def from_column_blocks(blocks):
    ys, hs = lax.axis_size("y"), lax.axis_size("h")
    depth, width = blocks.shape[1:]
    split = blocks.reshape(4, 2, depth, ys, hs, width // (ys * hs)).transpose(2, 3, 0, 4, 1, 5)
    return split.reshape(depth, 8 * width)


def rows_in_order(value):
    ys, hs = lax.axis_size("y"), lax.axis_size("h")
    split = value.reshape(ys, hs, 4, 2, *value.shape[2:])
    return split.transpose(0, 2, 1, 3, 4, 5)


def rows_by_copy(value):
    ys, hs = value.shape[0], value.shape[2]
    split = value.transpose(0, 2, 1, 3, 4, 5)
    return split.reshape(ys * hs, 8, *value.shape[4:])


def layer(*args):
    (
        hidden_in,
        layer_input,
        seq_lengths,
        cotangent,
        query_weight,
        key_matrix,
        value_matrix,
        output_weight,
        laurel_left,
        laurel_right,
        input_gate,
        input_projection,
        gate_weight,
        up_weight,
        down_weight,
        norm_gains,
        head_gains,
    ) = args
    rows, width = hidden_in.shape
    hops = max(1, WINDOW // rows)
    groups = QUERY_HEADS // KEY_VALUE_HEADS
    piece = lax.axis_index(("h", "l"))
    places = piece * rows + jnp.arange(rows, dtype=jnp.int32)
    key_places = (piece - hops) * rows + jnp.arange((hops + 1) * rows, dtype=jnp.int32)
    live = (places < seq_lengths[0]).astype(F32)[:, None]

    head_width = QUERY_HEADS * HEAD_SIZE
    kv_width = KEY_VALUE_HEADS * HEAD_SIZE
    rank = laurel_left.shape[1]
    side = layer_input.shape[1]
    depth, head_part = query_weight.shape[0], head_gains.shape[1]
    columns = (
        query_weight,
        key_matrix,
        value_matrix,
        output_weight,
        input_gate,
        input_projection.T,
        laurel_left,
        laurel_right.T,
        norm_gains.T,
        jnp.pad(head_gains.T, ((0, depth - head_part), (0, 0))),
    )
    edges = [0]
    for column in columns:
        edges.append(edges[-1] + column.shape[1])
    full_width = -(-edges[-1] // 128) * 128
    local_columns = jnp.pad(
        jnp.concatenate(columns, axis=1), ((0, 0), (0, full_width - edges[-1]))
    )
    full, gate_cols, up_cols, far_down = weights_in(
        local_columns, gate_weight, up_weight, down_weight
    )
    first = full[:, : edges[3]]
    output_all, side_gate_all, projection_all, left_all, right_all = (
        full[:, edges[i] : edges[i + 1]] for i in range(3, 8)
    )
    gains = full[:, edges[8] : edges[9]].T.astype(F32)
    head_gain = (
        full[:, edges[9] : edges[10]].reshape(-1, depth, 2)[:, :head_part].reshape(-1, 2).T
    ).astype(F32)

    hidden = hidden_in.astype(F32)
    side_input = layer_input.astype(F32)
    cosine, sine = rope_tables(places)

    hidden_inv = inverse_rms(hidden)
    normed = hidden * hidden_inv * gains[0]
    normed_low = normed.astype(BF16)
    raw = dot(normed_low, first)
    left_low = dot(normed_low, left_all).astype(BF16)
    query_low, pair_low = heads(raw, cosine, sine, head_gain)
    pairs = [pair_low]
    for _ in range(hops):
        pairs.insert(0, shift(pairs[0], 1))
    window = jnp.concatenate(pairs, axis=1).reshape(2, -1, KEY_VALUE_HEADS, HEAD_SIZE)
    grouped = query_low.reshape(rows, KEY_VALUE_HEADS, groups, HEAD_SIZE)
    scores = jnp.einsum("qkgd,tkd->kgqt", grouped, window[0], preferred_element_type=F32)
    allowed = (
        (key_places[None, :] <= places[:, None])
        & (places[:, None] - key_places[None, :] < WINDOW)
        & (key_places[None, :] >= 0)
    )
    scores = jnp.where(allowed, scores, MASKED)
    weights = jnp.exp(scores - jnp.max(scores, axis=-1, keepdims=True))
    probs = weights / jnp.sum(weights, axis=-1, keepdims=True)
    probs_low = probs.astype(BF16)
    mixed = (
        jnp.einsum("kgqt,tkd->qkgd", probs_low, window[1], preferred_element_type=F32)
        .reshape(rows, head_width)
        .astype(BF16)
    )
    attention_raw = dot(mixed, output_all)
    attention_inv = inverse_rms(attention_raw)
    right_raw = dot(left_low, right_all, 1, 1)
    right_inv = inverse_rms(right_raw)
    merged = (
        hidden
        + attention_raw * attention_inv * gains[1]
        + normed
        + right_raw * right_inv * gains[2]
    ) * HALF_ROOT
    merged_inv = inverse_rms(merged)
    expand_low = (merged * merged_inv * gains[3]).astype(BF16)

    expand_all, down_rows = team_gather_with(expand_low, down_weight, far_down)
    gate_raw = dot(expand_all, gate_cols)
    up_raw = dot(expand_all, up_cols)
    act_low = (gelu(gate_raw) * up_raw).astype(BF16)
    reduced_raw = team_scatter(dot(act_low, down_rows).astype(BF16))
    reduced_inv = inverse_rms(reduced_raw)
    after_feed = merged + reduced_raw * reduced_inv * gains[4]
    after_low = after_feed.astype(BF16)
    side_raw = dot(after_low, side_gate_all)
    side_low = (gelu(side_raw) * side_input).astype(BF16)
    side_out = dot(side_low, projection_all, 1, 1)
    side_inv = inverse_rms(side_out)
    block_out = (after_feed + side_out * side_inv * gains[5]) * live

    upstream = cotangent.astype(F32) * live
    grad_side, gain_five = rms_back(side_out, side_inv, gains[5], upstream)
    grad_side_low = grad_side.astype(BF16)
    grad_side_raw = (
        dot(grad_side_low, projection_all) * side_input * gelu_slope(side_raw)
    ).astype(BF16)
    grad_after = upstream + dot(grad_side_raw, side_gate_all, 1, 1)
    grad_reduced, gain_four = rms_back(reduced_raw, reduced_inv, gains[4], grad_after)
    grad_reduced_low = grad_reduced.astype(BF16)

    grad_reduced_all = team_gather(grad_reduced_low)
    grad_product = dot(grad_reduced_all, down_rows, 1, 1)
    grad_gate_low = (grad_product * up_raw * gelu_slope(gate_raw)).astype(BF16)
    grad_up_low = (grad_product * gelu(gate_raw)).astype(BF16)
    part_down = dot(act_low, grad_reduced_all, 0, 0).astype(BF16)
    part_low = (dot(grad_gate_low, gate_cols, 1, 1) + dot(grad_up_low, up_cols, 1, 1)).astype(BF16)
    part_gate = dot(expand_all, grad_gate_low, 0, 0).astype(BF16)
    part_up = dot(expand_all, grad_up_low, 0, 0).astype(BF16)
    down_blocks = part_down.reshape(-1, *down_weight.shape)
    part_gate, part_up = (
        value.reshape(lax.axis_size("y"), 4, -1, 2, depth, value.shape[1])
        for value in (part_gate, part_up)
    )
    part_low, part_gate, part_up = lax.optimization_barrier((part_low, part_gate, part_up))
    if small_grid():
        part, down_sums = team_scatter(part_low, down_blocks)
    else:
        part = team_scatter(part_low)
        down_sums = None
    sums_gate = lane_sums(part_gate)
    grad_merged, gain_three = rms_back(merged, merged_inv, gains[3], part)
    grad_sum = (grad_after + grad_merged) * HALF_ROOT
    grad_right, gain_two = rms_back(right_raw, right_inv, gains[2], grad_sum)
    grad_right_low = grad_right.astype(BF16)
    grad_left_low = dot(grad_right_low, right_all).astype(BF16)
    grad_attention, gain_one = rms_back(attention_raw, attention_inv, gains[1], grad_sum)
    grad_attention_low = grad_attention.astype(BF16)
    grad_mixed = (
        dot(grad_attention_low, output_all, 1, 1)
        .astype(BF16)
        .reshape(rows, KEY_VALUE_HEADS, groups, HEAD_SIZE)
    )
    grad_probs = jnp.einsum("qkgd,tkd->kgqt", grad_mixed, window[1], preferred_element_type=F32)
    inner = jnp.sum(probs * grad_probs, axis=-1, keepdims=True)
    grad_scores = (probs * (grad_probs - inner)).astype(BF16)
    grad_query_rot = jnp.einsum(
        "kgqt,tkd->qkgd", grad_scores, window[0], preferred_element_type=F32
    ).reshape(rows, head_width)
    grad_window = jnp.stack(
        [
            jnp.einsum("kgqt,qkgd->tkd", grad_scores, grouped, preferred_element_type=F32),
            jnp.einsum("kgqt,qkgd->tkd", probs_low, grad_mixed, preferred_element_type=F32),
        ]
    ).reshape(2, -1, kv_width)
    carried = grad_window[:, :rows]
    for hop in range(1, hops + 1):
        carried = shift(carried.astype(BF16), -1).astype(F32)
        carried = carried + grad_window[:, hop * rows : (hop + 1) * rows]
    if down_sums is None:
        grad_down = lax.psum_scatter(down_blocks, COPIES, scatter_dimension=0).astype(F32)
    else:
        carried, leaving = lax.optimization_barrier((carried, down_sums[0]))
        grad_down = plus(down_sums[1], lax.ppermute(leaving, "h", [(0, 1), (1, 0)]))
    grad_raw, head_grads = heads_back(raw, grad_query_rot, carried, cosine, sine, head_gain)
    grad_normed = grad_sum + dot(grad_raw, first, 1, 1) + dot(grad_left_low, left_all, 1, 1)
    grad_input, gain_zero = rms_back(hidden, hidden_inv, gains[0], grad_normed)
    grad_hidden = grad_sum + grad_input

    gain_grads = jnp.stack(
        [
            jnp.sum(g, axis=0)
            for g in (gain_zero, gain_one, gain_two, gain_three, gain_four, gain_five)
        ]
    )
    head_column = jnp.pad(
        head_grads.T.reshape(-1, head_part, 2), ((0, 0), (0, depth - head_part), (0, 0))
    ).reshape(-1, 2)
    tail = full_width - edges[6]
    small = (
        dot(normed_low, jnp.pad(grad_left_low, ((0, 0), (0, tail - rank))), 0, 0)
        + dot(grad_right_low, jnp.pad(left_low, ((0, 0), (rank, tail - 2 * rank))), 0, 0)
        + jnp.pad(gain_grads.T, ((0, 0), (2 * rank, tail - 2 * rank - 6)))
        + jnp.pad(head_column, ((0, 0), (2 * rank + 6, tail - 2 * rank - 8)))
    )
    weight_grads = (
        dot(normed_low, grad_raw, 0, 0).astype(BF16),
        dot(mixed, grad_attention_low, 0, 0).astype(BF16),
        dot(after_low, grad_side_raw, 0, 0).astype(BF16),
        dot(grad_side_low, side_low, 0, 0).astype(BF16),
        small.astype(BF16),
    )
    summed, grad_gate, grad_up = grads_out(weight_grads, sums_gate, part_up)
    (
        d_query,
        d_key,
        d_value,
        d_output,
        d_side_gate,
        d_projection,
        d_left,
        d_right,
        d_gains,
        d_heads,
    ) = (summed[:, edges[i] : edges[i + 1]] for i in range(10))
    d_right, d_projection, d_gains = d_right.T, d_projection.T, d_gains.T
    d_heads = d_heads[:head_part].T
    return (
        block_out,
        grad_hidden,
        d_query,
        d_key,
        d_value,
        d_output,
        d_left,
        d_right,
        d_side_gate,
        d_projection,
        grad_gate,
        grad_up,
        grad_down,
        d_gains,
        d_heads,
    )


def solution(mesh):
    dp, seq = mesh.shape["dp"], mesh.shape["seq"]
    grid = Mesh(mesh.devices.reshape(dp // 4, 4, seq // 2, 2), AXES)
    row, column = P(AXES, None), P(None, AXES)
    return jax.shard_map(
        layer,
        mesh=grid,
        in_specs=(row, row, P(("y", "xc")))
        + (row,) * 6
        + (column, row, column)
        + (row,) * 3
        + (column,) * 2,
        out_specs=(row,) * 7 + (column, row, column) + (row,) * 3 + (column,) * 2,
        check_vma=False,
    )
```

```python
from functools import partial

import jax
import jax.numpy as jnp
from jax import lax
from jax.experimental import pallas as pl
from jax.experimental.pallas import tpu as pltpu
from jax.sharding import Mesh, PartitionSpec as P

QUERY_HEADS = 8
KEY_VALUE_HEADS = 2
HEAD_SIZE = 256
WINDOW = 512
EPSILON = 1e-06
ROPE_BASE = 10000.0
HALF_ROOT = 0.7071067811865476
MASKED = -1e30
GELU_SCALE = 0.7978845608028654
GELU_CUBE = 0.044715
F32 = jnp.float32
BF16 = jnp.bfloat16


def dot(left, right, left_dim=1, right_dim=0):
    return lax.dot_general(
        left, right, (((left_dim,), (right_dim,)), ((), ())), preferred_element_type=F32
    )


def inverse_rms(value):
    return lax.rsqrt(jnp.mean(value * value, axis=-1, keepdims=True) + EPSILON)


def rms_back(value, inverse, gain, grad):
    scaled = grad * gain
    inner = jnp.mean(scaled * value, axis=-1, keepdims=True)
    unit = value * inverse
    return inverse * (scaled - unit * (inverse * inner)), grad * unit


def rope_tables(positions):
    half = HEAD_SIZE // 2
    rate = ROPE_BASE ** (-jnp.arange(half, dtype=F32) * 2.0 / HEAD_SIZE)
    angle = positions.astype(F32)[:, None] * rate[None, :]
    return jnp.cos(angle), jnp.sin(angle)


def head_columns(head):
    return pl.ds(head * HEAD_SIZE, HEAD_SIZE)


def heads_kernel(raw_ref, cos_ref, sin_ref, gain_ref, query_ref, pair_ref):
    half = HEAD_SIZE // 2
    cosine, sine = cos_ref[...], sin_ref[...]
    for head in range(QUERY_HEADS + 2 * KEY_VALUE_HEADS):
        value = raw_ref[:, head_columns(head)]
        value = value * inverse_rms(value)
        slot, kind = head - QUERY_HEADS, (head - QUERY_HEADS) // KEY_VALUE_HEADS
        if kind == 1:
            pair_ref[1, :, head_columns(slot - KEY_VALUE_HEADS)] = value.astype(BF16)
            continue
        value = value * gain_ref[pl.ds(0 if slot < 0 else 1, 1), :]
        first, second = value[:, :half], value[:, half:]
        turned = jnp.concatenate(
            [first * cosine - second * sine, second * cosine + first * sine], axis=1
        ).astype(BF16)
        if slot < 0:
            query_ref[:, head_columns(head)] = turned
        else:
            pair_ref[0, :, head_columns(slot)] = turned


def heads_back_kernel(
    raw_ref, query_ref, pair_ref, cos_ref, sin_ref, gain_ref, out_ref, gain_grad_ref
):
    half = HEAD_SIZE // 2
    cosine, sine = cos_ref[...], sin_ref[...]

    @pl.when(pl.program_id(0) == 0)
    def _():
        gain_grad_ref[...] = jnp.zeros_like(gain_grad_ref)

    for head in range(QUERY_HEADS + 2 * KEY_VALUE_HEADS):
        value = raw_ref[:, head_columns(head)]
        slot, kind = head - QUERY_HEADS, (head - QUERY_HEADS) // KEY_VALUE_HEADS
        if slot < 0:
            grad = query_ref[:, head_columns(head)]
        else:
            grad = pair_ref[kind, :, head_columns(slot - kind * KEY_VALUE_HEADS)]
        gain = 1.0
        if kind < 1:
            row = pl.ds(0 if slot < 0 else 1, 1)
            gain = gain_ref[row, :]
            first, second = grad[:, :half], grad[:, half:]
            grad = jnp.concatenate(
                [first * cosine + second * sine, second * cosine - first * sine], axis=1
            )
        result, gain_part = rms_back(value, inverse_rms(value), gain, grad)
        out_ref[:, head_columns(head)] = result.astype(BF16)
        if kind < 1:
            gain_grad_ref[row, :] += jnp.sum(gain_part, axis=0, keepdims=True)


def strip_spec(rows, *shape):
    front = len(shape) - 2
    return pl.BlockSpec(
        (*shape[:front], rows, shape[-1]), lambda i: (*(0,) * front, i, 0)
    )


def heads(raw, cosine, sine, gain):
    rows, width = raw.shape
    strip = min(64, rows)
    query_width, pair_width = QUERY_HEADS * HEAD_SIZE, KEY_VALUE_HEADS * HEAD_SIZE
    return pl.pallas_call(
        heads_kernel,
        out_shape=(
            jax.ShapeDtypeStruct((rows, query_width), BF16),
            jax.ShapeDtypeStruct((2, rows, pair_width), BF16),
        ),
        grid=(rows // strip,),
        in_specs=[
            strip_spec(strip, rows, width),
            strip_spec(strip, *cosine.shape),
            strip_spec(strip, *sine.shape),
            pl.BlockSpec(gain.shape, lambda i: (0, 0)),
        ],
        out_specs=(
            strip_spec(strip, rows, query_width),
            strip_spec(strip, 2, rows, pair_width),
        ),
    )(raw, cosine, sine, gain)


def heads_back(raw, query_grad, pair_grad, cosine, sine, gain):
    rows, width = raw.shape
    strip = min(64, rows)
    return pl.pallas_call(
        heads_back_kernel,
        out_shape=(
            jax.ShapeDtypeStruct((rows, width), BF16),
            jax.ShapeDtypeStruct(gain.shape, F32),
        ),
        grid=(rows // strip,),
        in_specs=[
            strip_spec(strip, rows, width),
            strip_spec(strip, *query_grad.shape),
            strip_spec(strip, *pair_grad.shape),
            strip_spec(strip, *cosine.shape),
            strip_spec(strip, *sine.shape),
            pl.BlockSpec(gain.shape, lambda i: (0, 0)),
        ],
        out_specs=(
            strip_spec(strip, rows, width),
            pl.BlockSpec(gain.shape, lambda i: (0, 0)),
        ),
    )(raw, query_grad, pair_grad, cosine, sine, gain)


def gelu_tanh(value):
    return jnp.tanh(GELU_SCALE * (value + GELU_CUBE * value * value * value))


def gelu(value):
    return 0.5 * value * (1.0 + gelu_tanh(value))


def gelu_slope(value):
    t = gelu_tanh(value)
    inner = GELU_SCALE * (1.0 + 3.0 * GELU_CUBE * value * value)
    return 0.5 * (1.0 + t) + 0.5 * value * (1.0 - t * t) * inner


AXES = ("y", "xc", "h", "l")
TEAM = ("xc", "l")
COPIES = ("y", "h")


class Sender:
    def __init__(self, send, recv):
        self.send, self.recv, self.count, self.started = send, recv, 0, []

    def go(self, source, target, peer):
        i = self.count
        self.count += 1
        copy = pltpu.make_async_remote_copy(
            src_ref=source,
            dst_ref=target,
            send_sem=self.send.at[i],
            recv_sem=self.recv.at[i],
            device_id=peer,
            device_id_type=pl.DeviceIdType.MESH,
        )
        copy.start()
        self.started.append(copy)
        return copy

    def finish(self):
        for copy in self.started:
            copy.wait_send()


def greet(peers):
    barrier = pltpu.get_barrier_semaphore()
    for peer in peers:
        pl.semaphore_signal(barrier, inc=1, device_id=peer, device_id_type=pl.DeviceIdType.MESH)
    pl.semaphore_wait(barrier, len(peers))


def plus(*parts):
    total = parts[0].astype(F32)
    for part in parts[1:]:
        total = total + part.astype(F32)
    return total


def strips(ref):
    if len(ref.shape) == 4:
        return [ref.at[i, j] for i in range(ref.shape[0]) for j in range(ref.shape[1])]
    step = min(16, ref.shape[0])
    return [ref.at[pl.ds(i, step)] for i in range(0, ref.shape[0], step)]


def add_into(target, *sources):
    for strip, *others in zip(strips(target), *[strips(source) for source in sources]):
        total = strip[...]
        if len(others) > 1:
            total = plus(total, *[other[...] for other in others])
        else:
            total = total + others[0][...].astype(total.dtype)
        strip[...] = total.astype(target.dtype)


def add_to(target, *sources):
    for strip, *others in zip(strips(target), *[strips(source) for source in sources]):
        strip[...] = plus(*[other[...] for other in others]).astype(target.dtype)


def remote_call(kernel, out, copies, identity, scratch=(), vmem=None, spaces=pl.ANY, inputs=1):
    places = [pl.BlockSpec(memory_space=space) for space in spaces] if isinstance(
        spaces, (list, tuple)
    ) else pl.BlockSpec(memory_space=spaces)
    return pl.pallas_call(
        kernel,
        out_shape=out,
        in_specs=[pl.BlockSpec(memory_space=pl.ANY)] * inputs,
        out_specs=places,
        scratch_shapes=[
            pltpu.SemaphoreType.DMA((copies,)),
            pltpu.SemaphoreType.DMA((copies,)),
            *scratch,
        ],
        compiler_params=pltpu.CompilerParams(
            collective_id=identity, has_side_effects=True, vmem_limit_bytes=vmem
        ),
    )


def team_places():
    xc, l = lax.axis_index("xc"), lax.axis_index("l")
    core = lax.rem(xc, 2)
    other = xc + 1 - 2 * core
    cross, side = lax.rem(xc + 2, 4), 1 - l
    own = {"O": xc * 2 + l, "X": cross * 2 + l, "L": xc * 2 + side, "D": cross * 2 + side}
    far = lax.rem(other + 2, 4)
    twin = {"O": other * 2 + l, "X": far * 2 + l, "L": other * 2 + side, "D": far * 2 + side}
    return own, twin, {"xc": other}, {"xc": cross}, {"l": side}


def team_gather_kernel(extra, *refs):
    if extra:
        x_ref, near_ref, far_ref, o_ref, blocks_ref, send, recv, local = refs
    else:
        x_ref, o_ref, send, recv, local = refs
    own, _, core, cross, side = team_places()
    half = x_ref.shape[0] // 2
    top, low = pl.ds(0, half), pl.ds(half, half)
    keeps = [pltpu.make_async_copy(x_ref, o_ref.at[own["O"]], local.at[0])]
    lane = {"y": 1 - lax.axis_index("y")} if extra else None
    if extra:
        spot = copy_places()
        near, far = blocks_ref.at[spot["O"]], blocks_ref.at[spot["H"]]
        keeps.append(pltpu.make_async_copy(near_ref, near, local.at[1]))
        keeps.append(pltpu.make_async_copy(far_ref, far, local.at[2]))
    for keep in keeps:
        keep.start()
    greet([core, cross, side] + ([lane] if extra else []))
    out = Sender(send, recv)
    twins = [out.go(near_ref, near, lane), out.go(far_ref, far, lane)] if extra else []
    mine, from_side, from_cross = o_ref.at[own["O"]], o_ref.at[own["L"]], o_ref.at[own["X"]]
    diagonal = o_ref.at[own["D"]]
    side_top = out.go(x_ref.at[top], mine.at[top], side)
    cross_low = out.go(x_ref.at[low], mine.at[low], cross)
    side_low = out.go(x_ref.at[low], mine.at[low], side)
    cross_top = out.go(x_ref.at[top], mine.at[top], cross)
    twins.append(out.go(x_ref, mine, core))
    side_top.wait_recv()
    diagonal_top = out.go(from_side.at[top], from_side.at[top], cross)
    twins.append(out.go(from_side.at[top], from_side.at[top], core))
    cross_low.wait_recv()
    diagonal_low = out.go(from_cross.at[low], from_cross.at[low], side)
    twins.append(out.go(from_cross.at[low], from_cross.at[low], core))
    side_low.wait_recv()
    twins.append(out.go(from_side.at[low], from_side.at[low], core))
    cross_top.wait_recv()
    twins.append(out.go(from_cross.at[top], from_cross.at[top], core))
    diagonal_top.wait_recv()
    twins.append(out.go(diagonal.at[top], diagonal.at[top], core))
    diagonal_low.wait_recv()
    twins.append(out.go(diagonal.at[low], diagonal.at[low], core))
    for copy in twins:
        copy.wait_recv()
    out.finish()
    for keep in keeps:
        keep.wait()


def team_gather(block):
    rows, width = block.shape
    gathered = remote_call(
        partial(team_gather_kernel, False),
        jax.ShapeDtypeStruct((8, rows, width), block.dtype),
        13,
        0,
        [pltpu.SemaphoreType.DMA((1,))],
        40 * 2**20,
        pltpu.VMEM,
    )(block)
    return gathered.reshape(8 * rows, width)


def team_gather_with(block, near, far):
    rows, width = block.shape
    if far is None:
        return team_gather(block), lax.all_gather(near, COPIES, axis=0, tiled=True)
    gathered, blocks = remote_call(
        partial(team_gather_kernel, True),
        (
            jax.ShapeDtypeStruct((8, rows, width), block.dtype),
            jax.ShapeDtypeStruct((4, *near.shape), near.dtype),
        ),
        15,
        2,
        [pltpu.SemaphoreType.DMA((3,))],
        vmem=40 * 2**20,
        spaces=[pltpu.VMEM] * 2,
        inputs=3,
    )(block, near, far)
    return gathered.reshape(8 * rows, width), blocks.reshape(-1, near.shape[1])


def team_scatter_kernel(extra, *refs):
    if extra:
        p_ref, f_ref, o_ref, sum_ref, send, recv, local = refs[:7]
        lane_mine, lane_in = refs[12:]
    else:
        p_ref, o_ref, send, recv, local = refs[:5]
    mine, twin_in, cross_in, side_in, bent_in = refs[7:12] if extra else refs[5:]
    own, twin, core, cross, side = team_places()
    half = p_ref.shape[1] // 2
    top, low = pl.ds(0, half), pl.ds(half, half)
    loads = []
    for i, k in enumerate("DXLO"):
        loads.append(pltpu.make_async_copy(p_ref.at[own[k]], mine.at[i], local.at[i]))
        loads[-1].start()
    lane = {"y": 1 - lax.axis_index("y")} if extra else None
    if extra:
        spot = copy_places()
        for j, k in enumerate("HO"):
            loads.append(
                pltpu.make_async_copy(f_ref.at[spot[k]], lane_mine.at[j], local.at[4 + j])
            )
            loads[-1].start()
    greet([core, cross, side] + ([lane] if extra else []))
    out = Sender(send, recv)
    lanes = []
    if extra:
        lanes = [out.go(f_ref.at[spot[k]], lane_in.at[j], lane) for j, k in enumerate("DY")]
    swaps = [out.go(p_ref.at[twin[k]], twin_in.at[i], core) for i, k in enumerate("DXLO")]

    def join(i):
        loads[i].wait()
        swaps[i].wait_recv()
        add_into(mine.at[i], twin_in.at[i])

    join(0)
    bent_cross = out.go(mine.at[0].at[top], bent_in.at[0], cross)
    bent_side = out.go(mine.at[0].at[low], bent_in.at[1], side)
    join(1)
    cross_top = out.go(mine.at[1].at[top], cross_in.at[top], cross)
    join(2)
    side_low = out.go(mine.at[2].at[low], side_in.at[low], side)
    bent_cross.wait_recv()
    add_into(mine.at[2, top], bent_in.at[0])
    side_top = out.go(mine.at[2].at[top], side_in.at[top], side)
    bent_side.wait_recv()
    add_into(mine.at[1, low], bent_in.at[1])
    cross_low = out.go(mine.at[1].at[low], cross_in.at[low], cross)
    loads[3].wait()
    swaps[3].wait_recv()
    cross_top.wait_recv()
    side_low.wait_recv()
    add_to(o_ref.at[top], mine.at[3, top], twin_in.at[3, top], cross_in.at[top])
    add_to(o_ref.at[low], mine.at[3, low], twin_in.at[3, low], side_in.at[low])
    side_top.wait_recv()
    cross_low.wait_recv()
    add_into(o_ref.at[top], side_in.at[top])
    add_into(o_ref.at[low], cross_in.at[low])
    for j, copy in enumerate(lanes):
        loads[4 + j].wait()
        copy.wait_recv()
        add_to(sum_ref.at[j], lane_mine.at[j], lane_in.at[j])
    out.finish()


def team_scatter(partial_sum, lane_sum=None):
    rows, width = partial_sum.shape[0] // 8, partial_sum.shape[1]
    scratch = [
        pltpu.VMEM((4, rows, width), BF16),
        pltpu.VMEM((4, rows, width), BF16),
        pltpu.VMEM((rows, width), BF16),
        pltpu.VMEM((rows, width), BF16),
        pltpu.VMEM((2, rows // 2, width), BF16),
    ]
    total = jax.ShapeDtypeStruct((rows, width), F32)
    blocks = partial_sum.reshape(8, rows, width)
    if lane_sum is None:
        return remote_call(
            partial(team_scatter_kernel, False),
            total,
            10,
            1,
            [pltpu.SemaphoreType.DMA((4,)), *scratch],
            40 * 2**20,
            pltpu.VMEM,
        )(blocks)
    pair = (2, *lane_sum.shape[1:])
    return remote_call(
        partial(team_scatter_kernel, True),
        (total, jax.ShapeDtypeStruct(pair, BF16)),
        12,
        5,
        [pltpu.SemaphoreType.DMA((6,)), *scratch, pltpu.VMEM(pair, BF16), pltpu.VMEM(pair, BF16)],
        48 * 2**20,
        [pltpu.VMEM] * 2,
        2,
    )(blocks, lane_sum)


def team_peers():
    xc, l = lax.axis_index("xc"), lax.axis_index("l")
    peers = []
    for i in range(1, 8):
        far, side = lax.rem(xc + i // 2, 4), lax.rem(l + i % 2, 2)
        peers.append(((far, side), {"xc": far, "l": side}))
    return (xc, l), peers


def full_places():
    y, xc = lax.axis_index("y"), lax.axis_index("xc")
    h, l = lax.axis_index("h"), lax.axis_index("l")
    core = lax.rem(xc, 2)

    def rank(plane, depth, twin=False):
        b = xc + 1 - 2 * core if twin else xc
        b = lax.rem(b + 2, 4) if plane in "XD" else b
        a = 1 - y if plane in "YD" else y
        u = 1 - h if depth in ("H", "HL") else h
        v = 1 - l if depth in ("L", "HL") else l
        return ((a * 4 + b) * 2 + u) * 2 + v

    peers = {
        "C": {"xc": xc + 1 - 2 * core},
        "X": {"xc": lax.rem(xc + 2, 4)},
        "Y": {"y": 1 - y},
        "H": {"h": 1 - h},
        "L": {"l": 1 - l},
    }
    return rank, peers


DEPTHS = ("O", "L", "H", "HL")


def copy_places():
    y, h = lax.axis_index("y"), lax.axis_index("h")
    return {
        "O": y * 2 + h,
        "Y": (1 - y) * 2 + h,
        "H": y * 2 + 1 - h,
        "D": (1 - y) * 2 + 1 - h,
    }


def weights_in_kernel(
    x_ref, gate_in, up_in, down_ref, o_ref, gates_ref, ups_ref, far_ref, send, recv, local, split,
    gate_ref, up_ref,
):
    rank, peers = full_places()
    me, team = team_peers()
    y, h = lax.axis_index("y"), lax.axis_index("h")

    def at(plane, depth):
        return o_ref.at[rank(plane, depth)]

    pieces = []
    for source, target in ((gate_in, gate_ref), (up_in, up_ref)):
        width = source.shape[1] // 32
        for r in range(8):
            for c in range(4):
                begin = ((c // 2 * 4 + r // 2) * 2 + c % 2) * 2 + r % 2
                pieces.append(
                    pltpu.make_async_copy(
                        source.at[:, pl.ds(begin * width, width)],
                        target.at[r // 2, r % 2, :, pl.ds(c * width, width)],
                        split.at[len(pieces)],
                    )
                )
    for piece in pieces:
        piece.start()
    keeps = [
        pltpu.make_async_copy(x_ref, at("O", "O"), local.at[0]),
        pltpu.make_async_copy(gate_ref.at[me], gates_ref.at[y, me[0], h, me[1]], local.at[1]),
        pltpu.make_async_copy(up_ref.at[me], ups_ref.at[y, me[0], h, me[1]], local.at[2]),
    ]
    keeps[0].start()
    greet([peer for _, peer in team] + [peers["Y"], peers["H"]])
    out = Sender(send, recv)
    swaps, twins = [], []
    to_h = out.go(x_ref, at("O", "O"), peers["H"])
    to_l = out.go(x_ref, at("O", "O"), peers["L"])
    for piece in pieces:
        piece.wait()
    keeps[1].start()
    keeps[2].start()
    for place, peer in team:
        swaps.append(out.go(gate_ref.at[place], gates_ref.at[y, me[0], h, me[1]], peer))
        swaps.append(out.go(up_ref.at[place], ups_ref.at[y, me[0], h, me[1]], peer))
    direct, bent = {}, {}

    def begin(depth):
        source = x_ref if depth == "O" else at("O", depth)
        target = at("O", depth)
        to_y = out.go(source, target, peers["Y"])
        to_x = out.go(source, target, peers["X"])
        twins.append(out.go(source, target, peers["C"]))
        direct[depth] = (to_y, to_x)

    def bend(depth):
        to_y, to_x = direct[depth]
        to_y.wait_recv()
        bent[depth] = out.go(at("Y", depth), at("Y", depth), peers["X"])
        twins.append(out.go(at("Y", depth), at("Y", depth), peers["C"]))
        to_x.wait_recv()
        twins.append(out.go(at("X", depth), at("X", depth), peers["C"]))

    def close(depth):
        bent[depth].wait_recv()
        twins.append(out.go(at("D", depth), at("D", depth), peers["C"]))

    blocks = {"gate": gates_ref, "up": ups_ref}
    flats, arrivals = {}, []

    def spread(name):
        mine = blocks[name].at[y, :, h]
        flats[name] = out.go(mine, mine, peers["H"])
        arrivals.append(out.go(mine, mine, peers["Y"]))

    def corner(name):
        flats[name].wait_recv()
        piece = blocks[name].at[y, :, 1 - h]
        arrivals.append(out.go(piece, piece, peers["Y"]))

    begin("O")
    for swap in swaps:
        swap.wait_recv()
    keeps[1].wait()
    keeps[2].wait()
    spread("gate")
    to_h.wait_recv()
    to_hl = out.go(at("O", "H"), at("O", "H"), peers["L"])
    to_l.wait_recv()
    begin("L")
    begin("H")
    bend("O")
    spread("up")
    to_hl.wait_recv()
    begin("HL")
    bend("L")
    corner("gate")
    arrivals.append(out.go(down_ref, far_ref, peers["H"]))
    bend("H")
    close("O")
    close("L")
    bend("HL")
    corner("up")
    close("H")
    close("HL")
    for copy in twins + arrivals:
        copy.wait_recv()
    out.finish()
    keeps[0].wait()


def weights_in(columns, gate, up, down):
    rows, width = columns.shape
    depth, part = gate.shape[0], gate.shape[1] // 8
    if not small_grid():
        full = lax.all_gather(columns, AXES, axis=0, tiled=False)
        gates, ups = (
            rows_in_order(
                lax.all_gather(lax.all_to_all(b, TEAM, 0, 0), COPIES, axis=0, tiled=False)
            )
            for b in (column_blocks(gate), column_blocks(up))
        )
        far = None
    else:
        full, gates, ups, far = remote_call(
            weights_in_kernel,
            (
                jax.ShapeDtypeStruct((32, rows, width), BF16),
                jax.ShapeDtypeStruct((2, 4, 2, 2, depth, part), BF16),
                jax.ShapeDtypeStruct((2, 4, 2, 2, depth, part), BF16),
                jax.ShapeDtypeStruct(down.shape, BF16),
            ),
            14 + 3 + 28 + 7,
            3,
            [
                pltpu.SemaphoreType.DMA((3,)),
                pltpu.SemaphoreType.DMA((64,)),
                pltpu.VMEM((4, 2, depth, part), BF16),
                pltpu.VMEM((4, 2, depth, part), BF16),
            ],
            spaces=[pl.ANY] * 4,
            inputs=4,
        )(columns, gate, up, down)
    return full.reshape(-1, width), gates.reshape(-1, part), ups.reshape(-1, part), far


PLANES = ("D", "X", "Y", "O")
SUMS = ("HL", "L", "H", "O")


def grads_out_kernel(edges, *refs):
    n = len(edges)
    parts, (far_ref, near_ref, raw_ref) = refs[:n], refs[n : n + 3]
    o_ref, gate_ref, up_ref, send, recv, local = refs[n + 3 : n + 9]
    mine, twin_in, cross_in, lane_in, bent_in, depth_in = refs[n + 9 : n + 15]
    flat, flat_h, back_in = refs[n + 15 : n + 17], refs[n + 17 : n + 19], refs[n + 19 : n + 21]
    flat_far, flat_y = refs[n + 21], refs[n + 22 :]
    rank, peers = full_places()
    me, team = team_peers()
    y, h = lax.axis_index("y"), lax.axis_index("h")
    half = mine.shape[2] // 2
    top, low = pl.ds(0, half), pl.ds(half, half)
    loads, swaps, flights = {}, {}, {}
    count = 0

    def load(source, target):
        nonlocal count
        copy = pltpu.make_async_copy(source, target, local.at[count])
        count += 1
        copy.start()
        return copy

    for t, depth in enumerate(SUMS):
        for k, plane in enumerate(PLANES):
            place = rank(plane, depth)
            loads[t, k] = [
                load(part.at[place], mine.at[t, k, :, pl.ds(begin, part.shape[2])])
                for part, begin in zip(parts, edges)
            ]
    own_loads = [load(near_ref, flat[0]), load(raw_ref.at[y, :, h], flat[1])]
    far_load = load(raw_ref.at[y, :, 1 - h], flat_far)
    greet([peer for _, peer in team] + [peers["Y"], peers["H"]])
    out = Sender(send, recv)

    def swap(t):
        for k, plane in enumerate(PLANES):
            place = rank(plane, SUMS[t], True)
            swaps[t, k] = [
                out.go(
                    part.at[place], twin_in.at[t, k, :, pl.ds(begin, part.shape[2])], peers["C"]
                )
                for part, begin in zip(parts, edges)
            ]

    def join(t, k):
        for copy in loads[t, k]:
            copy.wait()
        for copy in swaps[t, k]:
            copy.wait_recv()
        add_into(mine.at[t, k], twin_in.at[t, k])

    def diagonal(t):
        flights[t] = [
            out.go(mine.at[t, 0, top], bent_in.at[t, top], peers["X"]),
            out.go(mine.at[t, 0, low], bent_in.at[t, low], peers["Y"]),
        ]

    def straight(t):
        flights[t].append(out.go(mine.at[t, 1, top], cross_in.at[t, top], peers["X"]))
        flights[t].append(out.go(mine.at[t, 2, low], lane_in.at[t, low], peers["Y"]))

    def bend(t):
        flights[t][0].wait_recv()
        add_into(mine.at[t, 2, top], bent_in.at[t, top])
        flights[t].append(out.go(mine.at[t, 2, top], lane_in.at[t, top], peers["Y"]))
        flights[t][1].wait_recv()
        add_into(mine.at[t, 1, low], bent_in.at[t, low])
        flights[t].append(out.go(mine.at[t, 1, low], cross_in.at[t, low], peers["X"]))

    def close(t):
        for copy in flights[t][2:]:
            copy.wait_recv()
        return (cross_in.at[t], lane_in.at[t])

    swap(0)
    h_side = [out.go(far_ref, flat_h[0], peers["H"])]
    y_side = [out.go(raw_ref.at[1 - y, :, 1 - h], flat_y[0], peers["Y"])]
    swap(1)
    swap(2)
    swap(3)
    for t in (0, 1):
        for k in (0, 1, 2):
            join(t, k)
        diagonal(t)
        straight(t)
    join(0, 3)
    join(1, 3)
    far_load.wait()
    y_side[0].wait_recv()
    add_into(flat_far, flat_y[0])
    h_side.append(out.go(flat_far, flat_h[1], peers["H"]))
    y_side.append(out.go(raw_ref.at[1 - y, :, h], flat_y[1], peers["Y"]))
    bend(0)
    for k in (0, 1, 2):
        join(2, k)
    diagonal(2)
    straight(2)
    bend(1)
    for k in (0, 1, 2):
        join(3, k)
    diagonal(3)
    straight(3)
    join(2, 3)
    join(3, 3)
    add_into(mine.at[0, 3], *close(0))
    to_hl = out.go(mine.at[0, 3], depth_in.at[0], peers["L"])
    bend(2)
    add_into(mine.at[1, 3], *close(1))
    to_l = out.go(mine.at[1, 3], depth_in.at[1], peers["L"])
    bend(3)
    ready = close(2)
    to_hl.wait_recv()
    add_into(mine.at[2, 3], *ready, depth_in.at[0])
    to_h = out.go(mine.at[2, 3], depth_in.at[2], peers["H"])
    returns = []
    for i in range(2):
        own_loads[i].wait()
        h_side[i].wait_recv()
        arrived = [flat_h[i]]
        if i == 1:
            y_side[1].wait_recv()
            arrived.append(flat_y[1])
        add_into(flat[i], *arrived)
        returns.append([load(flat[i].at[me], back_in[i].at[me])])
        for place, peer in team:
            returns[i].append(out.go(flat[i].at[place], back_in[i].at[me], peer))
    ready = close(3)
    to_l.wait_recv()
    add_to(o_ref, mine.at[3, 3], *ready, depth_in.at[1])
    to_h.wait_recv()
    add_into(o_ref, depth_in.at[2])
    for i, target in enumerate((gate_ref, up_ref)):
        returns[i][0].wait()
        for copy in returns[i][1:]:
            copy.wait_recv()
        width = target.shape[1] // 32
        for r in range(8):
            for c in range(4):
                begin = ((c // 2 * 4 + r // 2) * 2 + c % 2) * 2 + r % 2
                target[:, pl.ds(begin * width, width)] = back_in[i][
                    r // 2, r % 2, :, pl.ds(c * width, width)
                ].astype(F32)
    out.finish()


def grads_out(parts, gate, up):
    shares = lax.axis_size("y") * lax.axis_size("h") * 8
    rows = parts[0].shape[0] // shares
    blocks = [part.reshape(shares, rows, part.shape[1]) for part in parts]
    if not small_grid():
        block = jnp.concatenate(blocks, axis=2)
        total = lax.psum_scatter(block, AXES, scatter_dimension=0, tiled=False).astype(F32)
        up = lax.psum_scatter(rows_by_copy(up), COPIES, scatter_dimension=0, tiled=False)
        gate, up = (
            from_column_blocks(lax.all_to_all(value, TEAM, 0, 0)).astype(F32)
            for value in (gate, up)
        )
        return total, gate, up
    edges = [0]
    for part in parts:
        edges.append(edges[-1] + part.shape[1])
    width = edges.pop()
    flat = gate[0].shape
    return remote_call(
        partial(grads_out_kernel, tuple(edges)),
        (
            jax.ShapeDtypeStruct((rows, width), F32),
            jax.ShapeDtypeStruct((flat[2], 8 * flat[3]), F32),
            jax.ShapeDtypeStruct((flat[2], 8 * flat[3]), F32),
        ),
        16 * len(parts) + 24 + 3 + 4 + 14,
        4,
        [
            pltpu.SemaphoreType.DMA((16 * len(parts) + 3 + 2,)),
            pltpu.VMEM((4, 4, rows, width), BF16),
            pltpu.VMEM((4, 4, rows, width), BF16),
            pltpu.VMEM((4, rows, width), BF16),
            pltpu.VMEM((4, rows, width), BF16),
            pltpu.VMEM((4, rows, width), BF16),
            pltpu.VMEM((3, rows, width), BF16),
            *[pltpu.VMEM(flat, BF16)] * 9,
        ],
        56 * 2**20,
        [pltpu.VMEM] * 3,
        len(parts) + 3,
    )(*blocks, *gate, up)


def small_grid():
    return lax.axis_size("y") == 2 and lax.axis_size("h") == 2


def lane_sums(value):
    if not small_grid():
        return lax.psum_scatter(rows_by_copy(value), COPIES, scatter_dimension=0, tiled=False)
    y, h = lax.axis_index("y"), lax.axis_index("h")

    def piece(a, b):
        plane = lax.dynamic_index_in_dim(value, a, axis=0, keepdims=False)
        return lax.dynamic_index_in_dim(plane, b, axis=1, keepdims=False)

    sent = jnp.stack([piece(1 - y, 1 - h), piece(1 - y, h)])
    arrived = lax.ppermute(sent, "y", [(0, 1), (1, 0)])
    return [
        plus(piece(y, 1 - h), arrived[0]).astype(BF16),
        plus(piece(y, h), arrived[1]).astype(BF16),
    ]


def shift(block, distance):
    pieces = lax.axis_size("h") * lax.axis_size("l")
    route = [(i, i + distance) for i in range(pieces) if 0 <= i + distance < pieces]
    return lax.ppermute(block, ("h", "l"), route)


def column_blocks(weight):
    ys, hs = lax.axis_size("y"), lax.axis_size("h")
    depth, width = weight.shape
    split = weight.reshape(depth, ys, 4, hs, 2, width // (ys * hs * 8))
    return split.transpose(2, 4, 0, 1, 3, 5).reshape(8, depth, width // 8)


def from_column_blocks(blocks):
    ys, hs = lax.axis_size("y"), lax.axis_size("h")
    depth, width = blocks.shape[1:]
    split = blocks.reshape(4, 2, depth, ys, hs, width // (ys * hs)).transpose(2, 3, 0, 4, 1, 5)
    return split.reshape(depth, 8 * width)


def rows_in_order(value):
    ys, hs = lax.axis_size("y"), lax.axis_size("h")
    split = value.reshape(ys, hs, 4, 2, *value.shape[2:])
    return split.transpose(0, 2, 1, 3, 4, 5)


def rows_by_copy(value):
    ys, hs = value.shape[0], value.shape[2]
    split = value.transpose(0, 2, 1, 3, 4, 5)
    return split.reshape(ys * hs, 8, *value.shape[4:])


def layer(*args):
    (
        hidden_in,
        layer_input,
        seq_lengths,
        cotangent,
        query_weight,
        key_matrix,
        value_matrix,
        output_weight,
        laurel_left,
        laurel_right,
        input_gate,
        input_projection,
        gate_weight,
        up_weight,
        down_weight,
        norm_gains,
        head_gains,
    ) = args
    rows, width = hidden_in.shape
    hops = max(1, WINDOW // rows)
    groups = QUERY_HEADS // KEY_VALUE_HEADS
    piece = lax.axis_index(("h", "l"))
    places = piece * rows + jnp.arange(rows, dtype=jnp.int32)
    key_places = (piece - hops) * rows + jnp.arange((hops + 1) * rows, dtype=jnp.int32)
    live = (places < seq_lengths[0]).astype(F32)[:, None]

    head_width = QUERY_HEADS * HEAD_SIZE
    kv_width = KEY_VALUE_HEADS * HEAD_SIZE
    rank = laurel_left.shape[1]
    side = layer_input.shape[1]
    depth, head_part = query_weight.shape[0], head_gains.shape[1]
    columns = (
        query_weight,
        key_matrix,
        value_matrix,
        output_weight,
        input_gate,
        input_projection.T,
        laurel_left,
        laurel_right.T,
        norm_gains.T,
        jnp.pad(head_gains.T, ((0, depth - head_part), (0, 0))),
    )
    edges = [0]
    for column in columns:
        edges.append(edges[-1] + column.shape[1])
    full_width = -(-edges[-1] // 128) * 128
    local_columns = jnp.pad(
        jnp.concatenate(columns, axis=1), ((0, 0), (0, full_width - edges[-1]))
    )
    full, gate_cols, up_cols, far_down = weights_in(
        local_columns, gate_weight, up_weight, down_weight
    )
    first = full[:, : edges[3]]
    output_all, side_gate_all, projection_all, left_all, right_all = (
        full[:, edges[i] : edges[i + 1]] for i in range(3, 8)
    )
    gains = full[:, edges[8] : edges[9]].T.astype(F32)
    head_gain = (
        full[:, edges[9] : edges[10]].reshape(-1, depth, 2)[:, :head_part].reshape(-1, 2).T
    ).astype(F32)

    hidden = hidden_in.astype(F32)
    side_input = layer_input.astype(F32)
    cosine, sine = rope_tables(places)

    hidden_inv = inverse_rms(hidden)
    normed = hidden * hidden_inv * gains[0]
    normed_low = normed.astype(BF16)
    raw = dot(normed_low, first)
    left_low = dot(normed_low, left_all).astype(BF16)
    query_low, pair_low = heads(raw, cosine, sine, head_gain)
    pairs = [pair_low]
    for _ in range(hops):
        pairs.insert(0, shift(pairs[0], 1))
    window = jnp.concatenate(pairs, axis=1).reshape(2, -1, KEY_VALUE_HEADS, HEAD_SIZE)
    grouped = query_low.reshape(rows, KEY_VALUE_HEADS, groups, HEAD_SIZE)
    scores = jnp.einsum("qkgd,tkd->kgqt", grouped, window[0], preferred_element_type=F32)
    allowed = (
        (key_places[None, :] <= places[:, None])
        & (places[:, None] - key_places[None, :] < WINDOW)
        & (key_places[None, :] >= 0)
    )
    scores = jnp.where(allowed, scores, MASKED)
    weights = jnp.exp(scores - jnp.max(scores, axis=-1, keepdims=True))
    probs = weights / jnp.sum(weights, axis=-1, keepdims=True)
    probs_low = probs.astype(BF16)
    mixed = (
        jnp.einsum("kgqt,tkd->qkgd", probs_low, window[1], preferred_element_type=F32)
        .reshape(rows, head_width)
        .astype(BF16)
    )
    attention_raw = dot(mixed, output_all)
    attention_inv = inverse_rms(attention_raw)
    right_raw = dot(left_low, right_all, 1, 1)
    right_inv = inverse_rms(right_raw)
    merged = (
        hidden
        + attention_raw * attention_inv * gains[1]
        + normed
        + right_raw * right_inv * gains[2]
    ) * HALF_ROOT
    merged_inv = inverse_rms(merged)
    expand_low = (merged * merged_inv * gains[3]).astype(BF16)

    expand_all, down_rows = team_gather_with(expand_low, down_weight, far_down)
    gate_raw = dot(expand_all, gate_cols)
    up_raw = dot(expand_all, up_cols)
    act_low = (gelu(gate_raw) * up_raw).astype(BF16)
    reduced_raw = team_scatter(dot(act_low, down_rows).astype(BF16))
    reduced_inv = inverse_rms(reduced_raw)
    after_feed = merged + reduced_raw * reduced_inv * gains[4]
    after_low = after_feed.astype(BF16)
    side_raw = dot(after_low, side_gate_all)
    side_low = (gelu(side_raw) * side_input).astype(BF16)
    side_out = dot(side_low, projection_all, 1, 1)
    side_inv = inverse_rms(side_out)
    block_out = (after_feed + side_out * side_inv * gains[5]) * live

    upstream = cotangent.astype(F32) * live
    grad_side, gain_five = rms_back(side_out, side_inv, gains[5], upstream)
    grad_side_low = grad_side.astype(BF16)
    grad_side_raw = (
        dot(grad_side_low, projection_all) * side_input * gelu_slope(side_raw)
    ).astype(BF16)
    grad_after = upstream + dot(grad_side_raw, side_gate_all, 1, 1)
    grad_reduced, gain_four = rms_back(reduced_raw, reduced_inv, gains[4], grad_after)
    grad_reduced_low = grad_reduced.astype(BF16)

    grad_reduced_all = team_gather(grad_reduced_low)
    grad_product = dot(grad_reduced_all, down_rows, 1, 1)
    grad_gate_low = (grad_product * up_raw * gelu_slope(gate_raw)).astype(BF16)
    grad_up_low = (grad_product * gelu(gate_raw)).astype(BF16)
    part_down = dot(act_low, grad_reduced_all, 0, 0).astype(BF16)
    part_low = (dot(grad_gate_low, gate_cols, 1, 1) + dot(grad_up_low, up_cols, 1, 1)).astype(BF16)
    part_gate = dot(expand_all, grad_gate_low, 0, 0).astype(BF16)
    part_up = dot(expand_all, grad_up_low, 0, 0).astype(BF16)
    down_blocks = part_down.reshape(-1, *down_weight.shape)
    part_gate, part_up = (
        value.reshape(lax.axis_size("y"), 4, -1, 2, depth, value.shape[1])
        for value in (part_gate, part_up)
    )
    part_low, part_gate = lax.optimization_barrier((part_low, part_gate))
    if small_grid():
        part, down_sums = team_scatter(part_low, down_blocks)
    else:
        part = team_scatter(part_low)
        down_sums = None
    sums_gate = lane_sums(part_gate)
    grad_merged, gain_three = rms_back(merged, merged_inv, gains[3], part)
    grad_sum = (grad_after + grad_merged) * HALF_ROOT
    grad_right, gain_two = rms_back(right_raw, right_inv, gains[2], grad_sum)
    grad_right_low = grad_right.astype(BF16)
    grad_left_low = dot(grad_right_low, right_all).astype(BF16)
    grad_attention, gain_one = rms_back(attention_raw, attention_inv, gains[1], grad_sum)
    grad_attention_low = grad_attention.astype(BF16)
    grad_mixed = (
        dot(grad_attention_low, output_all, 1, 1)
        .astype(BF16)
        .reshape(rows, KEY_VALUE_HEADS, groups, HEAD_SIZE)
    )
    grad_probs = jnp.einsum("qkgd,tkd->kgqt", grad_mixed, window[1], preferred_element_type=F32)
    inner = jnp.sum(probs * grad_probs, axis=-1, keepdims=True)
    grad_scores = (probs * (grad_probs - inner)).astype(BF16)
    grad_query_rot = jnp.einsum(
        "kgqt,tkd->qkgd", grad_scores, window[0], preferred_element_type=F32
    ).reshape(rows, head_width)
    grad_window = jnp.stack(
        [
            jnp.einsum("kgqt,qkgd->tkd", grad_scores, grouped, preferred_element_type=F32),
            jnp.einsum("kgqt,qkgd->tkd", probs_low, grad_mixed, preferred_element_type=F32),
        ]
    ).reshape(2, -1, kv_width)
    carried = grad_window[:, :rows]
    for hop in range(1, hops + 1):
        carried = shift(carried.astype(BF16), -1).astype(F32)
        carried = carried + grad_window[:, hop * rows : (hop + 1) * rows]
    if down_sums is None:
        grad_down = lax.psum_scatter(down_blocks, COPIES, scatter_dimension=0).astype(F32)
    else:
        carried, leaving = lax.optimization_barrier((carried, down_sums[0]))
        grad_down = plus(down_sums[1], lax.ppermute(leaving, "h", [(0, 1), (1, 0)]))
    grad_raw, head_grads = heads_back(raw, grad_query_rot, carried, cosine, sine, head_gain)
    grad_normed = grad_sum + dot(grad_raw, first, 1, 1) + dot(grad_left_low, left_all, 1, 1)
    grad_input, gain_zero = rms_back(hidden, hidden_inv, gains[0], grad_normed)
    grad_hidden = grad_sum + grad_input

    gain_grads = jnp.stack(
        [
            jnp.sum(g, axis=0)
            for g in (gain_zero, gain_one, gain_two, gain_three, gain_four, gain_five)
        ]
    )
    head_column = jnp.pad(
        head_grads.T.reshape(-1, head_part, 2), ((0, 0), (0, depth - head_part), (0, 0))
    ).reshape(-1, 2)
    tail = full_width - edges[6]
    small = (
        dot(normed_low, jnp.pad(grad_left_low, ((0, 0), (0, tail - rank))), 0, 0)
        + dot(grad_right_low, jnp.pad(left_low, ((0, 0), (rank, tail - 2 * rank))), 0, 0)
        + jnp.pad(gain_grads.T, ((0, 0), (2 * rank, tail - 2 * rank - 6)))
        + jnp.pad(head_column, ((0, 0), (2 * rank + 6, tail - 2 * rank - 8)))
    )
    weight_grads = (
        dot(normed_low, grad_raw, 0, 0).astype(BF16),
        dot(mixed, grad_attention_low, 0, 0).astype(BF16),
        dot(after_low, grad_side_raw, 0, 0).astype(BF16),
        dot(grad_side_low, side_low, 0, 0).astype(BF16),
        small.astype(BF16),
    )
    summed, grad_gate, grad_up = grads_out(weight_grads, sums_gate, part_up)
    (
        d_query,
        d_key,
        d_value,
        d_output,
        d_side_gate,
        d_projection,
        d_left,
        d_right,
        d_gains,
        d_heads,
    ) = (summed[:, edges[i] : edges[i + 1]] for i in range(10))
    d_right, d_projection, d_gains = d_right.T, d_projection.T, d_gains.T
    d_heads = d_heads[:head_part].T
    return (
        block_out,
        grad_hidden,
        d_query,
        d_key,
        d_value,
        d_output,
        d_left,
        d_right,
        d_side_gate,
        d_projection,
        grad_gate,
        grad_up,
        grad_down,
        d_gains,
        d_heads,
    )


def solution(mesh):
    dp, seq = mesh.shape["dp"], mesh.shape["seq"]
    grid = Mesh(mesh.devices.reshape(dp // 4, 4, seq // 2, 2), AXES)
    row, column = P(AXES, None), P(None, AXES)
    return jax.shard_map(
        layer,
        mesh=grid,
        in_specs=(row, row, P(("y", "xc")))
        + (row,) * 6
        + (column, row, column)
        + (row,) * 3
        + (column,) * 2,
        out_specs=(row,) * 7 + (column, row, column) + (row,) * 3 + (column,) * 2,
        check_vma=False,
    )
```
